32 devices in a mesh: dp: 8 (over y, x, core), tensor: 4 (over z).
Axes of the slice: x: 2, y: 2, z: 4, core: 2. Of those that a mesh axis runs over, the one named last changes fastest.
Arguments:
- tokens: bfloat16 [20480, 768], P(('dp', 'tensor')), may hold values from -6 to 6
- visible_counts: int32 [256], P('dp'), may hold values from 20 to 78, as said below
- norm_one_gain: float32 [768], replicated, may hold values from 0.1 to 1.9
- norm_one_shift: float32 [768], replicated, may hold values from -1.8 to 1.8
- input_weight: bfloat16 [768, 3, 768], P(None, None, 'tensor'), may hold values from -0.21875 to 0.21875
- input_bias: bfloat16 [2, 768], P(None, 'tensor'), may hold values from -1.796875 to 1.796875
- mixer_weight: bfloat16 [768, 768], P('tensor'), may hold values from -1.25 to 1.25
- mixer_bias: float32 [768], replicated, may hold values from -1.8 to 1.8
- norm_two_gain: float32 [768], replicated, may hold values from 0.1 to 1.9
- norm_two_shift: float32 [768], replicated, may hold values from -1.8 to 1.8
- up_weight: bfloat16 [768, 3072], P(None, 'tensor'), may hold values from -0.21875 to 0.21875
- up_bias: bfloat16 [3072], P('tensor'), may hold values from -1.796875 to 1.796875
- down_weight: bfloat16 [3072, 768], P('tensor'), may hold values from -0.109375 to 0.109375
- down_bias: float32 [768], replicated, may hold values from -1.8 to 1.8
- output_grad: bfloat16 [20480, 768], P(('dp', 'tensor')), may hold values from -6 to 6
Outputs:
- block_output: bfloat16 [20480, 768], P(('dp', 'tensor'))
- grad_tokens: float32 [20480, 768], P(('dp', 'tensor'))
- grad_norm_one_gain: float32 [768], replicated
- grad_norm_one_shift: float32 [768], replicated
- grad_input_weight: float32 [768, 3, 768], P(None, None, 'tensor')
- grad_input_bias: float32 [2, 768], P(None, 'tensor')
- grad_mixer_weight: float32 [768, 768], P('tensor')
- grad_mixer_bias: float32 [768], replicated
- grad_norm_two_gain: float32 [768], replicated
- grad_norm_two_shift: float32 [768], replicated
- grad_up_weight: float32 [768, 3072], P(None, 'tensor')
- grad_up_bias: float32 [3072], P('tensor')
- grad_down_weight: float32 [3072, 768], P('tensor')
- grad_down_bias: float32 [768], replicated
The draws below stay inside these ranges and needn't reach their ends.
Inputs may be any that keep to these rules, and one draw needn't show every extreme that they name: `visible_counts`: each image has 20 to 78 visible patches; some image has exactly 78 and some exactly 20.
All inputs are finite; a program needn't handle non-finite values.
Results may differ from the reference program's by a relative error of at most 0.014.
Values may be sent and summed in bfloat16 or wider, within the bound.
No kernel may reach another device: no remote copies, remote signals or barrier semaphores. Data moves between devices by JAX's collectives and lax.ppermute only.
A program may use at most 128 MiB of HBM per device.

```python
import jax
import jax.numpy as jnp
from jax import lax

D = 768
HEADS = 12
HD = 64
FF = 3072
SLOTS = 80
IMG_DEV = 32
IMAGES = 256
ROWS = 20480


def draw_visible_counts(key, part):
    key_base, key_top, key_low = jax.random.split(key, 3)
    counts = jax.random.randint(key_base, (IMAGES,), SLOTS // 4, SLOTS - 1)
    top_at = jax.random.randint(key_top, (), 0, IMAGES)
    low_at = (top_at + 1 + jax.random.randint(key_low, (), 0, IMAGES - 1)) % IMAGES
    counts = counts.at[top_at].set(SLOTS - 2).at[low_at].set(SLOTS // 4)
    return counts.astype(jnp.int32)


def level_of(rng, dims, cuts, smallest, top_value):
    def one(position, parts):
        draws = jax.random.uniform(jax.random.fold_in(jax.random.fold_in(rng, 6), position), (parts,), jnp.float32, smallest / len(cuts), top_value / len(cuts))
        return jnp.repeat(jnp.exp(draws), dims[position] // parts).reshape((-1,) + (1,) * (len(dims) - position - 1))

    gain = one(*cuts[0])
    for cut in cuts[1:]:
        gain = gain * one(*cut)
    return gain


def centred(key, shape, deviation, reach, cuts=(), kind=jnp.bfloat16):
    factor_of = level_of(key, shape, cuts, -0.22, 0.18) if cuts else 1.0
    entries = jax.random.normal(key, shape, jnp.float32) * deviation * factor_of
    return jnp.minimum(jnp.maximum(entries, -reach), reach).astype(kind)


def setup_inputs(seed: int = 0) -> dict:
    splits = jax.random.split(jax.random.key(seed), 16)
    tokens = centred(splits[0], (ROWS, D), 1.0, 6.0, ((0, 32),))
    visible_counts = draw_visible_counts(jax.random.fold_in(splits[15], 71), 0)
    norm_one_gain = jnp.clip(1.0 + 0.18 * jax.random.normal(splits[2], (D,), jnp.float32), 0.1, 1.9)
    norm_one_shift = centred(splits[3], (D,), 0.3, 1.8, (), jnp.float32)
    input_weight = centred(splits[4], (D, 3, D), D ** -0.5, 0.21875, ((2, 4),))
    input_bias = centred(splits[5], (2, D), 0.3, 1.796875, ((1, 4),))
    mixer_weight = centred(splits[6], (D, D), (max(2 * D // SLOTS, 1)) ** -0.5, 1.25, ((0, 4),))
    mixer_bias = centred(splits[7], (D,), 0.3, 1.8, (), jnp.float32)
    norm_two_gain = jnp.clip(1.0 + 0.18 * jax.random.normal(splits[8], (D,), jnp.float32), 0.1, 1.9)
    norm_two_shift = centred(splits[9], (D,), 0.3, 1.8, (), jnp.float32)
    up_weight = centred(splits[10], (D, FF), D ** -0.5, 0.21875, ((1, 4),))
    up_bias = centred(splits[11], (FF,), 0.3, 1.796875, ((0, 4),))
    down_weight = centred(splits[12], (FF, D), FF ** -0.5, 0.109375, ((0, 4),))
    down_bias = centred(splits[13], (D,), 0.3, 1.8, (), jnp.float32)
    output_grad = centred(splits[14], (ROWS, D), 1.0, 6.0, ((0, 32),))
    return {"tokens": tokens, "visible_counts": visible_counts, "norm_one_gain": norm_one_gain, "norm_one_shift": norm_one_shift, "input_weight": input_weight, "input_bias": input_bias, "mixer_weight": mixer_weight, "mixer_bias": mixer_bias, "norm_two_gain": norm_two_gain, "norm_two_shift": norm_two_shift, "up_weight": up_weight, "up_bias": up_bias, "down_weight": down_weight, "down_bias": down_bias, "output_grad": output_grad}


best_precision = lax.Precision.HIGHEST
masked_score = -1000000000.0

@jax.custom_vjp
def low(v):
    return lax.optimization_barrier(v.astype(jnp.bfloat16)).astype(jnp.float32)

@jax.custom_vjp
def low_back(v):
    return v

def low_keep(v):
    return (low(v), None)

def low_pass(kept, grad):
    return (grad,)

def back_keep(v):
    return (v, None)

def back_low(kept, grad):
    return (low(grad),)
low.defvjp(low_keep, low_pass)
low_back.defvjp(back_keep, back_low)

def layer_norm(inputs, norm_gain, norm_shift):
    center = inputs - lax.optimization_barrier(jnp.mean(inputs, axis=-1, keepdims=True))
    spread = lax.optimization_barrier(jnp.mean(center * center, axis=-1, keepdims=True))
    return center * lax.rsqrt(spread + 1e-06) * norm_gain + norm_shift

def attend_group(pieces):
    queries, key_rows, values, counts = pieces
    factor = HD ** (-0.5)
    scores = low_back(jnp.einsum('bqhd,bkhd->bhqk', queries, key_rows, precision=best_precision) * factor)
    visible = (lax.broadcasted_iota(jnp.int32, (counts.shape[0], SLOTS), 1) < counts[:, None])[:, None, None, :]
    scores = jnp.where(visible, scores, masked_score)
    maxima = lax.optimization_barrier(jnp.max(scores, axis=-1, keepdims=True))
    exponent = jnp.exp(scores - maxima)
    totals = lax.optimization_barrier(jnp.sum(exponent, axis=-1, keepdims=True))
    soft_low = low(exponent / totals)
    return jnp.einsum('bhqk,bkhd->bqhd', soft_low, values, precision=best_precision)

def forward(tokens, counts, norm_one_gain, norm_one_shift, input_weight, input_bias, mixer_weight, mixer_bias, norm_two_gain, norm_two_shift, up_weight, up_bias, down_weight, down_bias):
    normed_one = low(layer_norm(tokens, norm_one_gain, norm_one_shift))
    queries = low(low_back(jnp.dot(normed_one, input_weight[:, 0, :], precision=best_precision)) + input_bias[0])
    key_rows = low(low_back(jnp.dot(normed_one, input_weight[:, 1, :], precision=best_precision)))
    values = low(low_back(jnp.dot(normed_one, input_weight[:, 2, :], precision=best_precision)) + input_bias[1])
    groups = IMAGES // IMG_DEV
    layout = (groups, IMG_DEV, SLOTS, HEADS, HD)
    blended = lax.map(jax.checkpoint(attend_group), (queries.reshape(layout), key_rows.reshape(layout), values.reshape(layout), counts.reshape(groups, IMG_DEV)))
    blended = low(low_back(blended.reshape(tokens.shape)))
    first_sum = tokens + low_back(jnp.dot(blended, mixer_weight, precision=best_precision)) + mixer_bias
    normed_two = low(layer_norm(first_sum, norm_two_gain, norm_two_shift))
    hidden_pre = low_back(jnp.dot(normed_two, up_weight, precision=best_precision)) + up_bias
    active = low(jax.nn.gelu(hidden_pre, approximate=False))
    return first_sum + low_back(jnp.dot(active, down_weight, precision=best_precision)) + down_bias

def reference(tokens, visible_counts, norm_one_gain, norm_one_shift, input_weight, input_bias, mixer_weight, mixer_bias, norm_two_gain, norm_two_shift, up_weight, up_bias, down_weight, down_bias, output_grad):

    def wrapped(*pieces):
        return forward(pieces[0], visible_counts, *pieces[1:])
    floats_in = [element.astype(jnp.float32) for element in (tokens, norm_one_gain, norm_one_shift, input_weight, input_bias, mixer_weight, mixer_bias, norm_two_gain, norm_two_shift, up_weight, up_bias, down_weight, down_bias)]
    result, pullback = jax.vjp(wrapped, *floats_in)
    gradients = pullback(output_grad.astype(jnp.float32))
    return (result.astype(jnp.bfloat16), gradients[0], gradients[1], gradients[2], gradients[3], gradients[4], gradients[5], gradients[6], gradients[7], gradients[8], gradients[9], gradients[10], gradients[11], gradients[12])
```

```python
import functools

import jax
import jax.numpy as jnp
import numpy as np
from jax import lax
from jax.experimental import pallas as pl
from jax.experimental.pallas import tpu as pltpu
from jax.sharding import PartitionSpec as P

HD = 64
SLOTS = 80
LANES = 128
TILE_IMAGES = 4
MASKED = -1000000000.0
EPS = 1e-06
F32 = jnp.float32
BF16 = jnp.bfloat16

ANY = pl.BlockSpec(memory_space=pl.ANY)
SMEM = pl.BlockSpec(memory_space=pltpu.SMEM)
VMEM = pl.BlockSpec(memory_space=pltpu.VMEM)


def shape(dims, kind):
    return jax.ShapeDtypeStruct(tuple(dims), kind)


def params(megabytes, grid_dims=0):
    semantics = ("arbitrary",) * grid_dims if grid_dims else None
    return pltpu.CompilerParams(
        vmem_limit_bytes=megabytes * 1024 * 1024, dimension_semantics=semantics
    )


def cost(flops, moved):
    return pl.CostEstimate(flops=int(flops), bytes_accessed=int(moved), transcendentals=0)


def dot(left, right):
    return lax.dot_general(left, right, (((1,), (0,)), ((), ())), preferred_element_type=F32)


def dot_rows(left, right):
    return lax.dot_general(left, right, (((1,), (1,)), ((), ())), preferred_element_type=F32)


def dot_columns(left, right):
    return lax.dot_general(left, right, (((0,), (0,)), ((), ())), preferred_element_type=F32)


def centred(rows):
    center = rows - jnp.mean(rows, axis=-1, keepdims=True)
    spread = jnp.mean(center * center, axis=-1, keepdims=True)
    return center, lax.rsqrt(spread + EPS)


def norm_back(rows, gain, grad):
    center, rstd = centred(rows)
    xhat = center * rstd
    e = grad * gain
    back = rstd * (
        e - jnp.mean(e, axis=-1, keepdims=True) - xhat * jnp.mean(e * xhat, axis=-1, keepdims=True)
    )
    return (
        back,
        jnp.sum(grad * xhat, axis=0, keepdims=True),
        jnp.sum(grad, axis=0, keepdims=True),
    )


def norm_one_kernel(images, chunk, place, counts, tokens, gain, shift, out):
    rows = tokens.shape[0]

    @pl.loop(0, rows // chunk)
    def _(step):
        at = pl.ds(pl.multiple_of(step * chunk, chunk), chunk)
        center, rstd = centred(tokens[at, :].astype(F32))
        out[at, :] = (center * rstd * gain[...] + shift[...]).astype(BF16)

    extra = out.shape[0] - rows
    row = lax.broadcasted_iota(jnp.int32, (extra, out.shape[1]), 0)
    table = jnp.zeros((extra, out.shape[1]), F32)
    first = place[2] * images
    for image in range(images):
        table = jnp.where(row == image, counts[first + image].astype(F32), table)
    out[rows:, :] = table.astype(BF16)


def norm_one(place, counts, tokens, gain, shift):
    rows, width = tokens.shape
    images = rows // SLOTS
    return pl.pallas_call(
        functools.partial(norm_one_kernel, images, SLOTS),
        out_shape=shape((rows + 16, width), BF16),
        in_specs=[SMEM, SMEM, VMEM, VMEM, VMEM],
        out_specs=VMEM,
        compiler_params=params(16),
        cost_estimate=cost(rows * width * 10, rows * width * 4),
    )(place, counts, tokens, gain, shift)


def norm_two_kernel(tokens, mine, received, bias, gain, shift, first_sum, normed):
    total = tokens[...].astype(F32) + (mine[...] + received[...].astype(F32)) + bias[...]
    first_sum[...] = total
    center, rstd = centred(total)
    normed[...] = (center * rstd * gain[...] + shift[...]).astype(BF16)


def rows_spec(tile, width):
    return pl.BlockSpec((tile, width), lambda i: (i, 0))


def fixed_spec(*dims):
    return pl.BlockSpec(dims, lambda i: (0,) * len(dims))


def norm_two(tokens, mine, received, bias, gain, shift):
    rows, width = tokens.shape
    tile = 2 * SLOTS
    row = rows_spec(tile, width)
    vector = fixed_spec(1, width)
    return pl.pallas_call(
        norm_two_kernel,
        grid=(rows // tile,),
        out_shape=(shape((rows, width), F32), shape((rows, width), BF16)),
        in_specs=[row, row, row, vector, vector, vector],
        out_specs=(row, row),
        compiler_params=params(16, 1),
        cost_estimate=cost(rows * width * 12, rows * width * 14),
    )(tokens, mine, received, bias, gain, shift)


def norm_two_back_kernel(mine, received, first_sum, gain, output_grad, grad_first, low, sums):
    grad = mine[...] + received[...].astype(F32)
    back, grad_gain, grad_shift = norm_back(first_sum[...], gain[...], grad)
    out_grad = output_grad[...].astype(F32)
    total = out_grad + back
    grad_first[...] = total
    low[...] = total.astype(BF16)

    @pl.when(pl.program_id(0) == 0)
    def _():
        sums[...] = jnp.zeros_like(sums)

    sums[0:1, :] += grad_gain
    sums[1:2, :] += grad_shift
    sums[2:3, :] += jnp.sum(total, axis=0, keepdims=True)
    sums[3:4, :] += jnp.sum(out_grad, axis=0, keepdims=True)


def norm_two_back(mine, received, first_sum, gain, output_grad):
    rows, width = mine.shape
    tile = 2 * SLOTS
    row = rows_spec(tile, width)
    return pl.pallas_call(
        norm_two_back_kernel,
        grid=(rows // tile,),
        out_shape=(shape((rows, width), F32), shape((rows, width), BF16), shape((8, width), F32)),
        in_specs=[row, row, row, fixed_spec(1, width), row],
        out_specs=(row, row, fixed_spec(8, width)),
        compiler_params=params(16, 1),
        cost_estimate=cost(rows * width * 25, rows * width * 18),
    )(mine, received, first_sum, gain, output_grad)


def norm_one_back_kernel(mine, received, tokens, gain, grad_first, grad_tokens, sums):
    grad = mine[...] + received[...].astype(F32)
    back, grad_gain, grad_shift = norm_back(tokens[...].astype(F32), gain[...], grad)
    grad_tokens[...] = grad_first[...] + back

    @pl.when(pl.program_id(0) == 0)
    def _():
        sums[...] = jnp.zeros_like(sums)

    sums[0:1, :] += grad_gain
    sums[1:2, :] += grad_shift


def norm_one_back(mine, received, tokens, gain, grad_first):
    rows, width = mine.shape
    tile = 2 * SLOTS
    row = rows_spec(tile, width)
    return pl.pallas_call(
        norm_one_back_kernel,
        grid=(rows // tile,),
        out_shape=(shape((rows, width), F32), shape((8, width), F32)),
        in_specs=[row, row, row, fixed_spec(1, width), row],
        out_specs=(row, fixed_spec(8, width)),
        compiler_params=params(16, 1),
        cost_estimate=cost(rows * width * 25, rows * width * 16),
    )(mine, received, tokens, gain, grad_first)


def pack_attention_kernel(place, projection, mixer, bias, out, sem):
    quarter = place[0]
    size = out.shape[0] - 16
    feature_rows = projection.shape[0]
    first = pl.multiple_of(quarter * size, 16)
    from_projection = quarter * size < feature_rows

    @pl.when(from_projection)
    def _():
        copy = pltpu.make_async_copy(
            projection.at[pl.ds(first, size)], out.at[pl.ds(0, size)], sem
        )
        copy.start()
        copy.wait()

    @pl.when(jnp.logical_not(from_projection))
    def _():
        copy = pltpu.make_async_copy(mixer, out.at[pl.ds(0, size)], sem)
        copy.start()
        copy.wait()

    columns = bias.shape[1]
    row = lax.broadcasted_iota(jnp.int32, (16, columns), 0)
    both = bias[...].astype(F32)
    rows = jnp.where(row == 0, both[0:1, :], jnp.where(row == 1, both[1:2, :], 0.0))
    out[size:, :] = jnp.zeros((16, out.shape[1]), BF16)
    out[size:, 0:columns] = rows.astype(BF16)


def pack_attention(place, projection, mixer, bias):
    size, width = mixer.shape
    return pl.pallas_call(
        pack_attention_kernel,
        out_shape=shape((size + 16, width), BF16),
        in_specs=[SMEM, ANY, ANY, VMEM],
        out_specs=VMEM,
        scratch_shapes=[pltpu.SemaphoreType.DMA(())],
        compiler_params=params(8),
        cost_estimate=cost(0, 2 * size * width),
    )(place, projection, mixer, bias)


def pack_hidden_kernel(place, up, down, bias, out, sems):
    size = (out.shape[0] - 16) // 2
    first = pl.multiple_of(place[0] * size, 16)
    copies = [
        pltpu.make_async_copy(
            source.at[pl.ds(first, size)], out.at[pl.ds(index * size, size)], sems.at[index]
        )
        for index, source in enumerate((up, down))
    ]
    for copy in copies:
        copy.start()
    row = lax.broadcasted_iota(jnp.int32, (16, out.shape[1]), 0)
    out[2 * size :, :] = jnp.where(row == 0, bias[...].astype(F32), 0.0).astype(BF16)
    for copy in copies:
        copy.wait()


def pack_hidden(place, up, down, bias):
    size, width = up.shape[0] // 4, up.shape[1]
    return pl.pallas_call(
        pack_hidden_kernel,
        out_shape=shape((2 * size + 16, width), BF16),
        in_specs=[SMEM, ANY, ANY, VMEM],
        out_specs=VMEM,
        scratch_shapes=[pltpu.SemaphoreType.DMA((2,))],
        compiler_params=params(8),
        cost_estimate=cost(0, 4 * size * width),
    )(place, up, down, bias)


def piece_copies(place, pieces, target, matrices, sems):
    size = (pieces[0].shape[0] - 16) // matrices
    copies = []
    for flip, piece in enumerate(pieces):
        quarter = lax.bitwise_xor(place[0], flip)
        for matrix in range(matrices):
            to = pl.multiple_of(matrix * 4 * size + quarter * size, 16)
            copies.append((piece.at[pl.ds(matrix * size, size)], target.at[pl.ds(to, size)]))
    copies.append(
        (pieces[0].at[pl.ds(matrices * size, 16)], target.at[pl.ds(matrices * 4 * size, 16)])
    )
    return [
        pltpu.make_async_copy(source, to, sems.at[index])
        for index, (source, to) in enumerate(copies)
    ]


def shard_copies(shards, piece, target, sems):
    copies = []
    at = 0
    for shard in shards:
        copies.append((shard, target.at[pl.ds(at, shard.shape[0])]))
        at += shard.shape[0]
    copies.append((piece.at[pl.ds(piece.shape[0] - 16, 16)], target.at[pl.ds(at, 16)]))
    return [
        pltpu.make_async_copy(source, to, sems.at[index])
        for index, (source, to) in enumerate(copies)
    ]


def run_copies(copies):
    for copy in copies:
        copy.start()
    for copy in copies:
        copy.wait()


def head_lanes(rows, width):
    return lax.broadcasted_iota(jnp.int32, (rows, width), 1) // HD


def spread_heads(block, lanes, heads):
    gap = jnp.zeros((LANES - SLOTS, block.shape[1]), block.dtype)
    parts = []
    for head in range(heads):
        parts.append(jnp.where(lanes == head, block, jnp.zeros_like(block)))
        parts.append(gap)
    return jnp.concatenate(parts, axis=0)


def gather_heads(product, lanes, heads):
    total = product[0:SLOTS]
    for head in range(1, heads):
        total = jnp.where(lanes == head, product[head * LANES : head * LANES + SLOTS], total)
    return total


def load_attention(place, projection, mixer, piece, near, far, weights, sems):
    @pl.when(pl.program_id(0) == 0)
    def _():
        copies = piece_copies(place, near, weights.at[1], 1, sems)
        for copy in copies:
            copy.start()

        @pl.when(place[1] == 0)
        def _():
            run_copies(
                shard_copies((projection, mixer), piece, weights.at[0], sems.at[pl.ds(8, 8)])
            )

        @pl.when(place[1] != 0)
        def _():
            run_copies(piece_copies(place, far, weights.at[0], 1, sems.at[pl.ds(8, 8)]))

        for copy in copies:
            copy.wait()


def attention_kernel(
    heads,
    place,
    projection,
    mixer,
    piece,
    near0,
    near1,
    near2,
    near3,
    far0,
    far1,
    far2,
    far3,
    normed,
    counts,
    *rest,
):
    saved, soft, part, weights, table, sems = rest[-6:]
    load_attention(
        place,
        projection,
        mixer,
        piece,
        (near0, near1, near2, near3),
        (far0, far1, far2, far3),
        weights,
        sems,
    )
    cols = heads * HD
    visible_rows = counts[:, 0:LANES].astype(F32)
    for image in range(visible_rows.shape[0]):
        table[image, :, :] = visible_rows[image : image + 1, :]
    rows = normed[...]
    for slot in range(2):
        for index in range(3):
            value = dot_rows(rows, weights[slot, index * cols : (index + 1) * cols, :])
            if index != 1:
                bias_row = 0 if index == 0 else 1
                bias = weights[slot, 4 * cols : 4 * cols + 16, 0:cols].astype(F32)
                value = value + bias[bias_row : bias_row + 1, :]
            saved[4 * slot + index, :, :] = value.astype(BF16)

    lanes = head_lanes(SLOTS, cols)
    key_index = lax.broadcasted_iota(jnp.int32, (SLOTS, LANES), 1).astype(F32)
    first = pl.program_id(0) * TILE_IMAGES

    def one_image(image, carry):
        at = pl.ds(pl.multiple_of(image * SLOTS, 16), SLOTS)
        visible = key_index < table[first + image]
        for slot in range(2):
            queries = saved[4 * slot, at, :]
            keys = spread_heads(saved[4 * slot + 1, at, :], lanes, heads)
            values = spread_heads(saved[4 * slot + 2, at, :], lanes, heads)
            scores = dot_rows(queries, keys) * (HD**-0.5)
            lows = []
            for head in range(heads):
                one = jnp.where(visible, scores[:, head * LANES : (head + 1) * LANES], MASKED)
                exponent = jnp.exp(one - jnp.max(one, axis=-1, keepdims=True))
                total = jnp.sum(exponent, axis=-1, keepdims=True)
                lows.append((exponent / total).astype(BF16))
            low = jnp.concatenate(lows, axis=1)
            soft[at, slot * heads * LANES : (slot + 1) * heads * LANES] = low
            saved[4 * slot + 3, at, :] = dot(low, values).astype(BF16)
        return carry

    lax.fori_loop(0, TILE_IMAGES, one_image, 0, unroll=2)
    total = dot(saved[3, :, :], weights[0, 3 * cols : 4 * cols, :])
    total = total + dot(saved[7, :, :], weights[1, 3 * cols : 4 * cols, :])
    part[...] = total.astype(part.dtype)


def attention(place, own, near, far, normed, before, kind):
    projection, mixer, piece = own
    cols, width = mixer.shape
    heads = cols // HD
    rows = normed.shape[0] - 16
    tile = TILE_IMAGES * SLOTS
    tiles = rows // tile
    base = tiles if before is None else 0
    extra = () if before is None else tuple(before)
    args = (place, projection, mixer, piece, *near, *far, normed, normed, *extra)
    return pl.pallas_call(
        functools.partial(attention_kernel, heads),
        grid=(tiles,),
        out_shape=(
            shape((8, 2 * rows, cols), BF16),
            shape((2 * rows, 2 * heads * LANES), BF16),
            shape((rows, width), kind),
        ),
        in_specs=[SMEM]
        + [ANY] * 11
        + [
            pl.BlockSpec((tile, width), lambda i: (i, 0)),
            pl.BlockSpec((16, width), lambda i: (rows // 16, 0)),
        ]
        + [ANY] * len(extra),
        out_specs=(
            pl.BlockSpec((8, tile, cols), lambda i: (0, base + i, 0)),
            pl.BlockSpec((tile, 2 * heads * LANES), lambda i: (base + i, 0)),
            pl.BlockSpec((tile, width), lambda i: (i, 0)),
        ),
        scratch_shapes=[
            pltpu.VMEM((2, 4 * cols + 16, width), BF16),
            pltpu.VMEM((16, 1, LANES), F32),
            pltpu.SemaphoreType.DMA((16,)),
        ],
        input_output_aliases={14: 0, 15: 1} if extra else {},
        compiler_params=params(32, 1),
        cost_estimate=cost(rows * width * cols * 16 + rows * 400000, rows * width * 10 + 5e6),
    )(*args)


def split_gradient(place, source, matrices, send_x, send_y, keep_x, keep_y):
    half = send_x.shape[2]
    for flip in range(4):
        quarter = lax.bitwise_xor(place[0], flip)
        for part in range(2):
            at = pl.ds(pl.multiple_of((2 * quarter + part) * half, 16), half)
            if part == 0:
                ref, index = (keep_x, flip // 2) if flip % 2 == 0 else (send_x, flip // 2)
            else:
                ref, index = (keep_y, flip % 2) if flip < 2 else (send_y, flip % 2)
            for matrix in range(matrices):
                ref[matrix, index, :, :] = source(matrix, at).astype(BF16)


def gradient_outputs(matrices, size, width):
    spec = pl.BlockSpec((matrices, 2, size // 8, width), lambda i: (0, 0, 0, 0))
    return (shape((matrices, 2, size // 8, width), BF16),) * 4, (spec,) * 4


def attention_back_kernel(
    heads,
    place,
    projection,
    mixer,
    piece,
    near0,
    near1,
    near2,
    near3,
    far0,
    far1,
    far2,
    far3,
    normed_mine,
    normed_other,
    grad_mine,
    grad_other,
    saved,
    soft,
    send_x,
    send_y,
    keep_x,
    keep_y,
    back_mine,
    back_other,
    bias_sums,
    weights,
    sums,
    grads,
    sems,
):
    step = pl.program_id(0)
    steps = pl.num_programs(0)
    load_attention(
        place,
        projection,
        mixer,
        piece,
        (near0, near1, near2, near3),
        (far0, far1, far2, far3),
        weights,
        sems,
    )
    cols = heads * HD
    mine = step < steps // 2
    normed = jnp.where(mine, normed_mine[...], normed_other[...])
    grad = jnp.where(mine, grad_mine[...], grad_other[...])

    @pl.when(step == 0)
    def _():
        sums[...] = jnp.zeros_like(sums)
        bias_sums[...] = jnp.zeros_like(bias_sums)

    for slot in range(2):
        grads[4 * slot + 3, :, :] = dot_rows(
            grad, weights[slot, 3 * cols : 4 * cols, :]
        ).astype(BF16)

    lanes = head_lanes(SLOTS, cols)

    def one_image(image, carry):
        at = pl.ds(pl.multiple_of(image * SLOTS, 16), SLOTS)
        for slot in range(2):
            queries = saved[4 * slot, at, :]
            keys = spread_heads(saved[4 * slot + 1, at, :], lanes, heads)
            values = spread_heads(saved[4 * slot + 2, at, :], lanes, heads)
            grad_mixed = grads[4 * slot + 3, at, :]
            low = soft[at, slot * heads * LANES : (slot + 1) * heads * LANES]
            grad_soft = dot_rows(grad_mixed, values)
            lows = []
            for head in range(heads):
                one = low[:, head * LANES : (head + 1) * LANES].astype(F32)
                grad_one = grad_soft[:, head * LANES : (head + 1) * LANES]
                inner = jnp.sum(grad_one * one, axis=-1, keepdims=True)
                lows.append((one * (grad_one - inner) * (HD**-0.5)).astype(BF16))
            grad_scores = jnp.concatenate(lows, axis=1)
            grad_queries = dot(grad_scores, keys)
            grad_values = gather_heads(dot_columns(low, grad_mixed), lanes, heads)
            grad_keys = gather_heads(dot_columns(grad_scores, queries), lanes, heads)
            bias_sums[2 * slot : 2 * slot + 1, :] += jnp.sum(grad_queries, axis=0, keepdims=True)
            bias_sums[2 * slot + 1 : 2 * slot + 2, :] += jnp.sum(
                grad_values, axis=0, keepdims=True
            )
            grads[4 * slot, at, :] = grad_queries.astype(BF16)
            grads[4 * slot + 1, at, :] = grad_keys.astype(BF16)
            grads[4 * slot + 2, at, :] = grad_values.astype(BF16)
        return carry

    lax.fori_loop(0, TILE_IMAGES, one_image, 0, unroll=2)
    back = None
    for slot in range(2):
        for index in range(3):
            at = slice(index * cols, (index + 1) * cols)
            value = grads[4 * slot + index, :, :]
            term = dot(value, weights[slot, at, :])
            back = term if back is None else back + term
            sums[slot, at, :] += dot_columns(value, normed)
        sums[slot, 3 * cols : 4 * cols, :] += dot_columns(saved[4 * slot + 3, :, :], grad)

    @pl.when(mine)
    def _():
        back_mine[...] = back

    @pl.when(jnp.logical_not(mine))
    def _():
        back_other[...] = back.astype(BF16)

    @pl.when(step == steps - 1)
    def _():
        split_gradient(
            place, lambda m, at: sums[m, at, :], 2, send_x, send_y, keep_x, keep_y
        )


def half_spec(tile, width, tiles, second):
    if second:
        return pl.BlockSpec((tile, width), lambda i: (jnp.maximum(i - tiles, 0), 0))
    return pl.BlockSpec((tile, width), lambda i: (jnp.minimum(i, tiles - 1), 0))


def attention_back(place, own, near, far, normed, grads, saved, soft):
    projection, mixer, piece = own
    cols, width = mixer.shape
    heads = cols // HD
    rows = grads[0].shape[0]
    tile = TILE_IMAGES * SLOTS
    tiles = rows // tile
    mine, other = half_spec(tile, width, tiles, False), half_spec(tile, width, tiles, True)
    grad_shapes, grad_specs = gradient_outputs(2, 4 * cols, width)
    return pl.pallas_call(
        functools.partial(attention_back_kernel, heads),
        grid=(2 * tiles,),
        out_shape=(
            *grad_shapes,
            shape((rows, width), F32),
            shape((rows, width), BF16),
            shape((8, cols), F32),
        ),
        in_specs=[SMEM]
        + [ANY] * 11
        + [
            mine,
            other,
            mine,
            other,
            pl.BlockSpec((8, tile, cols), lambda i: (0, i, 0)),
            pl.BlockSpec((tile, 2 * heads * LANES), lambda i: (i, 0)),
        ],
        out_specs=(*grad_specs, mine, other, fixed_spec(8, cols)),
        scratch_shapes=[
            pltpu.VMEM((2, 4 * cols + 16, width), BF16),
            pltpu.VMEM((2, 4 * cols, width), F32),
            pltpu.VMEM((8, tile, cols), BF16),
            pltpu.SemaphoreType.DMA((16,)),
        ],
        compiler_params=params(48, 1),
        cost_estimate=cost(rows * width * cols * 60 + rows * 1.2e6, rows * width * 20 + 8e6),
    )(place, projection, mixer, piece, *near, *far, *normed, *grads, saved, soft)


def hidden_kernel(
    whole,
    last,
    place,
    up,
    down,
    piece,
    piece0,
    piece1,
    piece2,
    piece3,
    normed_mine,
    normed_other,
    grad_mine,
    grad_other,
    *rest,
):
    if last:
        out_in, back_in = rest[:2]
        rest = rest[2:]
        send_x, send_y, keep_x, keep_y, bias_sums = rest[:5]
        out_mine, out_other, back_mine, back_other = rest[5:9]
        rest = rest[9:]
    else:
        send_x, send_y, keep_x, keep_y, bias_sums = rest[:5]
        out_sum, back_sum = rest[5:7]
        rest = rest[7:]
    weights, sums_up, sums_down, out_part, back_part, sems = rest
    step = pl.program_id(0)
    steps = pl.num_programs(0)
    width = normed_mine.shape[1]

    @pl.when(step == 0)
    def _():
        pieces = (piece0, piece1, piece2, piece3)
        if whole:

            @pl.when(place[1] == 0)
            def _():
                run_copies(shard_copies((up, down), piece, weights, sems))

            @pl.when(place[1] != 0)
            def _():
                run_copies(piece_copies(place, pieces, weights, 2, sems))

        else:
            run_copies(piece_copies(place, pieces, weights, 2, sems))
        sums_up[...] = jnp.zeros_like(sums_up)
        sums_down[...] = jnp.zeros_like(sums_down)
        bias_sums[...] = jnp.zeros_like(bias_sums)

    mine = step < steps // 2
    normed = jnp.where(mine, normed_mine[...], normed_other[...])
    grad = jnp.where(mine, grad_mine[...], grad_other[...])
    bias_rows = weights[2 * width : 2 * width + 16, :].astype(F32)
    chunk = 256
    for first in range(0, width, chunk):
        columns = slice(first, first + chunk)
        up_part = weights[0:width, columns]
        down_part = weights[width + first : width + first + chunk, :]
        hidden = dot(normed, up_part) + bias_rows[0:1, columns]
        phi = 0.5 + 0.5 * lax.erf(hidden * (0.5**0.5))
        slope = phi + hidden * (jnp.exp(-0.5 * hidden * hidden) * ((2.0 * np.pi) ** -0.5))
        active = (hidden * phi).astype(BF16)
        grad_pre = dot_rows(grad, down_part) * slope
        bias_sums[0:1, columns] += jnp.sum(grad_pre, axis=0, keepdims=True)
        grad_low = grad_pre.astype(BF16)
        out_term = dot(active, down_part)
        back_term = dot_rows(grad_low, up_part)
        if first == 0:
            if last:
                out_part[...] = out_in[...] + out_term
                back_part[...] = back_in[...] + back_term
            else:
                out_part[...] = out_term
                back_part[...] = back_term
        else:
            out_part[...] += out_term
            back_part[...] += back_term
        sums_up[:, columns] += dot_columns(normed, grad_low)
        sums_down[columns, :] += dot_columns(active, grad)

    if last:

        @pl.when(mine)
        def _():
            out_mine[...] = out_part[...]
            back_mine[...] = back_part[...]

        @pl.when(jnp.logical_not(mine))
        def _():
            out_other[...] = out_part[...].astype(BF16)
            back_other[...] = back_part[...].astype(BF16)

    else:
        out_sum[...] = out_part[...]
        back_sum[...] = back_part[...]

    @pl.when(step == steps - 1)
    def _():
        split_gradient(
            place,
            lambda m, at: (sums_up if m == 0 else sums_down)[at, :],
            2,
            send_x,
            send_y,
            keep_x,
            keep_y,
        )


def hidden_block(place, own, pieces, normed, grads, sums_before, whole):
    up, down, piece = own
    width = up.shape[0]
    rows = normed[0].shape[0]
    tile = TILE_IMAGES * SLOTS
    tiles = rows // tile
    last = sums_before is not None
    mine, other = half_spec(tile, width, tiles, False), half_spec(tile, width, tiles, True)
    both = rows_spec(tile, width)
    grad_shapes, grad_specs = gradient_outputs(2, width, width)
    if last:
        more_shapes = (
            shape((rows, width), F32),
            shape((rows, width), BF16),
            shape((rows, width), F32),
            shape((rows, width), BF16),
        )
        more_specs = (mine, other, mine, other)
    else:
        more_shapes = (shape((2 * rows, width), F32),) * 2
        more_specs = (both, both)
    return pl.pallas_call(
        functools.partial(hidden_kernel, whole, last),
        grid=(2 * tiles,),
        out_shape=(*grad_shapes, shape((8, width), F32), *more_shapes),
        in_specs=[SMEM]
        + [ANY] * 7
        + [mine, other, mine, other]
        + ([both, both] if last else []),
        out_specs=(*grad_specs, fixed_spec(8, width), *more_specs),
        scratch_shapes=[
            pltpu.VMEM((2 * width + 16, width), BF16),
            pltpu.VMEM((width, width), F32),
            pltpu.VMEM((width, width), F32),
            pltpu.VMEM((tile, width), F32),
            pltpu.VMEM((tile, width), F32),
            pltpu.SemaphoreType.DMA((16,)),
        ],
        compiler_params=params(52, 1),
        cost_estimate=cost(rows * width * width * 24, rows * width * 24 + 8e6),
    )(place, up, down, piece, *pieces, *normed, *grads, *(sums_before or ()))


def finish_kernel(place, mine, other, *outs):
    half = mine.shape[2]
    for flip in range(4):
        quarter = lax.bitwise_xor(place[0], flip)
        for side, ref in enumerate((mine, other)):
            part = place[1] if side == 0 else 1 - place[1]
            for matrix, out in enumerate(outs):
                at = pl.ds(pl.multiple_of((2 * quarter + part) * half, 8), half)
                out[at, :] = ref[flip, matrix, :, :].astype(F32)


def finish(place, mine, other):
    matrices, half, width = mine.shape[1:]
    return pl.pallas_call(
        finish_kernel,
        out_shape=(shape((8 * half, width), F32),) * matrices,
        in_specs=[SMEM, VMEM, VMEM],
        out_specs=(VMEM,) * matrices,
        compiler_params=params(32),
        cost_estimate=cost(0, matrices * half * width * 48),
    )(place, mine, other)


def local(
    tokens,
    visible_counts,
    norm_one_gain,
    norm_one_shift,
    input_weight,
    input_bias,
    mixer_weight,
    mixer_bias,
    norm_two_gain,
    norm_two_shift,
    up_weight,
    up_bias,
    down_weight,
    down_bias,
    output_grad,
    groups,
    outer,
):
    width = tokens.shape[1]
    rows = tokens.shape[0]
    cols = mixer_weight.shape[0]
    t = lax.axis_index("t")
    core = lax.axis_index("c")
    place = jnp.stack([2 * lax.axis_index("a") + lax.axis_index("b"), core, t]).astype(jnp.int32)
    one_row = lambda v: v.reshape(1, -1)

    swap = [(0, 1), (1, 0)]
    cross = [(0, 3), (1, 2), (2, 1), (3, 0)]
    to_near = [(z, (z + 1) % groups) for z in range(groups)] + [
        (groups + z, groups + (z + 2) % groups) for z in range(groups)
    ]
    to_far = [(groups + z, groups + (z + 3) % groups) for z in range(groups)]
    back_near = [(j, i) for i, j in to_near]
    back_far = [(j, i) for i, j in to_far]
    flip_x = [(2 * i + 1, 2 * (i ^ 1) + 1) for i in range(4)]
    flip_y = [(2 * i + 1, 2 * (i ^ 2) + 1) for i in range(4)]
    flip_xy = [(2 * i + 1, 2 * (i ^ 3) + 1) for i in range(4)]

    def spread(piece):
        return (
            piece,
            lax.ppermute(piece, "b", swap),
            lax.ppermute(piece, "a", swap),
            lax.ppermute(piece, ("a", "b"), cross),
        )

    def spread_second(piece):
        return (
            piece,
            lax.ppermute(piece, ("a", "b", "c"), flip_x),
            lax.ppermute(piece, ("a", "b", "c"), flip_y),
            lax.ppermute(piece, ("a", "b", "c"), flip_xy),
        )

    projection = input_weight.transpose(1, 2, 0).reshape(3 * cols, width)
    piece_one = pack_attention(place, projection, mixer_weight, input_bias)
    near_one = spread(lax.ppermute(piece_one, ("c", "t"), to_near))
    far_one = spread_second(lax.ppermute(piece_one, ("c", "t"), to_far))
    normed_one = norm_one(
        place, visible_counts, tokens, one_row(norm_one_gain), one_row(norm_one_shift)
    )
    normed_other = lax.ppermute(normed_one, "c", swap)
    piece_two = pack_hidden(place, up_weight, down_weight, one_row(up_bias))
    near_two = spread(lax.ppermute(piece_two, ("c", "t"), to_near))
    far_two = spread_second(lax.ppermute(piece_two, ("c", "t"), to_far))
    grad_other = lax.ppermute(output_grad, "c", swap)

    own_one = (projection, mixer_weight, piece_one)
    saved, soft, part = attention(place, own_one, near_one, far_one, normed_other, None, BF16)
    part_received = lax.ppermute(part, "c", swap)
    saved, soft, part = attention(
        place, own_one, near_one, far_one, normed_one, (saved, soft), F32
    )
    first_sum, normed_two = norm_two(
        tokens,
        part,
        part_received,
        one_row(mixer_bias),
        one_row(norm_two_gain),
        one_row(norm_two_shift),
    )
    normed_two_both = (normed_two, lax.ppermute(normed_two, "c", swap))

    own_two = (up_weight, down_weight, piece_two)
    grad_both = (output_grad, grad_other)
    *grads_near, bias_near, out_sum, back_sum = hidden_block(
        place, own_two, near_two, normed_two_both, grad_both, None, False
    )
    *grads_far, bias_far, out_mine, out_send, back_mine, back_send = hidden_block(
        place, own_two, far_two, normed_two_both, grad_both, (out_sum, back_sum), True
    )
    back_received = lax.ppermute(back_send, "c", swap)
    grad_first, grad_first_low, sums_two = norm_two_back(
        back_mine, back_received, first_sum, one_row(norm_two_gain), output_grad
    )
    out_received = lax.ppermute(out_send, "c", swap)
    result = (first_sum + (out_mine + out_received.astype(F32)) + down_bias).astype(BF16)

    first_both = (grad_first_low, lax.ppermute(grad_first_low, "c", swap))
    *grads_one, back_mine, back_send, bias_one = attention_back(
        place, own_one, near_one, far_one, (normed_one, normed_other), first_both, saved, soft
    )
    back_received = lax.ppermute(back_send, "c", swap)
    grad_tokens, sums_one = norm_one_back(
        back_mine, back_received, tokens, one_row(norm_one_gain), grad_first
    )

    def plane_sum(send_x, send_y, keep_x, keep_y):
        got_x = lax.ppermute(send_x, "b", swap)
        got_y = lax.ppermute(send_y, "a", swap)
        add = lambda u, v: u.astype(F32) + v.astype(F32)
        next_y = lax.ppermute(add(keep_x[:, 1], got_x[:, 1]).astype(BF16), "a", swap)
        next_x = lax.ppermute(add(keep_y[:, 1], got_y[:, 1]).astype(BF16), "b", swap)
        first = (add(keep_x[:, 0], got_x[:, 0]) + next_y.astype(F32)).astype(BF16)
        second = (add(keep_y[:, 0], got_y[:, 0]) + next_x.astype(F32)).astype(BF16)
        return jnp.stack([first, second])

    is_first = core == 0

    def depth_sum(local_far, far, near):
        total = jnp.where(is_first, local_far, far).astype(F32) + near.astype(F32)
        keep = jnp.where(is_first, total[0], total[1])
        send = jnp.where(is_first, total[1], total[0]).astype(BF16)
        total = keep + lax.ppermute(send, "c", swap).astype(F32)
        if outer > 1:
            total = lax.psum(total, "o")
        return total.astype(BF16)

    def collect(part):
        mine = jnp.stack(spread(part))
        return finish(place, mine, lax.ppermute(mine, "c", swap))

    plane_near = plane_sum(*grads_near)
    plane_far = plane_sum(*grads_far)
    depth_near = lax.ppermute(plane_near, ("c", "t"), back_near)
    depth_far = lax.ppermute(plane_far, ("c", "t"), back_far)
    grad_up, grad_down = collect(depth_sum(plane_far, depth_far, depth_near))

    plane_one = plane_sum(*grads_one)
    far_part, near_part = plane_one[:, 0:1], plane_one[:, 1:2]
    depth_near = lax.ppermute(near_part, ("c", "t"), back_near)
    depth_far = lax.ppermute(far_part, ("c", "t"), back_far)
    (grad_block,) = collect(depth_sum(far_part, depth_far, depth_near))
    grad_input = grad_block[: 3 * cols].reshape(3, cols, width).transpose(2, 0, 1)
    grad_mixer = grad_block[3 * cols :]

    near_owner = jnp.where(is_first, t - 1, t - 2) % groups
    far_owner = jnp.where(is_first, t, t - 3) % groups
    owners = jnp.arange(groups)[:, None]
    by_owner = lambda near, far: jnp.where(owners == near_owner, near, 0.0) + jnp.where(
        owners == far_owner, far, 0.0
    )
    wide = lambda v: jnp.pad(v.reshape(1, -1), ((0, 0), (0, width - v.size)))
    bias_rows = by_owner(bias_near[0:1], bias_far[0:1])
    input_rows = by_owner(wide(bias_one[2:4]), wide(bias_one[0:2]))
    vectors = jnp.concatenate([sums_one[0:2], sums_two[0:4], bias_rows, input_rows])
    for axis in ("c", "b", "a"):
        vectors = vectors + lax.ppermute(vectors, axis, swap)
    turns = [
        lax.ppermute(vectors, "t", [(z, (z + k) % groups) for z in range(groups)])
        for k in range(1, groups)
    ]
    for turn in turns:
        vectors = vectors + turn
    if outer > 1:
        vectors = lax.psum(vectors, "o")
    grad_up_bias = lax.dynamic_slice_in_dim(vectors, 6 + t, 1)[0]
    grad_input_bias = lax.dynamic_slice_in_dim(vectors, 6 + groups + t, 1)[0, : 2 * cols].reshape(
        2, cols
    )
    return (
        result,
        grad_tokens,
        vectors[0],
        vectors[1],
        grad_input,
        grad_input_bias,
        grad_mixer,
        vectors[4],
        vectors[2],
        vectors[3],
        grad_up,
        grad_up_bias,
        grad_down,
        vectors[5],
    )


def solution(mesh):
    dp, groups = mesh.shape["dp"], mesh.shape["tensor"]
    outer = dp // 8
    split = jax.sharding.Mesh(
        mesh.devices.reshape(outer, 2, 2, 2, groups), ("o", "a", "b", "c", "t")
    )
    dp_axes = ("o", "a", "b", "c")
    all_axes = dp_axes + ("t",)
    in_specs = (
        P(all_axes, None),
        P(dp_axes),
        P(),
        P(),
        P(None, None, "t"),
        P(None, "t"),
        P("t", None),
        P(),
        P(),
        P(),
        P(None, "t"),
        P("t"),
        P("t", None),
        P(),
        P(all_axes, None),
    )
    out_specs = (
        P(all_axes, None),
        P(all_axes, None),
        P(),
        P(),
        P(None, None, "t"),
        P(None, "t"),
        P("t", None),
        P(),
        P(),
        P(),
        P(None, "t"),
        P("t"),
        P("t", None),
        P(),
    )
    return jax.shard_map(
        functools.partial(local, groups=groups, outer=outer),
        mesh=split,
        in_specs=in_specs,
        out_specs=out_specs,
        check_vma=False,
    )
```

```python
import functools

import jax
import jax.numpy as jnp
import numpy as np
from jax import lax
from jax.experimental import pallas as pl
from jax.experimental.pallas import tpu as pltpu
from jax.sharding import PartitionSpec as P

HD = 64
SLOTS = 80
LANES = 128
TILE_IMAGES = 4
MASKED = -1000000000.0
EPS = 1e-06
F32 = jnp.float32
BF16 = jnp.bfloat16

ANY = pl.BlockSpec(memory_space=pl.ANY)
SMEM = pl.BlockSpec(memory_space=pltpu.SMEM)
VMEM = pl.BlockSpec(memory_space=pltpu.VMEM)


def shape(dims, kind):
    return jax.ShapeDtypeStruct(tuple(dims), kind)


def kept(dims, kind):
    return pltpu.HBM(tuple(dims), kind)


def from_hbm(*arrays):
    return tuple(pltpu.with_memory_space_constraint(a, pltpu.HBM) for a in arrays)


def params(megabytes, grid_dims=0):
    semantics = ("arbitrary",) * grid_dims if grid_dims else None
    return pltpu.CompilerParams(
        vmem_limit_bytes=megabytes * 1024 * 1024, dimension_semantics=semantics
    )


def cost(flops, moved):
    return pl.CostEstimate(flops=int(flops), bytes_accessed=int(moved), transcendentals=0)


def dot(left, right):
    return lax.dot_general(left, right, (((1,), (0,)), ((), ())), preferred_element_type=F32)


def dot_rows(left, right):
    return lax.dot_general(left, right, (((1,), (1,)), ((), ())), preferred_element_type=F32)


def dot_columns(left, right):
    return lax.dot_general(left, right, (((0,), (0,)), ((), ())), preferred_element_type=F32)


def centred(rows):
    center = rows - jnp.mean(rows, axis=-1, keepdims=True)
    spread = jnp.mean(center * center, axis=-1, keepdims=True)
    return center, lax.rsqrt(spread + EPS)


def norm_back(rows, gain, grad):
    center, rstd = centred(rows)
    xhat = center * rstd
    e = grad * gain
    back = rstd * (
        e - jnp.mean(e, axis=-1, keepdims=True) - xhat * jnp.mean(e * xhat, axis=-1, keepdims=True)
    )
    return (
        back,
        jnp.sum(grad * xhat, axis=0, keepdims=True),
        jnp.sum(grad, axis=0, keepdims=True),
    )


def norm_one_kernel(images, chunk, place, counts, tokens, gain, shift, out):
    rows = tokens.shape[0]

    @pl.loop(0, rows // chunk)
    def _(step):
        at = pl.ds(pl.multiple_of(step * chunk, chunk), chunk)
        center, rstd = centred(tokens[at, :].astype(F32))
        out[at, :] = (center * rstd * gain[...] + shift[...]).astype(BF16)

    extra = out.shape[0] - rows
    row = lax.broadcasted_iota(jnp.int32, (extra, out.shape[1]), 0)
    table = jnp.zeros((extra, out.shape[1]), F32)
    first = place[2] * images
    for image in range(images):
        table = jnp.where(row == image, counts[first + image].astype(F32), table)
    out[rows:, :] = table.astype(BF16)


def norm_one(place, counts, tokens, gain, shift):
    rows, width = tokens.shape
    images = rows // SLOTS
    return pl.pallas_call(
        functools.partial(norm_one_kernel, images, SLOTS),
        out_shape=shape((rows + 16, width), BF16),
        in_specs=[SMEM, SMEM, VMEM, VMEM, VMEM],
        out_specs=VMEM,
        compiler_params=params(16),
        cost_estimate=cost(rows * width * 10, rows * width * 4),
    )(place, counts, tokens, gain, shift)


def norm_two_kernel(tokens, mine, received, bias, gain, shift, first_sum, normed):
    total = tokens[...].astype(F32) + (mine[...] + received[...].astype(F32)) + bias[...]
    first_sum[...] = total
    center, rstd = centred(total)
    normed[...] = (center * rstd * gain[...] + shift[...]).astype(BF16)


def rows_spec(tile, width):
    return pl.BlockSpec((tile, width), lambda i: (i, 0))


def fixed_spec(*dims):
    return pl.BlockSpec(dims, lambda i: (0,) * len(dims))


def norm_two(tokens, mine, received, bias, gain, shift):
    rows, width = tokens.shape
    tile = 2 * SLOTS
    row = rows_spec(tile, width)
    vector = fixed_spec(1, width)
    return pl.pallas_call(
        norm_two_kernel,
        grid=(rows // tile,),
        out_shape=(kept((rows, width), F32), shape((rows, width), BF16)),
        in_specs=[row, row, row, vector, vector, vector],
        out_specs=(row, row),
        compiler_params=params(16, 1),
        cost_estimate=cost(rows * width * 12, rows * width * 14),
    )(*from_hbm(tokens), mine, received, bias, gain, shift)


def norm_two_back_kernel(mine, received, first_sum, gain, output_grad, grad_first, low, sums):
    grad = mine[...] + received[...].astype(F32)
    back, grad_gain, grad_shift = norm_back(first_sum[...], gain[...], grad)
    out_grad = output_grad[...].astype(F32)
    total = out_grad + back
    grad_first[...] = total
    low[...] = total.astype(BF16)

    @pl.when(pl.program_id(0) == 0)
    def _():
        sums[...] = jnp.zeros_like(sums)

    sums[0:1, :] += grad_gain
    sums[1:2, :] += grad_shift
    sums[2:3, :] += jnp.sum(total, axis=0, keepdims=True)
    sums[3:4, :] += jnp.sum(out_grad, axis=0, keepdims=True)


def norm_two_back(mine, received, first_sum, gain, output_grad):
    rows, width = mine.shape
    tile = 2 * SLOTS
    row = rows_spec(tile, width)
    return pl.pallas_call(
        norm_two_back_kernel,
        grid=(rows // tile,),
        out_shape=(kept((rows, width), F32), shape((rows, width), BF16), shape((8, width), F32)),
        in_specs=[row, row, row, fixed_spec(1, width), row],
        out_specs=(row, row, fixed_spec(8, width)),
        compiler_params=params(16, 1),
        cost_estimate=cost(rows * width * 25, rows * width * 18),
    )(mine, received, *from_hbm(first_sum), gain, *from_hbm(output_grad))


def norm_one_back_kernel(
    groups,
    place,
    mine,
    received,
    tokens,
    gain,
    grad_first,
    sums_two,
    bias_near,
    bias_far,
    input_near,
    input_far,
    grad_tokens,
    vectors,
):
    grad = mine[...] + received[...].astype(F32)
    back, grad_gain, grad_shift = norm_back(tokens[...].astype(F32), gain[...], grad)
    grad_tokens[...] = grad_first[...] + back

    @pl.when(pl.program_id(0) == 0)
    def _():
        near = lax.rem(place[2] - 1 - place[1] + groups, groups)
        far = lax.rem(place[2] - 3 * place[1] + groups, groups)
        row = lax.broadcasted_iota(jnp.int32, vectors.shape, 0)
        table = jnp.zeros(vectors.shape, F32)
        for index in range(4):
            table = jnp.where(row == 2 + index, sums_two[index : index + 1, :], table)
        table = jnp.where(row == 6 + near, bias_near[0:1, :], table)
        vectors[...] = jnp.where(row == 6 + far, bias_far[0:1, :], table)
        columns = input_near.shape[1]
        few = lax.broadcasted_iota(jnp.int32, (vectors.shape[0], columns), 0)
        for index in range(2):
            table = jnp.where(
                few == 6 + groups + near, input_near[index : index + 1, :], 0.0
            ) + jnp.where(few == 6 + groups + far, input_far[index : index + 1, :], 0.0)
            vectors[:, 2 * index * LANES : 2 * index * LANES + columns] += table

    vectors[0:1, :] += grad_gain
    vectors[1:2, :] += grad_shift


def norm_one_back(groups, place, mine, received, tokens, gain, grad_first, *small):
    rows, width = mine.shape
    tile = 2 * SLOTS
    row = rows_spec(tile, width)
    return pl.pallas_call(
        functools.partial(norm_one_back_kernel, groups),
        grid=(rows // tile,),
        out_shape=(kept((rows, width), F32), shape((16, width), F32)),
        in_specs=[SMEM, row, row, row, fixed_spec(1, width), row]
        + [fixed_spec(*array.shape) for array in small],
        out_specs=(row, fixed_spec(16, width)),
        compiler_params=params(16, 1),
        cost_estimate=cost(rows * width * 25, rows * width * 16),
    )(place, mine, received, *from_hbm(tokens), gain, *from_hbm(grad_first), *small)


def pack_attention_kernel(place, projection, mixer, bias, up_bias, out, tail, sem, tail_sem):
    quarter = place[0]
    tail_copy = pltpu.make_async_copy(mixer, tail.at[pl.ds(0, mixer.shape[0])], tail_sem)
    tail_copy.start()
    size = out.shape[0] - 16
    feature_rows = projection.shape[0]
    first = pl.multiple_of(quarter * size, 16)
    from_projection = quarter * size < feature_rows

    @pl.when(from_projection)
    def _():
        copy = pltpu.make_async_copy(
            projection.at[pl.ds(first, size)], out.at[pl.ds(0, size)], sem
        )
        copy.start()
        copy.wait()

    @pl.when(jnp.logical_not(from_projection))
    def _():
        copy = pltpu.make_async_copy(mixer, out.at[pl.ds(0, size)], sem)
        copy.start()
        copy.wait()

    columns = bias.shape[1]
    row = lax.broadcasted_iota(jnp.int32, (16, columns), 0)
    both = bias[...].astype(F32)
    rows = jnp.where(row == 0, both[0:1, :], jnp.where(row == 1, both[1:2, :], 0.0))
    row_all = lax.broadcasted_iota(jnp.int32, (16, out.shape[1]), 0)
    out[size:, :] = jnp.where(row_all == 2, up_bias[...].astype(F32), 0.0).astype(BF16)
    row_two = jnp.where(row == 2, up_bias[:, 0:columns].astype(F32), rows)
    out[size:, 0:columns] = row_two.astype(BF16)
    tail[size:, :] = out[size:, :]
    tail_copy.wait()


def pack_attention(place, projection, mixer, bias, up_bias):
    size, width = mixer.shape
    return pl.pallas_call(
        pack_attention_kernel,
        out_shape=(shape((size + 16, width), BF16),) * 2,
        in_specs=[SMEM, ANY, ANY, VMEM, VMEM],
        out_specs=(VMEM, VMEM),
        scratch_shapes=[pltpu.SemaphoreType.DMA(()), pltpu.SemaphoreType.DMA(())],
        compiler_params=params(16),
        cost_estimate=cost(0, 2 * size * width),
    )(place, *from_hbm(projection, mixer), bias, up_bias)


def pack_hidden_kernel(place, up, down, out, sems):
    size = out.shape[0] // 2
    first = pl.multiple_of(place[0] * size, 16)
    copies = [
        pltpu.make_async_copy(
            source.at[pl.ds(first, size)], out.at[pl.ds(index * size, size)], sems.at[index]
        )
        for index, source in enumerate((up, down))
    ]
    run_copies(copies)


def pack_hidden(place, up, down):
    size, width = up.shape[0] // 4, up.shape[1]
    return pl.pallas_call(
        pack_hidden_kernel,
        out_shape=shape((2 * size, width), BF16),
        in_specs=[SMEM, ANY, ANY],
        out_specs=VMEM,
        scratch_shapes=[pltpu.SemaphoreType.DMA((2,))],
        compiler_params=params(16),
        cost_estimate=cost(0, 4 * size * width),
    )(place, *from_hbm(up, down))


def run_copies(copies):
    for copy in copies:
        copy.start()
    for copy in copies:
        copy.wait()


def make_copies(copies, sems):
    return [
        pltpu.make_async_copy(source, to, sems.at[index])
        for index, (source, to) in enumerate(copies)
    ]


def piece_copies(place, pieces, target, sems):
    size = pieces[0].shape[0] - 16
    copies = []
    for flip, piece in enumerate(pieces):
        to = pl.multiple_of(lax.bitwise_xor(place[0], flip) * size, 16)
        copies.append((piece.at[pl.ds(0, size)], target.at[pl.ds(to, size)]))
    copies.append((pieces[0].at[pl.ds(size, 16)], target.at[pl.ds(4 * size, 16)]))
    return make_copies(copies, sems)


def hidden_copies(place, pieces, bias_piece, target, sems):
    size = pieces[0].shape[0] // 2
    copies = []
    for flip in range(4):
        quarter = lax.bitwise_xor(place[0], flip)
        for matrix in range(2):
            to = pl.multiple_of((4 * matrix + quarter) * size, 16)
            source = pieces[3 + matrix] if flip == 3 else pieces[flip].at[pl.ds(matrix * size, size)]
            copies.append((source, target.at[pl.ds(to, size)]))
    first = bias_piece.shape[0] - 16
    copies.append((bias_piece.at[pl.ds(first, 16)], target.at[pl.ds(8 * size, 16)]))
    return make_copies(copies, sems)


def head_lanes(rows, width):
    return lax.broadcasted_iota(jnp.int32, (rows, width), 1) // HD


def spread_heads(block, lanes, heads):
    gap = jnp.zeros((LANES - SLOTS, block.shape[1]), block.dtype)
    parts = []
    for head in range(heads):
        parts.append(jnp.where(lanes == head, block, jnp.zeros_like(block)))
        parts.append(gap)
    return jnp.concatenate(parts, axis=0)


def gather_heads(product, lanes, heads):
    total = product[0:SLOTS]
    for head in range(1, heads):
        total = jnp.where(lanes == head, product[head * LANES : head * LANES + SLOTS], total)
    return total


def load_far(place, own, far, target, sems, bias_only):
    def copies(parts):
        at, out = 0, []
        for index, part in enumerate(parts):
            skip = part.shape[0] - 16 if bias_only and index == 2 else 0
            size = part.shape[0] - skip
            out.append((part.at[pl.ds(skip, size)], target.at[pl.ds(at, size)]))
            at += size
        return make_copies(out, sems)

    @pl.when(place[1] == 0)
    def _():
        run_copies(copies(own))

    @pl.when(place[1] != 0)
    def _():
        run_copies(copies(far))


def attention_kernel(
    heads,
    place,
    projection,
    tail,
    near0,
    near1,
    near2,
    near3,
    far0,
    far1,
    normed,
    counts,
    *rest,
):
    saved, soft, part, weights, table, sems = rest[-6:]

    @pl.when(pl.program_id(0) == 0)
    def _():
        copies = piece_copies(place, (near0, near1, near2, near3), weights.at[1], sems)
        for copy in copies:
            copy.start()
        far_sems = sems.at[pl.ds(8, 8)]
        load_far(place, (projection, tail), (far0, far1), weights.at[0], far_sems, False)
        for copy in copies:
            copy.wait()

    cols = heads * HD
    visible_rows = counts[:, 0:LANES].astype(F32)
    for image in range(visible_rows.shape[0]):
        table[image, :, :] = visible_rows[image : image + 1, :]
    rows = normed[...]
    for slot in range(2):
        for index in range(3):
            value = dot_rows(rows, weights[slot, index * cols : (index + 1) * cols, :])
            if index != 1:
                bias_row = 0 if index == 0 else 1
                bias = weights[slot, 4 * cols : 4 * cols + 16, 0:cols].astype(F32)
                value = value + bias[bias_row : bias_row + 1, :]
            saved[4 * slot + index, :, :] = value.astype(BF16)

    lanes = head_lanes(SLOTS, cols)
    key_index = lax.broadcasted_iota(jnp.int32, (SLOTS, LANES), 1).astype(F32)
    first = pl.program_id(0) * TILE_IMAGES

    def one_image(image, carry):
        at = pl.ds(pl.multiple_of(image * SLOTS, 16), SLOTS)
        visible = key_index < table[first + image]
        for slot in range(2):
            queries = saved[4 * slot, at, :]
            keys = spread_heads(saved[4 * slot + 1, at, :], lanes, heads)
            values = spread_heads(saved[4 * slot + 2, at, :], lanes, heads)
            scores = dot_rows(queries, keys) * (HD**-0.5)
            lows = []
            for head in range(heads):
                one = jnp.where(visible, scores[:, head * LANES : (head + 1) * LANES], MASKED)
                exponent = jnp.exp(one - jnp.max(one, axis=-1, keepdims=True))
                total = jnp.sum(exponent, axis=-1, keepdims=True)
                lows.append((exponent / total).astype(BF16))
            low = jnp.concatenate(lows, axis=1)
            soft[at, slot * heads * LANES : (slot + 1) * heads * LANES] = low
            saved[4 * slot + 3, at, :] = dot(low, values).astype(BF16)
        return carry

    lax.fori_loop(0, TILE_IMAGES, one_image, 0, unroll=2)
    total = dot(saved[3, :, :], weights[0, 3 * cols : 4 * cols, :])
    total = total + dot(saved[7, :, :], weights[1, 3 * cols : 4 * cols, :])
    part[...] = total.astype(part.dtype)


def attention(place, own, near, far, normed, before, kind):
    projection, tail = own
    cols, width = projection.shape[0] // 3, projection.shape[1]
    heads = cols // HD
    rows = normed.shape[0] - 16
    tile = TILE_IMAGES * SLOTS
    tiles = rows // tile
    base = tiles if before is None else 0
    extra = () if before is None else from_hbm(*before)
    args = (place, projection, tail, *near, *far, normed, normed, *extra)
    return pl.pallas_call(
        functools.partial(attention_kernel, heads),
        grid=(tiles,),
        out_shape=(
            kept((8, 2 * rows, cols), BF16),
            kept((2 * rows, 2 * heads * LANES), BF16),
            shape((rows, width), kind),
        ),
        in_specs=[SMEM]
        + [ANY] * 8
        + [
            pl.BlockSpec((tile, width), lambda i: (i, 0)),
            pl.BlockSpec((16, width), lambda i: (rows // 16, 0)),
        ]
        + [ANY] * len(extra),
        out_specs=(
            pl.BlockSpec((8, tile, cols), lambda i: (0, base + i, 0)),
            pl.BlockSpec((tile, 2 * heads * LANES), lambda i: (base + i, 0)),
            pl.BlockSpec((tile, width), lambda i: (i, 0)),
        ),
        scratch_shapes=[
            pltpu.VMEM((2, 4 * cols + 16, width), BF16),
            pltpu.VMEM((16, 1, LANES), F32),
            pltpu.SemaphoreType.DMA((16,)),
        ],
        input_output_aliases={11: 0, 12: 1} if extra else {},
        compiler_params=params(20, 1),
        cost_estimate=cost(rows * width * cols * 16 + rows * 400000, rows * width * 10 + 5e6),
    )(*args)


def split_gradient(place, source, matrices, send_x, send_y, keep_x, keep_y):
    half = send_x.shape[2]
    for flip in range(4):
        quarter = lax.bitwise_xor(place[0], flip)
        for part in range(2):
            at = pl.ds(pl.multiple_of((2 * quarter + part) * half, 16), half)
            if part == 0:
                ref, index = (keep_x, flip // 2) if flip % 2 == 0 else (send_x, flip // 2)
            else:
                ref, index = (keep_y, flip % 2) if flip < 2 else (send_y, flip % 2)
            for matrix in range(matrices):
                ref[index, matrix, :, :] = source(matrix, at).astype(BF16)


def gradient_outputs(matrices, size, width):
    spec = pl.BlockSpec((2, matrices, size // 8, width), lambda i: (0, 0, 0, 0))
    return (shape((2, matrices, size // 8, width), BF16),) * 4, (spec,) * 4


def attention_back_kernel(heads, far, last, place, *rest):
    count = 4
    pieces, rest = rest[:count], rest[count:]
    normed_mine, normed_other, grad_mine, grad_other, saved, soft = rest[:6]
    rest = rest[6:]
    if last:
        back_in, rest = rest[0], rest[1:]
    keep, send_x, send_y, send_xy, bias_sums = rest[:5]
    rest = rest[5:]
    if last:
        back_mine, back_other = rest[:2]
        rest = rest[2:]
    else:
        back_sum, rest = rest[0], rest[1:]
    weights, sums, grads, sems = rest
    step = pl.program_id(0)
    steps = pl.num_programs(0)
    cols = heads * HD
    mine = step < steps // 2

    @pl.when(step == 0)
    def _():
        if far:
            load_far(place, pieces[:2], pieces[2:], weights, sems, False)
        else:
            run_copies(piece_copies(place, pieces, weights, sems))
        sums[...] = jnp.zeros_like(sums)
        bias_sums[...] = jnp.zeros_like(bias_sums)

    normed = jnp.where(mine, normed_mine[...], normed_other[...])
    grad = jnp.where(mine, grad_mine[...], grad_other[...])
    grads[3, :, :] = dot_rows(grad, weights[3 * cols : 4 * cols, :]).astype(BF16)
    lanes = head_lanes(SLOTS, cols)

    def one_image(image, carry):
        at = pl.ds(pl.multiple_of(image * SLOTS, 16), SLOTS)
        queries = saved[0, at, :]
        keys = spread_heads(saved[1, at, :], lanes, heads)
        values = spread_heads(saved[2, at, :], lanes, heads)
        grad_mixed = grads[3, at, :]
        low = soft[at, :]
        grad_soft = dot_rows(grad_mixed, values)
        lows = []
        for head in range(heads):
            one = low[:, head * LANES : (head + 1) * LANES].astype(F32)
            grad_one = grad_soft[:, head * LANES : (head + 1) * LANES]
            inner = jnp.sum(grad_one * one, axis=-1, keepdims=True)
            lows.append((one * (grad_one - inner) * (HD**-0.5)).astype(BF16))
        grad_scores = jnp.concatenate(lows, axis=1)
        grad_queries = dot(grad_scores, keys)
        grad_values = gather_heads(dot_columns(low, grad_mixed), lanes, heads)
        grad_keys = gather_heads(dot_columns(grad_scores, queries), lanes, heads)
        bias_sums[0:1, :] += jnp.sum(grad_queries, axis=0, keepdims=True)
        bias_sums[1:2, :] += jnp.sum(grad_values, axis=0, keepdims=True)
        grads[0, at, :] = grad_queries.astype(BF16)
        grads[1, at, :] = grad_keys.astype(BF16)
        grads[2, at, :] = grad_values.astype(BF16)
        return carry

    lax.fori_loop(0, TILE_IMAGES, one_image, 0, unroll=True)
    back = back_in[...] if last else None
    for index in range(3):
        at = slice(index * cols, (index + 1) * cols)
        value = grads[index, :, :]
        term = dot(value, weights[at, :])
        back = term if back is None else back + term
        sums[at, :] += dot_columns(value, normed)
    sums[3 * cols : 4 * cols, :] += dot_columns(saved[3, :, :], grad)
    if last:

        @pl.when(mine)
        def _():
            back_mine[...] = back

        @pl.when(jnp.logical_not(mine))
        def _():
            back_other[...] = back.astype(BF16)

    else:
        back_sum[...] = back

    @pl.when(step == steps - 1)
    def _():
        size = keep.shape[2]
        for flip, ref in enumerate((keep, send_x, send_y, send_xy)):
            quarter = lax.bitwise_xor(place[0], flip)
            for half in range(2):
                at = pl.ds(pl.multiple_of((2 * quarter + half) * size, 16), size)
                ref[half, 0, :, :] = sums[at, :].astype(BF16)


def half_spec(tile, width, tiles, second):
    if second:
        return pl.BlockSpec((tile, width), lambda i: (jnp.maximum(i - tiles, 0), 0))
    return pl.BlockSpec((tile, width), lambda i: (jnp.minimum(i, tiles - 1), 0))


def attention_back(place, slot, own, pieces, normed, grads, saved, soft, before):
    rows, width = grads[0].shape
    cols = saved.shape[2]
    heads = cols // HD
    tile = TILE_IMAGES * SLOTS
    tiles = rows // tile
    far, last = own is not None, before is not None
    mine, other = half_spec(tile, width, tiles, False), half_spec(tile, width, tiles, True)
    both = rows_spec(tile, width)
    grad_shapes, grad_specs = gradient_outputs(1, 4 * cols, width)
    if last:
        more_shapes = (shape((rows, width), F32), shape((rows, width), BF16))
        more_specs = (mine, other)
    else:
        more_shapes = (kept((2 * rows, width), F32),)
        more_specs = (both,)
    weights = (*own, *pieces) if far else pieces
    return pl.pallas_call(
        functools.partial(attention_back_kernel, heads, far, last),
        grid=(2 * tiles,),
        out_shape=(*grad_shapes, shape((8, cols), F32), *more_shapes),
        in_specs=[SMEM]
        + [ANY] * len(weights)
        + [
            mine,
            other,
            mine,
            other,
            pl.BlockSpec((4, tile, cols), lambda i: (slot, i, 0)),
            pl.BlockSpec((tile, heads * LANES), lambda i: (i, slot)),
        ]
        + ([both] if last else []),
        out_specs=(*grad_specs, fixed_spec(8, cols), *more_specs),
        scratch_shapes=[
            pltpu.VMEM((4 * cols + 16, width), BF16),
            pltpu.VMEM((4 * cols, width), F32),
            pltpu.VMEM((4, tile, cols), BF16),
            pltpu.SemaphoreType.DMA((16,)),
        ],
        compiler_params=params(24, 1),
        cost_estimate=cost(rows * width * cols * 30 + rows * 6e5, rows * width * 20 + 4e6),
    )(place, *weights, *normed, *grads, *from_hbm(saved, soft, *(before or ())))


def hidden_kernel(whole, last, place, *rest):
    count = 6
    pieces, rest = rest[:count], rest[count:]
    normed_mine, normed_other, grad_mine, grad_other = rest[:4]
    rest = rest[4:]
    if last:
        out_in, back_in = rest[:2]
        rest = rest[2:]
        whole_grads, bias_sums = rest[:2]
        out_mine, out_other, back_mine, back_other = rest[2:6]
        rest = rest[6:]
    else:
        send_x, send_y, keep_x, keep_y, bias_sums = rest[:5]
        out_sum, back_sum = rest[5:7]
        rest = rest[7:]
    weights, sums_up, sums_down, out_part, back_part, sems = rest
    step = pl.program_id(0)
    steps = pl.num_programs(0)
    width = normed_mine.shape[1]

    @pl.when(step == 0)
    def _():
        if whole:
            load_far(place, pieces[:3], pieces[3:], weights, sems, True)
        else:
            run_copies(hidden_copies(place, pieces[:5], pieces[5], weights, sems))
        sums_up[...] = jnp.zeros_like(sums_up)
        sums_down[...] = jnp.zeros_like(sums_down)
        bias_sums[...] = jnp.zeros_like(bias_sums)

    mine = step < steps // 2
    normed = jnp.where(mine, normed_mine[...], normed_other[...])
    grad = jnp.where(mine, grad_mine[...], grad_other[...])
    bias_rows = weights[2 * width : 2 * width + 16, :].astype(F32)
    chunk = 256
    for first in range(0, width, chunk):
        columns = slice(first, first + chunk)
        up_part = weights[0:width, columns]
        down_part = weights[width + first : width + first + chunk, :]
        hidden = dot(normed, up_part) + bias_rows[2:3, columns]
        phi = 0.5 + 0.5 * lax.erf(hidden * (0.5**0.5))
        slope = phi + hidden * (jnp.exp(-0.5 * hidden * hidden) * ((2.0 * np.pi) ** -0.5))
        active = (hidden * phi).astype(BF16)
        grad_pre = dot_rows(grad, down_part) * slope
        bias_sums[0:1, columns] += jnp.sum(grad_pre, axis=0, keepdims=True)
        grad_low = grad_pre.astype(BF16)
        out_term = dot(active, down_part)
        back_term = dot_rows(grad_low, up_part)
        if first == 0:
            if last:
                out_part[...] = out_in[...] + out_term
                back_part[...] = back_in[...] + back_term
            else:
                out_part[...] = out_term
                back_part[...] = back_term
        else:
            out_part[...] += out_term
            back_part[...] += back_term
        sums_up[:, columns] += dot_columns(normed, grad_low)
        sums_down[columns, :] += dot_columns(active, grad)

    if last:

        @pl.when(mine)
        def _():
            out_mine[...] = out_part[...]
            back_mine[...] = back_part[...]

        @pl.when(jnp.logical_not(mine))
        def _():
            out_other[...] = out_part[...].astype(BF16)
            back_other[...] = back_part[...].astype(BF16)

    else:
        out_sum[...] = out_part[...]
        back_sum[...] = back_part[...]

    @pl.when(step == steps - 1)
    def _():
        if last:
            size = whole_grads.shape[3]
            for flip in range(4):
                quarter = lax.bitwise_xor(place[0], flip)
                for half in range(2):
                    at = pl.ds(pl.multiple_of((2 * quarter + half) * size, 16), size)
                    whole_grads[half, flip, 0, :, :] = sums_up[at, :].astype(BF16)
                    whole_grads[half, flip, 1, :, :] = sums_down[at, :].astype(BF16)
        else:
            split_gradient(
                place,
                lambda m, at: (sums_up if m == 0 else sums_down)[at, :],
                2,
                send_x,
                send_y,
                keep_x,
                keep_y,
            )


def hidden_block(place, pieces, normed, grads, sums_before, whole):
    rows, width = normed[0].shape
    tile = TILE_IMAGES * SLOTS
    tiles = rows // tile
    last = sums_before is not None
    mine, other = half_spec(tile, width, tiles, False), half_spec(tile, width, tiles, True)
    both = rows_spec(tile, width)
    if last:
        dims = (2, 4, 2, width // 8, width)
        grad_shapes, grad_specs = (shape(dims, BF16),), (fixed_spec(*dims),)
    else:
        grad_shapes, grad_specs = gradient_outputs(2, width, width)
    if last:
        more_shapes = (
            kept((rows, width), F32),
            shape((rows, width), BF16),
            shape((rows, width), F32),
            shape((rows, width), BF16),
        )
        more_specs = (mine, other, mine, other)
    else:
        more_shapes = (kept((2 * rows, width), F32),) * 2
        more_specs = (both, both)
    return pl.pallas_call(
        functools.partial(hidden_kernel, whole, last),
        grid=(2 * tiles,),
        out_shape=(*grad_shapes, shape((8, width), F32), *more_shapes),
        in_specs=[SMEM]
        + [ANY] * 6
        + [mine, other, mine, other]
        + ([both, both] if last else []),
        out_specs=(*grad_specs, fixed_spec(8, width), *more_specs),
        scratch_shapes=[
            pltpu.VMEM((2 * width + 16, width), BF16),
            pltpu.VMEM((width, width), F32),
            pltpu.VMEM((width, width), F32),
            pltpu.VMEM((tile, width), F32),
            pltpu.VMEM((tile, width), F32),
            pltpu.SemaphoreType.DMA((16,)),
        ],
        compiler_params=params(40, 1),
        cost_estimate=cost(rows * width * width * 24, rows * width * 24 + 8e6),
    )(place, *pieces, *normed, *grads, *from_hbm(*(sums_before or ())))


def first_sums_kernel(keep_x, keep_y, got_x, got_y, send_y, send_x, base):
    add = lambda u, v: u.astype(F32) + v.astype(F32)
    base[0] = add(keep_x[0], got_x[0])
    base[1] = add(keep_y[0], got_y[0])
    send_y[...] = add(keep_x[1], got_x[1]).astype(BF16)
    send_x[...] = add(keep_y[1], got_y[1]).astype(BF16)


def plane_sums_kernel(base, next_y, next_x, plane):
    plane[0] = (base[0] + next_y[...].astype(F32)).astype(BF16)
    plane[1] = (base[1] + next_x[...].astype(F32)).astype(BF16)


def depth_sums_kernel(core, local_far, far, near, keep, send):
    halves = []
    for half in range(2):
        first = jnp.where(core == 0, local_far[half], far[half])
        halves.append(first.astype(F32) + near[half].astype(F32))
    keep[...] = jnp.where(core == 0, halves[0], halves[1])
    send[...] = jnp.where(core == 0, halves[1], halves[0]).astype(BF16)


def pair_send_kernel(core, own, got, send):
    send[...] = jnp.where(core == 0, own[1], got[0])


def pair_sums_kernel(core, own, got, received, keep, send_x, send_y, send_xy):
    for flip, ref in enumerate((keep, send_x, send_y, send_xy)):
        half = jnp.where(core == 0, own[0, flip], got[1, flip])
        ref[...] = (half.astype(F32) + received[flip].astype(F32)).astype(BF16)


def half_split_kernel(core, both, keep, send):
    keep[...] = jnp.where(core == 0, both[0], both[1])
    send[...] = jnp.where(core == 0, both[1], both[0])


def last_sums_kernel(keep, received, total):
    total[...] = (keep[...] + received[...].astype(F32)).astype(BF16)


def total_kernel(*refs):
    total = refs[0][...].astype(F32)
    for ref in refs[1:-1]:
        total = total + ref[...].astype(F32)
    refs[-1][...] = total.astype(refs[-1].dtype)


def sums_kernel(parts, place, *refs):
    ins = sum(count for _, count, _ in parts)
    in_refs, out_refs = refs[:ins], refs[ins:]
    for body, count, outs in parts:
        mine, in_refs = in_refs[:count], in_refs[count:]
        results, out_refs = out_refs[:outs], out_refs[outs:]
        if body in (depth_sums_kernel, pair_send_kernel, pair_sums_kernel, half_split_kernel):
            body(place[1], *mine, *results)
        else:
            body(*mine, *results)


def sums(place, *work):
    parts, args, out_shapes = [], [], []
    for body, arrays in work:
        like = arrays[0].shape
        if body is first_sums_kernel:
            outs = [shape(like[1:], BF16), shape(like[1:], BF16), shape(like, F32)]
        elif body is plane_sums_kernel:
            outs = [shape(like, BF16)]
        elif body is pair_send_kernel:
            outs = [shape(like[1:], BF16)]
        elif body is pair_sums_kernel:
            outs = [shape(like[2:], BF16)] * 4
        elif body is half_split_kernel:
            outs = [shape(like[1:], BF16)] * 2
        elif body is depth_sums_kernel:
            outs = [shape(like[1:], F32), shape(like[1:], BF16)]
        else:
            outs = [shape(like, arrays[0].dtype if body is total_kernel else BF16)]
        parts.append((body, len(arrays), len(outs)))
        args += arrays
        out_shapes += outs
    moved = sum(4 * np.prod(o.shape) for o in out_shapes)
    results = pl.pallas_call(
        functools.partial(sums_kernel, tuple(parts)),
        out_shape=tuple(out_shapes),
        in_specs=[SMEM] + [VMEM] * len(args),
        out_specs=(VMEM,) * len(out_shapes),
        compiler_params=params(16),
        cost_estimate=cost(0, moved),
    )(place, *args)
    grouped = []
    for _, _, count in parts:
        grouped.append(tuple(results[:count]))
        results = results[count:]
    return grouped


def finish_kernel(place, *refs):
    mine, other, outs = refs[:4], refs[4:8], refs[8:]
    half = mine[0].shape[1]
    for flip in range(4):
        quarter = lax.bitwise_xor(place[0], flip)
        for side, parts in enumerate((mine, other)):
            part = place[1] if side == 0 else 1 - place[1]
            for matrix, out in enumerate(outs):
                at = pl.ds(pl.multiple_of((2 * quarter + part) * half, 8), half)
                out[at, :] = parts[flip][matrix, :, :].astype(F32)


def finish_attention_kernel(place, *refs):
    mine, other, (grad_input, grad_mixer) = refs[:4], refs[4:8], refs[8:]
    half = mine[0].shape[1]
    for flip in range(4):
        quarter = lax.bitwise_xor(place[0], flip)
        for side, parts in enumerate((mine, other)):
            part = place[1] if side == 0 else 1 - place[1]

            @pl.when(quarter < 3)
            def _():
                at = pl.ds(pl.multiple_of((2 * quarter + part) * half, 8), half)
                grad_input[at, :] = parts[flip][0, :, :].astype(F32)

            @pl.when(quarter == 3)
            def _():
                at = pl.ds(pl.multiple_of(part * half, 8), half)
                grad_mixer[at, :] = parts[flip][0, :, :].astype(F32)


def finish(place, mine, other):
    matrices, half, width = mine[0].shape
    if matrices == 1:
        kernel = finish_attention_kernel
        out_shapes = (shape((6 * half, width), F32), shape((2 * half, width), F32))
    else:
        kernel = finish_kernel
        out_shapes = (shape((8 * half, width), F32),) * matrices
    return pl.pallas_call(
        kernel,
        out_shape=out_shapes,
        in_specs=[SMEM] + [VMEM] * 8,
        out_specs=(VMEM,) * len(out_shapes),
        compiler_params=params(16),
        cost_estimate=cost(0, matrices * half * width * 48),
    )(place, *mine, *other)


def local(
    tokens,
    visible_counts,
    norm_one_gain,
    norm_one_shift,
    input_weight,
    input_bias,
    mixer_weight,
    mixer_bias,
    norm_two_gain,
    norm_two_shift,
    up_weight,
    up_bias,
    down_weight,
    down_bias,
    output_grad,
    groups,
    outer,
):
    width = tokens.shape[1]
    rows = tokens.shape[0]
    cols = mixer_weight.shape[0]
    t = lax.axis_index("t")
    core = lax.axis_index("c")
    place = jnp.stack([2 * lax.axis_index("a") + lax.axis_index("b"), core, t]).astype(jnp.int32)
    one_row = lambda v: v.reshape(1, -1)

    swap = [(0, 1), (1, 0)]
    cross = [(0, 3), (1, 2), (2, 1), (3, 0)]
    to_near = [(z, (z + 1) % groups) for z in range(groups)] + [
        (groups + z, groups + (z + 2) % groups) for z in range(groups)
    ]
    to_far = [(groups + z, groups + (z + 3) % groups) for z in range(groups)]
    back_near = [(j, i) for i, j in to_near]
    back_far = [(j, i) for i, j in to_far]

    def spread(piece):
        return (
            piece,
            lax.ppermute(piece, "b", swap),
            lax.ppermute(piece, "a", swap),
            lax.ppermute(piece, ("a", "b"), cross),
        )

    def together(*groups):
        return lax.optimization_barrier(groups)

    def after(value, *others):
        return lax.optimization_barrier((value, *others))[0]

    def first_exchange(send_x, send_y, keep_x, keep_y):
        got_x = lax.ppermute(send_x, "b", swap)
        got_y = lax.ppermute(send_y, "a", swap)
        return keep_x, keep_y, got_x, got_y

    def second_exchange(send_y, send_x, base):
        return base, lax.ppermute(send_y, "a", swap), lax.ppermute(send_x, "b", swap)

    def direct(keep, send_x, send_y, send_xy):
        return (
            keep,
            lax.ppermute(send_x, "b", swap),
            lax.ppermute(send_y, "a", swap),
            lax.ppermute(send_xy, ("a", "b"), cross),
        )

    def over_outer(value):
        return lax.psum(value.astype(F32), "o").astype(BF16) if outer > 1 else value

    projection = input_weight.transpose(1, 2, 0).reshape(3 * cols, width)
    normed_one = norm_one(
        place,
        visible_counts,
        tokens,
        one_row(norm_one_gain),
        one_row(norm_one_shift),
    )
    piece_one, tail_one = pack_attention(
        place, projection, mixer_weight, after(input_bias, normed_one), one_row(up_bias)
    )
    depth_near_one = lax.ppermute(piece_one, ("c", "t"), to_near)
    normed_other = lax.ppermute(normed_one, "c", swap)
    piece_two = pack_hidden(place, up_weight, down_weight)
    depth_near_one, normed_other, piece_two = together(depth_near_one, normed_other, piece_two)
    near_one = spread(depth_near_one)
    far_projection = lax.ppermute(after(projection, depth_near_one), ("c", "t"), to_far)
    far_mixer = lax.ppermute(after(tail_one, depth_near_one), ("c", "t"), to_far)
    near_two = lax.ppermute(after(piece_two, far_mixer, *near_one), ("c", "t"), to_near)

    own_one = (projection, tail_one)
    far_one = (far_projection, far_mixer)
    saved, soft, part = attention(place, own_one, near_one, far_one, normed_other, None, BF16)
    saved, soft, part, near_two = together(saved, soft, part, near_two)
    grad_other = lax.ppermute(after(output_grad, part), "c", swap)
    part_received = lax.ppermute(part, "c", swap)
    near_x = lax.ppermute(near_two, "b", swap)
    near_y = lax.ppermute(near_two, "a", swap)
    far_up = lax.ppermute(after(up_weight, near_two), ("c", "t"), to_far)
    saved, soft, part = attention(
        place, own_one, near_one, far_one, normed_one, (saved, soft), F32
    )
    part, part_received, near_x, near_y, far_up, grad_other = together(
        part, part_received, near_x, near_y, far_up, grad_other
    )
    quarter = near_two.shape[0] // 2
    near_up = lax.ppermute(near_y[:quarter], "b", swap)
    near_down = lax.ppermute(near_x[quarter:], "a", swap)
    first_sum, normed_two = norm_two(
        tokens,
        part,
        part_received,
        one_row(mixer_bias),
        one_row(norm_two_gain),
        one_row(norm_two_shift),
    )
    far_down = lax.ppermute(after(down_weight, far_up), ("c", "t"), to_far)
    normed_two_both = (normed_two, lax.ppermute(normed_two, "c", swap))

    grad_both = (output_grad, grad_other)
    pieces = (near_two, near_x, near_y, near_up, near_down, depth_near_one)
    near_outs = hidden_block(place, pieces, normed_two_both, grad_both, None, False)
    near_outs, far_down = together(near_outs, far_down)
    *grads_near, bias_near, out_sum, back_sum = near_outs
    stage_near = first_exchange(*grads_near)
    shards = (up_weight, down_weight, tail_one, far_up, far_down, far_mixer)
    far_outs = hidden_block(
        place, shards, normed_two_both, grad_both, (out_sum, back_sum), True
    )
    far_outs, stage_near = together(far_outs, stage_near)
    grads_far, bias_far, out_mine, out_send, back_mine, back_send = far_outs

    got_far = lax.ppermute(grads_far, ("c", "t"), back_far)
    back_received = lax.ppermute(back_send, "c", swap)
    (stage_near,) = sums(place, (first_sums_kernel, stage_near))
    back_received = after(back_received, *stage_near)
    stage_near = second_exchange(*stage_near)
    grad_first, grad_first_low, sums_two = norm_two_back(
        back_mine, back_received, first_sum, one_row(norm_two_gain), output_grad
    )
    first_other = lax.ppermute(grad_first_low, "c", swap)
    out_received = lax.ppermute(after(out_send, first_other), "c", swap)

    normed_both = (normed_one, normed_other)
    first_both = (grad_first_low, first_other)
    *grads_one_near, bias_one_near, back_sum = attention_back(
        place, 1, None, near_one, normed_both, first_both, saved, soft, None
    )
    grads_one_near, back_sum, stage_near, got_far, out_received = together(
        grads_one_near, back_sum, stage_near, got_far, out_received
    )
    one_near = direct(*grads_one_near)
    (plane_near,), (send_far,) = sums(
        place, (plane_sums_kernel, stage_near), (pair_send_kernel, (grads_far, got_far))
    )
    depth_near = lax.ppermute(plane_near, ("c", "t"), back_near)
    received_far = lax.ppermute(send_far, "c", swap)
    back_sum = after(back_sum, plane_near)
    *grads_one_far, bias_one_far, back_mine, back_send = attention_back(
        place, 0, own_one, far_one, normed_both, first_both, saved, soft, (back_sum,)
    )
    grads_one_far, back_mine, back_send, one_near, received_far, depth_near = together(
        grads_one_far, back_mine, back_send, one_near, received_far, depth_near
    )

    one_far = direct(*grads_one_far)
    back_received = lax.ppermute(back_send, "c", swap)
    (one_near,), sums_far, (keep_two, send_two) = sums(
        place,
        (total_kernel, one_near),
        (pair_sums_kernel, (grads_far, got_far, received_far)),
        (half_split_kernel, (depth_near,)),
    )
    one_depth_near = lax.ppermute(one_near, ("c", "t"), back_near)
    received_two = lax.ppermute(send_two, "c", swap)
    grad_tokens, vectors = norm_one_back(
        groups,
        place,
        back_mine,
        back_received,
        tokens,
        one_row(norm_one_gain),
        grad_first,
        sums_two,
        bias_near,
        bias_far,
        bias_one_near,
        bias_one_far,
    )
    vectors_core = lax.ppermute(vectors, "c", swap)
    vectors_core, one_far, received_two = together(vectors_core, one_far, received_two)
    (one_far,), (vectors,) = sums(
        place, (total_kernel, one_far), (total_kernel, (vectors, vectors_core))
    )
    one_depth_far = lax.ppermute(one_far, ("c", "t"), back_far)
    sums_far = direct(*sums_far)
    result = (first_sum + (out_mine + out_received.astype(F32)) + down_bias).astype(BF16)
    one_depth_far, one_depth_near, result = together(one_depth_far, one_depth_near, result)
    ((keep_one, send_one),) = sums(
        place, (depth_sums_kernel, (one_far, one_depth_far, one_depth_near))
    )
    received_one = lax.ppermute(send_one, "c", swap)
    vectors_plane = spread(vectors)
    received_one, vectors_plane, sums_far = together(received_one, vectors_plane, sums_far)
    (part_one,), (part_two,), (vectors,) = sums(
        place,
        (last_sums_kernel, (keep_one, received_one)),
        (total_kernel, (*sums_far, keep_two, received_two)),
        (total_kernel, vectors_plane),
    )
    mine_one = spread(over_outer(part_one))
    mine_two = spread(over_outer(part_two))
    turns = [
        lax.ppermute(vectors, "t", [(z, (z + k) % groups) for z in range(groups)])
        for k in range(1, groups)
    ]
    other_two = tuple(lax.ppermute(part, "c", swap) for part in mine_two)
    grad_up, grad_down = finish(place, mine_two, other_two)
    other_one = tuple(lax.ppermute(part, "c", swap) for part in mine_one)
    grad_input, grad_mixer = finish(place, mine_one, other_one)
    grad_input = grad_input.reshape(3, cols, width).transpose(2, 0, 1)
    vectors = sum(turns, vectors)
    if outer > 1:
        vectors = lax.psum(vectors, "o")
    grad_up_bias = lax.dynamic_slice_in_dim(vectors, 6 + t, 1)[0]
    grad_input_bias = lax.dynamic_slice_in_dim(vectors, 6 + groups + t, 1).reshape(-1, 2 * LANES)[
        :2, :cols
    ]
    return (
        result,
        grad_tokens,
        vectors[0],
        vectors[1],
        grad_input,
        grad_input_bias,
        grad_mixer,
        vectors[4],
        vectors[2],
        vectors[3],
        grad_up,
        grad_up_bias,
        grad_down,
        vectors[5],
    )


def solution(mesh):
    dp, groups = mesh.shape["dp"], mesh.shape["tensor"]
    outer = dp // 8
    split = jax.sharding.Mesh(
        mesh.devices.reshape(outer, 2, 2, 2, groups), ("o", "a", "b", "c", "t")
    )
    dp_axes = ("o", "a", "b", "c")
    all_axes = dp_axes + ("t",)
    in_specs = (
        P(all_axes, None),
        P(dp_axes),
        P(),
        P(),
        P(None, None, "t"),
        P(None, "t"),
        P("t", None),
        P(),
        P(),
        P(),
        P(None, "t"),
        P("t"),
        P("t", None),
        P(),
        P(all_axes, None),
    )
    out_specs = (
        P(all_axes, None),
        P(all_axes, None),
        P(),
        P(),
        P(None, None, "t"),
        P(None, "t"),
        P("t", None),
        P(),
        P(),
        P(),
        P(None, "t"),
        P("t"),
        P("t", None),
        P(),
    )
    return jax.shard_map(
        functools.partial(local, groups=groups, outer=outer),
        mesh=split,
        in_specs=in_specs,
        out_specs=out_specs,
        check_vma=False,
    )
```

```python
import functools

import jax
import jax.numpy as jnp
import numpy as np
from jax import lax
from jax.experimental import pallas as pl
from jax.experimental.pallas import tpu as pltpu
from jax.sharding import PartitionSpec as P

HD = 64
SLOTS = 80
LANES = 128
TILE_IMAGES = 4
MASKED = -1000000000.0
EPS = 1e-06
F32 = jnp.float32
BF16 = jnp.bfloat16

ANY = pl.BlockSpec(memory_space=pl.ANY)
SMEM = pl.BlockSpec(memory_space=pltpu.SMEM)
VMEM = pl.BlockSpec(memory_space=pltpu.VMEM)


def shape(dims, kind):
    return jax.ShapeDtypeStruct(tuple(dims), kind)


def kept(dims, kind):
    return pltpu.HBM(tuple(dims), kind)


def from_hbm(*arrays):
    return tuple(pltpu.with_memory_space_constraint(a, pltpu.HBM) for a in arrays)


def params(megabytes, grid_dims=0):
    semantics = ("arbitrary",) * grid_dims if grid_dims else None
    return pltpu.CompilerParams(
        vmem_limit_bytes=megabytes * 1024 * 1024, dimension_semantics=semantics
    )


def cost(flops, moved):
    return pl.CostEstimate(flops=int(flops), bytes_accessed=int(moved), transcendentals=0)


def dot(left, right):
    return lax.dot_general(left, right, (((1,), (0,)), ((), ())), preferred_element_type=F32)


def dot_rows(left, right):
    return lax.dot_general(left, right, (((1,), (1,)), ((), ())), preferred_element_type=F32)


def dot_columns(left, right):
    return lax.dot_general(left, right, (((0,), (0,)), ((), ())), preferred_element_type=F32)


def centred(rows):
    center = rows - jnp.mean(rows, axis=-1, keepdims=True)
    spread = jnp.mean(center * center, axis=-1, keepdims=True)
    return center, lax.rsqrt(spread + EPS)


def norm_back(rows, gain, grad):
    center, rstd = centred(rows)
    xhat = center * rstd
    e = grad * gain
    back = rstd * (
        e - jnp.mean(e, axis=-1, keepdims=True) - xhat * jnp.mean(e * xhat, axis=-1, keepdims=True)
    )
    return (
        back,
        jnp.sum(grad * xhat, axis=0, keepdims=True),
        jnp.sum(grad, axis=0, keepdims=True),
    )


def norm_one_kernel(images, chunk, place, counts, tokens, gain, shift, out):
    rows = tokens.shape[0]

    @pl.loop(0, rows // chunk)
    def _(step):
        at = pl.ds(pl.multiple_of(step * chunk, chunk), chunk)
        center, rstd = centred(tokens[at, :].astype(F32))
        out[at, :] = (center * rstd * gain[...] + shift[...]).astype(BF16)

    extra = out.shape[0] - rows
    row = lax.broadcasted_iota(jnp.int32, (extra, out.shape[1]), 0)
    table = jnp.zeros((extra, out.shape[1]), F32)
    first = place[2] * images
    for image in range(images):
        table = jnp.where(row == image, counts[first + image].astype(F32), table)
    out[rows:, :] = table.astype(BF16)


def norm_one(place, counts, tokens, gain, shift):
    rows, width = tokens.shape
    images = rows // SLOTS
    return pl.pallas_call(
        functools.partial(norm_one_kernel, images, SLOTS),
        out_shape=shape((rows + 16, width), BF16),
        in_specs=[SMEM, SMEM, VMEM, VMEM, VMEM],
        out_specs=VMEM,
        compiler_params=params(16),
        cost_estimate=cost(rows * width * 10, rows * width * 4),
    )(place, counts, tokens, gain, shift)


def norm_two_kernel(tokens, mine, received, bias, gain, shift, first_sum, normed):
    total = tokens[...].astype(F32) + (mine[...] + received[...].astype(F32)) + bias[...]
    first_sum[...] = total
    center, rstd = centred(total)
    normed[...] = (center * rstd * gain[...] + shift[...]).astype(BF16)


def rows_spec(tile, width):
    return pl.BlockSpec((tile, width), lambda i: (i, 0))


def fixed_spec(*dims):
    return pl.BlockSpec(dims, lambda i: (0,) * len(dims))


def norm_two(tokens, mine, received, bias, gain, shift):
    rows, width = tokens.shape
    tile = 2 * SLOTS
    row = rows_spec(tile, width)
    vector = fixed_spec(1, width)
    return pl.pallas_call(
        norm_two_kernel,
        grid=(rows // tile,),
        out_shape=(kept((rows, width), F32), shape((rows, width), BF16)),
        in_specs=[row, row, row, vector, vector, vector],
        out_specs=(row, row),
        compiler_params=params(16, 1),
        cost_estimate=cost(rows * width * 12, rows * width * 14),
    )(*from_hbm(tokens), mine, received, bias, gain, shift)


def added(*refs):
    total = refs[0][...].astype(F32)
    for ref in refs[1:]:
        total = total + ref[...].astype(F32)
    return total


def norm_two_back_kernel(
    part0, part1, part2, part3, first_sum, gain, output_grad, low, sums
):
    grad = added(part0, part1, part2, part3)
    back, grad_gain, grad_shift = norm_back(first_sum[...], gain[...], grad)
    out_grad = output_grad[...].astype(F32)
    total = out_grad + back
    low[...] = total.astype(BF16)

    @pl.when(pl.program_id(0) == 0)
    def _():
        sums[...] = jnp.zeros_like(sums)

    sums[0:1, :] += grad_gain
    sums[1:2, :] += grad_shift
    sums[2:3, :] += jnp.sum(total, axis=0, keepdims=True)
    sums[3:4, :] += jnp.sum(out_grad, axis=0, keepdims=True)


def norm_two_back(parts, first_sum, gain, output_grad):
    rows, width = parts[0].shape
    tile = 2 * SLOTS
    row = rows_spec(tile, width)
    return pl.pallas_call(
        norm_two_back_kernel,
        grid=(rows // tile,),
        out_shape=(shape((rows, width), BF16), shape((8, width), F32)),
        in_specs=[row] * 5 + [fixed_spec(1, width), row],
        out_specs=(row, fixed_spec(8, width)),
        compiler_params=params(16, 1),
        cost_estimate=cost(rows * width * 25, rows * width * 18),
    )(*parts, *from_hbm(first_sum), gain, *from_hbm(output_grad))


def norm_one_back_kernel(
    groups,
    place,
    part0,
    part1,
    part2,
    part3,
    tokens,
    gain,
    grad_first,
    sums_two,
    bias_near,
    bias_far,
    input_near,
    input_far,
    grad_tokens,
    vectors,
):
    grad = added(part0, part1, part2, part3)
    back, grad_gain, grad_shift = norm_back(tokens[...].astype(F32), gain[...], grad)
    grad_tokens[...] = grad_first[...].astype(F32) + back

    @pl.when(pl.program_id(0) == 0)
    def _():
        near = lax.rem(place[2] - 1 - place[1] + groups, groups)
        far = lax.rem(place[2] - 3 * place[1] + groups, groups)
        row = lax.broadcasted_iota(jnp.int32, vectors.shape, 0)
        table = jnp.zeros(vectors.shape, F32)
        for index in range(4):
            table = jnp.where(row == 2 + index, sums_two[index : index + 1, :], table)
        table = jnp.where(row == 6 + near, bias_near[0:1, :], table)
        vectors[...] = jnp.where(row == 6 + far, bias_far[0:1, :], table)
        columns = input_near.shape[1]
        few = lax.broadcasted_iota(jnp.int32, (vectors.shape[0], columns), 0)
        for index in range(2):
            table = jnp.where(
                few == 6 + groups + near, input_near[index : index + 1, :], 0.0
            ) + jnp.where(few == 6 + groups + far, input_far[index : index + 1, :], 0.0)
            vectors[:, index * columns : (index + 1) * columns] += table

    vectors[0:1, :] += grad_gain
    vectors[1:2, :] += grad_shift


def norm_one_back(groups, place, parts, tokens, gain, grad_first, *small):
    rows, width = parts[0].shape
    tile = 2 * SLOTS
    row = rows_spec(tile, width)
    return pl.pallas_call(
        functools.partial(norm_one_back_kernel, groups),
        grid=(rows // tile,),
        out_shape=(kept((rows, width), F32), shape((16, width), F32)),
        in_specs=[SMEM] + [row] * 5 + [fixed_spec(1, width), row]
        + [fixed_spec(*array.shape) for array in small],
        out_specs=(row, fixed_spec(16, width)),
        compiler_params=params(16, 1),
        cost_estimate=cost(rows * width * 25, rows * width * 16),
    )(place, *parts, *from_hbm(tokens), gain, *from_hbm(grad_first), *small)


def pack_attention_kernel(place, projection, mixer, bias, up_bias, out, tail, sem, tail_sem):
    quarter = place[0]
    tail_copy = pltpu.make_async_copy(mixer, tail.at[pl.ds(0, mixer.shape[0])], tail_sem)
    tail_copy.start()
    size = out.shape[0] - 16
    feature_rows = projection.shape[0]
    first = pl.multiple_of(quarter * size, 16)
    from_projection = quarter * size < feature_rows

    @pl.when(from_projection)
    def _():
        copy = pltpu.make_async_copy(
            projection.at[pl.ds(first, size)], out.at[pl.ds(0, size)], sem
        )
        copy.start()
        copy.wait()

    @pl.when(jnp.logical_not(from_projection))
    def _():
        copy = pltpu.make_async_copy(mixer, out.at[pl.ds(0, size)], sem)
        copy.start()
        copy.wait()

    columns = bias.shape[1]
    row = lax.broadcasted_iota(jnp.int32, (16, columns), 0)
    both = bias[...].astype(F32)
    rows = jnp.where(row == 0, both[0:1, :], jnp.where(row == 1, both[1:2, :], 0.0))
    row_all = lax.broadcasted_iota(jnp.int32, (16, out.shape[1]), 0)
    out[size:, :] = jnp.where(row_all == 2, up_bias[...].astype(F32), 0.0).astype(BF16)
    row_two = jnp.where(row == 2, up_bias[:, 0:columns].astype(F32), rows)
    out[size:, 0:columns] = row_two.astype(BF16)
    tail[size:, :] = out[size:, :]
    tail_copy.wait()


def pack_attention(place, projection, mixer, bias, up_bias):
    size, width = mixer.shape
    return pl.pallas_call(
        pack_attention_kernel,
        out_shape=(shape((size + 16, width), BF16),) * 2,
        in_specs=[SMEM, ANY, ANY, VMEM, VMEM],
        out_specs=(VMEM, VMEM),
        scratch_shapes=[pltpu.SemaphoreType.DMA(()), pltpu.SemaphoreType.DMA(())],
        compiler_params=params(16),
        cost_estimate=cost(0, 2 * size * width),
    )(place, *from_hbm(projection, mixer), bias, up_bias)


def pack_hidden_kernel(place, up, down, out, sems):
    size = out.shape[0] // 2
    first = pl.multiple_of(place[0] * size, 16)
    copies = [
        pltpu.make_async_copy(
            source.at[pl.ds(first, size)], out.at[pl.ds(index * size, size)], sems.at[index]
        )
        for index, source in enumerate((up, down))
    ]
    run_copies(copies)


def pack_hidden(place, up, down):
    size, width = up.shape[0] // 4, up.shape[1]
    return pl.pallas_call(
        pack_hidden_kernel,
        out_shape=shape((2 * size, width), BF16),
        in_specs=[SMEM, ANY, ANY],
        out_specs=VMEM,
        scratch_shapes=[pltpu.SemaphoreType.DMA((2,))],
        compiler_params=params(16),
        cost_estimate=cost(0, 4 * size * width),
    )(place, *from_hbm(up, down))


def run_copies(copies):
    for copy in copies:
        copy.start()
    for copy in copies:
        copy.wait()


def make_copies(copies, sems):
    return [
        pltpu.make_async_copy(source, to, sems.at[index])
        for index, (source, to) in enumerate(copies)
    ]


def piece_copies(place, pieces, target, sems):
    size = pieces[0].shape[0] - 16
    copies = []
    for flip, piece in enumerate(pieces):
        to = pl.multiple_of(lax.bitwise_xor(place[0], flip) * size, 16)
        copies.append((piece.at[pl.ds(0, size)], target.at[pl.ds(to, size)]))
    copies.append((pieces[0].at[pl.ds(size, 16)], target.at[pl.ds(4 * size, 16)]))
    return make_copies(copies, sems)


def hidden_copies(place, pieces, bias_piece, target, sems):
    size = pieces[0].shape[0] // 2
    copies = []
    for flip in range(4):
        quarter = lax.bitwise_xor(place[0], flip)
        for matrix in range(2):
            to = pl.multiple_of((4 * matrix + quarter) * size, 16)
            source = pieces[3 + matrix] if flip == 3 else pieces[flip].at[pl.ds(matrix * size, size)]
            copies.append((source, target.at[pl.ds(to, size)]))
    first = bias_piece.shape[0] - 16
    copies.append((bias_piece.at[pl.ds(first, 16)], target.at[pl.ds(8 * size, 16)]))
    return make_copies(copies, sems)


def head_lanes(rows, width):
    return lax.broadcasted_iota(jnp.int32, (rows, width), 1) // HD


def spread_heads(block, lanes, heads):
    gap = jnp.zeros((LANES - SLOTS, block.shape[1]), block.dtype)
    parts = []
    for head in range(heads):
        parts.append(jnp.where(lanes == head, block, jnp.zeros_like(block)))
        parts.append(gap)
    return jnp.concatenate(parts, axis=0)


def gather_heads(product, lanes, heads):
    total = product[0:SLOTS]
    for head in range(1, heads):
        total = jnp.where(lanes == head, product[head * LANES : head * LANES + SLOTS], total)
    return total


def start_on_core(place, own, far, cut, sems):
    copies = [make_copies(cut(parts), sems) for parts in (own, far)]
    for core, some in enumerate(copies):

        @pl.when(place[1] == core)
        def _():
            for copy in some:
                copy.start()

    return copies[0]


def start_far(place, own, far, target, sems):
    def cut(parts):
        size = parts[0].shape[0]
        return [
            (parts[0], target.at[pl.ds(0, size)]),
            (parts[1], target.at[pl.ds(size, parts[1].shape[0])]),
        ]

    return start_on_core(place, own, far, cut, sems)


def start_matrices(place, own, far, target, sems):
    def cut(parts):
        size = parts[0].shape[0]
        bias = parts[2].at[pl.ds(parts[2].shape[0] - 16, 16)]
        return [
            (parts[0], target.at[pl.ds(0, size)]),
            (parts[1], target.at[pl.ds(size, size)]),
            (bias, target.at[pl.ds(2 * size, 16)]),
        ]

    return start_on_core(place, own, far, cut, sems)


def attention_kernel(
    heads,
    place,
    projection,
    tail,
    near0,
    near1,
    near2,
    near3,
    far0,
    far1,
    normed,
    counts,
    *rest,
):
    saved, soft, part, weights, table, sems = rest[-6:]

    @pl.when(pl.program_id(0) == 0)
    def _():
        copies = piece_copies(place, (near0, near1, near2, near3), weights.at[1], sems)
        for copy in copies:
            copy.start()
        far_sems = sems.at[pl.ds(8, 8)]
        copies += start_far(place, (projection, tail), (far0, far1), weights.at[0], far_sems)
        for copy in copies:
            copy.wait()

    cols = heads * HD
    visible_rows = counts[:, 0:LANES].astype(F32)
    for image in range(visible_rows.shape[0]):
        table[image, :, :] = visible_rows[image : image + 1, :]
    rows = normed[...]
    for slot in range(2):
        for index in range(3):
            value = dot_rows(rows, weights[slot, index * cols : (index + 1) * cols, :])
            if index != 1:
                bias_row = 0 if index == 0 else 1
                bias = weights[slot, 4 * cols : 4 * cols + 16, 0:cols].astype(F32)
                value = value + bias[bias_row : bias_row + 1, :]
            saved[4 * slot + index, :, :] = value.astype(BF16)

    lanes = head_lanes(SLOTS, cols)
    key_index = lax.broadcasted_iota(jnp.int32, (SLOTS, LANES), 1).astype(F32)
    first = pl.program_id(0) * TILE_IMAGES

    def one_image(image, carry):
        at = pl.ds(pl.multiple_of(image * SLOTS, 16), SLOTS)
        visible = key_index < table[first + image]
        for slot in range(2):
            queries = saved[4 * slot, at, :]
            keys = spread_heads(saved[4 * slot + 1, at, :], lanes, heads)
            values = spread_heads(saved[4 * slot + 2, at, :], lanes, heads)
            scores = dot_rows(queries, keys) * (HD**-0.5)
            lows = []
            for head in range(heads):
                one = jnp.where(visible, scores[:, head * LANES : (head + 1) * LANES], MASKED)
                exponent = jnp.exp(one - jnp.max(one, axis=-1, keepdims=True))
                total = jnp.sum(exponent, axis=-1, keepdims=True)
                lows.append((exponent / total).astype(BF16))
            low = jnp.concatenate(lows, axis=1)
            soft[at, slot * heads * LANES : (slot + 1) * heads * LANES] = low
            saved[4 * slot + 3, at, :] = dot(low, values).astype(BF16)
        return carry

    lax.fori_loop(0, TILE_IMAGES, one_image, 0, unroll=True)
    total = dot(saved[3, :, :], weights[0, 3 * cols : 4 * cols, :])
    total = total + dot(saved[7, :, :], weights[1, 3 * cols : 4 * cols, :])
    part[...] = total.astype(part.dtype)


def attention(place, own, near, far, normed, before, kind):
    projection, tail = own
    cols, width = projection.shape[0] // 3, projection.shape[1]
    heads = cols // HD
    rows = normed.shape[0] - 16
    tile = TILE_IMAGES * SLOTS
    tiles = rows // tile
    base = tiles if before is None else 0
    extra = () if before is None else from_hbm(*before)
    args = (place, projection, tail, *near, *far, normed, normed, *extra)
    return pl.pallas_call(
        functools.partial(attention_kernel, heads),
        grid=(tiles,),
        out_shape=(
            kept((8, 2 * rows, cols), BF16),
            kept((2 * rows, 2 * heads * LANES), BF16),
            shape((rows, width), kind),
        ),
        in_specs=[SMEM]
        + [ANY] * 8
        + [
            pl.BlockSpec((tile, width), lambda i: (i, 0)),
            pl.BlockSpec((16, width), lambda i: (rows // 16, 0)),
        ]
        + [ANY] * len(extra),
        out_specs=(
            pl.BlockSpec((8, tile, cols), lambda i: (0, base + i, 0)),
            pl.BlockSpec((tile, 2 * heads * LANES), lambda i: (base + i, 0)),
            pl.BlockSpec((tile, width), lambda i: (i, 0)),
        ),
        scratch_shapes=[
            pltpu.VMEM((2, 4 * cols + 16, width), BF16),
            pltpu.VMEM((16, 1, LANES), F32),
            pltpu.SemaphoreType.DMA((16,)),
        ],
        input_output_aliases={11: 0, 12: 1} if extra else {},
        compiler_params=params(20, 1),
        cost_estimate=cost(rows * width * cols * 16 + rows * 400000, rows * width * 10 + 5e6),
    )(*args)


def attention_back_kernel(heads, far, place, *rest):
    count = 4
    pieces, rest = rest[:count], rest[count:]
    normed_mine, normed_other, grad_mine, grad_other, saved, soft = rest[:6]
    rest = rest[6:]
    keep, send_x, send_y, send_xy, bias_sums = rest[:5]
    rest = rest[5:]
    back_mine, back_other, weights, sums, grads, sems = rest
    step = pl.program_id(0)
    steps = pl.num_programs(0)
    cols = heads * HD
    mine = step < steps // 2

    @pl.when(step == 0)
    def _():
        if far:
            copies = start_far(place, pieces[:2], pieces[2:], weights, sems)
        else:
            copies = piece_copies(place, pieces, weights, sems)
            for copy in copies:
                copy.start()
        for copy in copies:
            copy.wait()
        sums[...] = jnp.zeros_like(sums)
        bias_sums[...] = jnp.zeros_like(bias_sums)

    normed = jnp.where(mine, normed_mine[...], normed_other[...])
    grad = jnp.where(mine, grad_mine[...], grad_other[...])
    grads[3, :, :] = dot_rows(grad, weights[3 * cols : 4 * cols, :]).astype(BF16)
    lanes = head_lanes(SLOTS, cols)

    def one_image(image, carry):
        at = pl.ds(pl.multiple_of(image * SLOTS, 16), SLOTS)
        queries = saved[0, at, :]
        keys = spread_heads(saved[1, at, :], lanes, heads)
        values = spread_heads(saved[2, at, :], lanes, heads)
        grad_mixed = grads[3, at, :]
        low = soft[at, :]
        grad_soft = dot_rows(grad_mixed, values)
        lows = []
        for head in range(heads):
            one = low[:, head * LANES : (head + 1) * LANES].astype(F32)
            grad_one = grad_soft[:, head * LANES : (head + 1) * LANES]
            inner = jnp.sum(grad_one * one, axis=-1, keepdims=True)
            lows.append((one * (grad_one - inner) * (HD**-0.5)).astype(BF16))
        grad_scores = jnp.concatenate(lows, axis=1)
        grad_queries = dot(grad_scores, keys)
        grad_values = gather_heads(dot_columns(low, grad_mixed), lanes, heads)
        grad_keys = gather_heads(dot_columns(grad_scores, queries), lanes, heads)
        bias_sums[0:1, :] += jnp.sum(grad_queries, axis=0, keepdims=True)
        bias_sums[1:2, :] += jnp.sum(grad_values, axis=0, keepdims=True)
        grads[0, at, :] = grad_queries.astype(BF16)
        grads[1, at, :] = grad_keys.astype(BF16)
        grads[2, at, :] = grad_values.astype(BF16)
        return carry

    lax.fori_loop(0, TILE_IMAGES, one_image, 0, unroll=True)
    back = None
    for index in range(3):
        at = slice(index * cols, (index + 1) * cols)
        value = grads[index, :, :]
        term = dot(value, weights[at, :])
        back = term if back is None else back + term
        sums[at, :] += dot_columns(value, normed)
    sums[3 * cols : 4 * cols, :] += dot_columns(saved[3, :, :], grad)

    @pl.when(mine)
    def _():
        back_mine[...] = back.astype(BF16)

    @pl.when(jnp.logical_not(mine))
    def _():
        back_other[...] = back.astype(BF16)

    @pl.when(step == steps - 1)
    def _():
        size = keep.shape[2]
        for flip, ref in enumerate((keep, send_x, send_y, send_xy)):
            quarter = lax.bitwise_xor(place[0], flip)
            for half in range(2):
                at = pl.ds(pl.multiple_of((2 * quarter + half) * size, 16), size)
                ref[half, 0, :, :] = sums[at, :].astype(BF16)


def half_spec(tile, width, tiles, second):
    if second:
        return pl.BlockSpec((tile, width), lambda i: (jnp.maximum(i - tiles, 0), 0))
    return pl.BlockSpec((tile, width), lambda i: (jnp.minimum(i, tiles - 1), 0))


def attention_back(place, slot, own, pieces, normed, grads, saved, soft):
    rows, width = grads[0].shape
    cols = saved.shape[2]
    heads = cols // HD
    tile = TILE_IMAGES * SLOTS
    tiles = rows // tile
    far = own is not None
    mine, other = half_spec(tile, width, tiles, False), half_spec(tile, width, tiles, True)
    dims = (2, 1, cols // 2, width)
    weights = (*own, *pieces) if far else pieces
    return pl.pallas_call(
        functools.partial(attention_back_kernel, heads, far),
        grid=(2 * tiles,),
        out_shape=(
            *(shape(dims, BF16),) * 4,
            shape((8, cols), F32),
            shape((rows, width), BF16),
            shape((rows, width), BF16),
        ),
        in_specs=[SMEM]
        + [ANY] * 4
        + [
            mine,
            other,
            mine,
            other,
            pl.BlockSpec((4, tile, cols), lambda i: (slot, i, 0)),
            pl.BlockSpec((tile, heads * LANES), lambda i: (i, slot)),
        ],
        out_specs=(*(fixed_spec(*dims),) * 4, fixed_spec(8, cols), mine, other),
        scratch_shapes=[
            pltpu.VMEM((4 * cols + 16, width), BF16),
            pltpu.VMEM((4 * cols, width), F32),
            pltpu.VMEM((4, tile, cols), BF16),
            pltpu.SemaphoreType.DMA((16,)),
        ],
        compiler_params=params(24, 1),
        cost_estimate=cost(rows * width * cols * 30 + rows * 6e5, rows * width * 20 + 4e6),
    )(place, *weights, *normed, *grads, *from_hbm(saved, soft))


def hidden_kernel(last, place, *rest):
    pieces, rest = rest[:6], rest[6:]
    normed_parts, grad_parts, rest = rest[:2], rest[2:4], rest[4:]
    if last:
        whole_grads, rest = rest[0], rest[1:]
    else:
        (send_x, send_y, keep_x, keep_y), rest = rest[:4], rest[4:]
    bias_sums, out_mine, out_other, back_mine, back_other = rest[:5]
    rest = rest[5:]
    weights, normed, grad, active, grad_low, sums_up, sums_down, summed = rest[:8]
    piece_sems, sems, out_sems = rest[8:]
    rows, width = normed.shape
    half = rows // 2

    def load(first, parts, target):
        return [
            pltpu.make_async_copy(part, target.at[pl.ds(index * half, half)], sems.at[first + index])
            for index, part in enumerate(parts)
        ]

    normed_copies, grad_copies = load(0, normed_parts, normed), load(2, grad_parts, grad)
    for copy in normed_copies:
        copy.start()
    if last:
        starts = start_matrices(place, pieces[:3], pieces[3:], weights, piece_sems)
        first_needed, then_needed = [starts[0], starts[2]], [starts[1]]
    else:
        starts = hidden_copies(place, pieces[:5], pieces[5], weights, piece_sems)
        first_needed, then_needed = starts[0:8:2] + [starts[8]], starts[1:8:2]
        for copy in first_needed + then_needed:
            copy.start()
    for copy in grad_copies:
        copy.start()
    for copy in normed_copies + first_needed:
        copy.wait()

    bias = weights[2 * width : 2 * width + 16, :].astype(F32)[2:3, :]
    chunk = 256
    chunks = [slice(first, first + chunk) for first in range(0, width, chunk)]

    def weight_sums(at):
        sums_up[:, at] = dot_columns(normed[...], grad_low[:, at]).astype(BF16)
        sums_down[at, :] = dot_columns(active[:, at], grad[...]).astype(BF16)

    for index, at in enumerate(chunks):
        hidden = dot(normed[...], weights[0:width, at]) + bias[:, at]
        if index == 0:
            for copy in grad_copies + then_needed:
                copy.wait()
        phi = 0.5 + 0.5 * lax.erf(hidden * (0.5**0.5))
        slope = phi + hidden * (jnp.exp(-0.5 * hidden * hidden) * ((2.0 * np.pi) ** -0.5))
        active[:, at] = (hidden * phi).astype(BF16)
        down_rows = weights[width + at.start : width + at.stop, :]
        grad_pre = dot_rows(grad[...], down_rows) * slope
        bias_sums[0:1, at] = jnp.sum(grad_pre, axis=0, keepdims=True)
        grad_low[:, at] = grad_pre.astype(BF16)
        if index:
            weight_sums(chunks[index - 1])
    weight_sums(chunks[-1])

    size = sums_up.shape[0] // 8
    copies = []
    for flip in range(4):
        quarter = lax.bitwise_xor(place[0], flip)
        for part in range(2):
            at = pl.ds(pl.multiple_of((2 * quarter + part) * size, 16), size)
            for matrix, source in enumerate((sums_up, sums_down)):
                if last:
                    target = whole_grads.at[part, flip, matrix]
                elif part == 0:
                    target = (keep_x if flip % 2 == 0 else send_x).at[flip // 2, matrix]
                else:
                    target = (keep_y if flip < 2 else send_y).at[flip % 2, matrix]
                sem = piece_sems.at[len(copies)]
                copies.append(pltpu.make_async_copy(source.at[at], target, sem))
    for copy in copies:
        copy.start()
    targets = ((out_mine, out_other), (back_mine, back_other))

    def out_copy(index, part, first, sem):
        target = targets[index][part]
        source = summed.at[index, pl.ds(part * half, target.shape[0]), pl.ds(first, chunk)]
        return pltpu.make_async_copy(source, target.at[:, pl.ds(first, chunk)], sem)

    def finish_chunk(step, carry):
        first = pl.multiple_of(step * chunk, chunk)
        at = pl.ds(first, chunk)
        back = dot_rows(grad_low[...], weights[at, :])
        out = dot(active[...], weights[width : 2 * width, at])
        for index, value in enumerate((out, back)):
            summed[index, :, at] = value.astype(BF16)
            for part in range(2):
                out_copy(index, part, first, out_sems.at[step, index, part]).start()
        return carry

    lax.fori_loop(0, len(chunks), finish_chunk, 0)
    for step in range(len(chunks)):
        for index in range(2):
            for part in range(2):
                out_copy(index, part, step * chunk, out_sems.at[step, index, part]).wait()
    for copy in copies:
        copy.wait()


def hidden_block(place, pieces, normed, grads, last):
    rows, width = normed[0].shape
    size = width // 8
    if last:
        grad_shapes = (kept((2, 4, 2, size, width), BF16),)
    else:
        grad_shapes = (kept((2, 2, size, width), BF16),) * 4
    return pl.pallas_call(
        functools.partial(hidden_kernel, last),
        out_shape=(
            *grad_shapes,
            shape((8, width), F32),
            kept((rows, width), BF16),
            kept((rows, width), BF16),
            kept((rows, width), BF16),
            kept((rows, width), BF16),
        ),
        in_specs=[SMEM] + [ANY] * 10,
        out_specs=(ANY,) * len(grad_shapes) + (VMEM,) + (ANY,) * 4,
        scratch_shapes=[
            pltpu.VMEM((2 * width + 16, width), BF16),
            pltpu.VMEM((2 * rows, width), BF16),
            pltpu.VMEM((2 * rows, width), BF16),
            pltpu.VMEM((2 * rows, width), BF16),
            pltpu.VMEM((2 * rows, width), BF16),
            pltpu.VMEM((width, width), BF16),
            pltpu.VMEM((width, width), BF16),
            pltpu.VMEM((2, 2 * rows, width), BF16),
            pltpu.SemaphoreType.DMA((16,)),
            pltpu.SemaphoreType.DMA((4,)),
            pltpu.SemaphoreType.DMA((width // 256, 2, 2)),
        ],
        compiler_params=params(44),
        cost_estimate=cost(rows * width * width * 24, rows * width * 24 + 8e6),
    )(place, *pieces, *from_hbm(*normed, *grads))


def first_sums_kernel(keep_x, keep_y, got_x, got_y, send_y, send_x, base):
    add = lambda u, v: u.astype(F32) + v.astype(F32)
    base[0] = add(keep_x[0], got_x[0])
    base[1] = add(keep_y[0], got_y[0])
    send_y[...] = add(keep_x[1], got_x[1]).astype(BF16)
    send_x[...] = add(keep_y[1], got_y[1]).astype(BF16)


def plane_sums_kernel(base, next_y, next_x, plane):
    plane[0] = (base[0] + next_y[...].astype(F32)).astype(BF16)
    plane[1] = (base[1] + next_x[...].astype(F32)).astype(BF16)


def depth_sums_kernel(core, local_far, far, near, keep, send):
    halves = []
    for half in range(2):
        first = jnp.where(core == 0, local_far[half], far[half])
        halves.append(first.astype(F32) + near[half].astype(F32))
    keep[...] = jnp.where(core == 0, halves[0], halves[1])
    send[...] = jnp.where(core == 0, halves[1], halves[0]).astype(BF16)


def pair_send_kernel(core, own, got, send):
    send[...] = jnp.where(core == 0, own[1], got[0])


def pair_sums_kernel(core, own, got, received, keep, send_x, send_y, send_xy):
    for flip, ref in enumerate((keep, send_x, send_y, send_xy)):
        half = jnp.where(core == 0, own[0, flip], got[1, flip])
        ref[...] = (half.astype(F32) + received[flip].astype(F32)).astype(BF16)


def half_split_kernel(core, both, keep, send):
    keep[...] = jnp.where(core == 0, both[0], both[1])
    send[...] = jnp.where(core == 0, both[1], both[0])


def last_sums_kernel(keep, received, *rest):
    total = rest[-1]
    total[0:1] = (keep[...] + received[...].astype(F32)).astype(BF16)
    both = rest[0][...].astype(F32)
    for ref in rest[1:-1]:
        both = both + ref[...].astype(F32)
    total[1:3] = both.astype(BF16)


def total_kernel(*refs):
    total = refs[0][...].astype(F32)
    for ref in refs[1:-1]:
        total = total + ref[...].astype(F32)
    refs[-1][...] = total.astype(refs[-1].dtype)


def sums_kernel(parts, place, *refs):
    ins = sum(count for _, count, _ in parts)
    in_refs, out_refs = refs[:ins], refs[ins:]
    for body, count, outs in parts:
        mine, in_refs = in_refs[:count], in_refs[count:]
        results, out_refs = out_refs[:outs], out_refs[outs:]
        if body in (depth_sums_kernel, pair_send_kernel, pair_sums_kernel, half_split_kernel):
            body(place[1], *mine, *results)
        else:
            body(*mine, *results)


def sums(place, *work):
    parts, args, out_shapes = [], [], []
    for body, arrays in work:
        like = arrays[0].shape
        if body is first_sums_kernel:
            outs = [shape(like[1:], BF16), shape(like[1:], BF16), shape(like, F32)]
        elif body is plane_sums_kernel:
            outs = [shape(like, BF16)]
        elif body is pair_send_kernel:
            outs = [shape(like[1:], BF16)]
        elif body is pair_sums_kernel:
            outs = [shape(like[2:], BF16)] * 4
        elif body is half_split_kernel:
            outs = [shape(like[1:], BF16)] * 2
        elif body is depth_sums_kernel:
            outs = [shape(like[1:], F32), shape(like[1:], BF16)]
        else:
            dims = (3, *like[1:]) if body is last_sums_kernel else like
            outs = [shape(dims, arrays[0].dtype if body is total_kernel else BF16)]
        parts.append((body, len(arrays), len(outs)))
        args += arrays
        out_shapes += outs
    moved = sum(4 * np.prod(o.shape) for o in out_shapes)
    results = pl.pallas_call(
        functools.partial(sums_kernel, tuple(parts)),
        out_shape=tuple(out_shapes),
        in_specs=[SMEM] + [VMEM] * len(args),
        out_specs=(VMEM,) * len(out_shapes),
        compiler_params=params(16),
        cost_estimate=cost(0, moved),
    )(place, *args)
    grouped = []
    for _, _, count in parts:
        grouped.append(tuple(results[:count]))
        results = results[count:]
    return grouped


def finish_kernel(place, *refs):
    mine, other, (grad_input, grad_mixer, *outs) = refs[:4], refs[4:8], refs[8:]
    half = mine[0].shape[1]
    for flip in range(4):
        quarter = lax.bitwise_xor(place[0], flip)
        for side, parts in enumerate((mine, other)):
            part = place[1] if side == 0 else 1 - place[1]
            at = pl.ds(pl.multiple_of((2 * quarter + part) * half, 8), half)
            for matrix, out in enumerate(outs):
                out[at, :] = parts[flip][1 + matrix, :, :].astype(F32)

            @pl.when(quarter < 3)
            def _():
                grad_input[at, :] = parts[flip][0, :, :].astype(F32)

            @pl.when(quarter == 3)
            def _():
                rows = pl.ds(pl.multiple_of(part * half, 8), half)
                grad_mixer[rows, :] = parts[flip][0, :, :].astype(F32)


def finish(place, mine, other):
    half, width = mine[0].shape[1:]
    return pl.pallas_call(
        finish_kernel,
        out_shape=tuple(shape((count * half, width), F32) for count in (6, 2, 8, 8)),
        in_specs=[SMEM] + [VMEM] * 8,
        out_specs=(VMEM,) * 4,
        compiler_params=params(20),
        cost_estimate=cost(0, half * width * 144),
    )(place, *mine, *other)


def local(
    tokens,
    visible_counts,
    norm_one_gain,
    norm_one_shift,
    input_weight,
    input_bias,
    mixer_weight,
    mixer_bias,
    norm_two_gain,
    norm_two_shift,
    up_weight,
    up_bias,
    down_weight,
    down_bias,
    output_grad,
    groups,
    outer,
):
    width = tokens.shape[1]
    rows = tokens.shape[0]
    cols = mixer_weight.shape[0]
    t = lax.axis_index("t")
    core = lax.axis_index("c")
    place = jnp.stack([2 * lax.axis_index("a") + lax.axis_index("b"), core, t]).astype(jnp.int32)
    one_row = lambda v: v.reshape(1, -1)

    swap = [(0, 1), (1, 0)]
    cross = [(0, 3), (1, 2), (2, 1), (3, 0)]
    to_near = [(z, (z + 1) % groups) for z in range(groups)] + [
        (groups + z, groups + (z + 2) % groups) for z in range(groups)
    ]
    to_far = [(groups + z, groups + (z + 3) % groups) for z in range(groups)]
    home_near = [(j, i) for i, j in to_near]
    home_far = [(j, i) for i, j in to_far]

    def spread(piece):
        return (
            piece,
            lax.ppermute(piece, "b", swap),
            lax.ppermute(piece, "a", swap),
            lax.ppermute(piece, ("a", "b"), cross),
        )

    def together(*groups):
        return lax.optimization_barrier(groups)

    def after(value, *others):
        return lax.optimization_barrier((value, *others))[0]

    def first_exchange(send_x, send_y, keep_x, keep_y):
        got_x = lax.ppermute(send_x, "b", swap)
        got_y = lax.ppermute(send_y, "a", swap)
        return keep_x, keep_y, got_x, got_y

    def second_exchange(send_y, send_x, base):
        return base, lax.ppermute(send_y, "a", swap), lax.ppermute(send_x, "b", swap)

    def direct(keep, send_x, send_y, send_xy):
        return (
            keep,
            lax.ppermute(send_x, "b", swap),
            lax.ppermute(send_y, "a", swap),
            lax.ppermute(send_xy, ("a", "b"), cross),
        )

    def over_outer(value):
        return lax.psum(value.astype(F32), "o").astype(BF16) if outer > 1 else value

    projection = input_weight.transpose(1, 2, 0).reshape(3 * cols, width)
    normed_one = norm_one(
        place,
        visible_counts,
        tokens,
        one_row(norm_one_gain),
        one_row(norm_one_shift),
    )
    piece_one, tail_one = pack_attention(
        place, projection, mixer_weight, after(input_bias, normed_one), one_row(up_bias)
    )
    depth_near_one = lax.ppermute(piece_one, ("c", "t"), to_near)
    normed_other = lax.ppermute(normed_one, "c", swap)
    piece_two = pack_hidden(place, up_weight, down_weight)
    depth_near_one, normed_other, piece_two = together(depth_near_one, normed_other, piece_two)
    near_one = spread(depth_near_one)
    far_projection = lax.ppermute(after(projection, depth_near_one), ("c", "t"), to_far)
    far_mixer = lax.ppermute(after(tail_one, depth_near_one), ("c", "t"), to_far)
    near_two = lax.ppermute(after(piece_two, far_mixer, *near_one), ("c", "t"), to_near)

    own_one = (projection, tail_one)
    far_one = (far_projection, far_mixer)
    saved, soft, part = attention(place, own_one, near_one, far_one, normed_other, None, BF16)
    saved, soft, part, near_two = together(saved, soft, part, near_two)
    grad_other = lax.ppermute(after(output_grad, part), "c", swap)
    part_received = lax.ppermute(part, "c", swap)
    near_x = lax.ppermute(near_two, "b", swap)
    near_y = lax.ppermute(near_two, "a", swap)
    far_up = lax.ppermute(after(up_weight, near_two), ("c", "t"), to_far)
    saved, soft, part = attention(
        place, own_one, near_one, far_one, normed_one, (saved, soft), F32
    )
    part, part_received, near_x, near_y, far_up, grad_other = together(
        part, part_received, near_x, near_y, far_up, grad_other
    )
    quarter = near_two.shape[0] // 2
    near_up = lax.ppermute(near_y[:quarter], "b", swap)
    near_down = lax.ppermute(near_x[quarter:], "a", swap)
    first_sum, normed_two = norm_two(
        tokens,
        part,
        part_received,
        one_row(mixer_bias),
        one_row(norm_two_gain),
        one_row(norm_two_shift),
    )
    normed_two_other = lax.ppermute(normed_two, "c", swap)
    normed_two, first_sum, near_up, near_down = together(
        normed_two, first_sum, near_up, near_down
    )
    far_down = lax.ppermute(after(down_weight, far_up), ("c", "t"), to_far)
    normed_two_both = (normed_two, normed_two_other)

    grad_both = (output_grad, grad_other)
    pieces = (near_two, near_x, near_y, near_up, near_down, depth_near_one)
    near_outs = hidden_block(place, pieces, normed_two_both, grad_both, False)
    near_outs, far_down = together(near_outs, far_down)
    *grads_near, bias_near, out_near, out_send, back_near, back_send = near_outs
    stage_near = first_exchange(*grads_near)
    back_near_received = lax.ppermute(back_send, "c", swap)
    out_near_received = lax.ppermute(out_send, "c", swap)
    shards = (up_weight, down_weight, tail_one, far_up, far_down, far_mixer)
    far_outs = hidden_block(place, shards, normed_two_both, grad_both, True)
    far_outs, stage_near, back_near_received, out_near_received = together(
        far_outs, stage_near, back_near_received, out_near_received
    )
    grads_far, bias_far, out_far, out_send, back_far_mine, back_send = far_outs

    got_far = lax.ppermute(grads_far, ("c", "t"), home_far)
    back_received = lax.ppermute(back_send, "c", swap)
    (stage_near,) = sums(place, (first_sums_kernel, stage_near))
    back_received = after(back_received, *stage_near)
    stage_near = second_exchange(*stage_near)
    grad_first_low, sums_two = norm_two_back(
        (back_near, back_near_received, back_far_mine, back_received),
        first_sum,
        one_row(norm_two_gain),
        output_grad,
    )
    first_other = lax.ppermute(grad_first_low, "c", swap)
    out_received = lax.ppermute(after(out_send, first_other), "c", swap)

    normed_both = (normed_one, normed_other)
    first_both = (grad_first_low, first_other)
    *grads_one_near, bias_one_near, back_near, back_send = attention_back(
        place, 1, None, near_one, normed_both, first_both, saved, soft
    )
    grads_one_near, back_near, back_send, stage_near, got_far, out_received = together(
        grads_one_near, back_near, back_send, stage_near, got_far, out_received
    )
    one_near = direct(*grads_one_near)
    (plane_near,), (send_far,) = sums(
        place, (plane_sums_kernel, stage_near), (pair_send_kernel, (grads_far, got_far))
    )
    depth_near = lax.ppermute(plane_near, ("c", "t"), home_near)
    received_far = lax.ppermute(send_far, "c", swap)
    back_near_send = after(back_send, received_far)
    grad_low_late = after(grad_first_low, plane_near)
    *grads_one_far, bias_one_far, back_far_mine, back_send = attention_back(
        place, 0, own_one, far_one, normed_both, (grad_low_late, first_other), saved, soft
    )
    grads_one_far, back_far_mine, back_send, one_near, received_far, depth_near = together(
        grads_one_far, back_far_mine, back_send, one_near, received_far, depth_near
    )
    back_near_received = lax.ppermute(back_near_send, "c", swap)

    one_far = direct(*grads_one_far)
    back_received = lax.ppermute(back_send, "c", swap)
    (one_near,), sums_far, (keep_two, send_two) = sums(
        place,
        (total_kernel, one_near),
        (pair_sums_kernel, (grads_far, got_far, received_far)),
        (half_split_kernel, (depth_near,)),
    )
    one_depth_near = lax.ppermute(one_near, ("c", "t"), home_near)
    received_two = lax.ppermute(send_two, "c", swap)
    grad_tokens, vectors = norm_one_back(
        groups,
        place,
        (back_near, back_near_received, back_far_mine, back_received),
        tokens,
        one_row(norm_one_gain),
        grad_first_low,
        sums_two,
        bias_near,
        bias_far,
        bias_one_near,
        bias_one_far,
    )
    vectors_core = lax.ppermute(vectors, "c", swap)
    vectors_core, one_far, received_two = together(vectors_core, one_far, received_two)
    (one_far,), (vectors,) = sums(
        place, (total_kernel, one_far), (total_kernel, (vectors, vectors_core))
    )
    one_depth_far = lax.ppermute(one_far, ("c", "t"), home_far)
    sums_far = direct(*sums_far)
    result = (
        first_sum
        + (out_near.astype(F32) + out_near_received.astype(F32))
        + (out_far.astype(F32) + out_received.astype(F32))
        + down_bias
    ).astype(BF16)
    one_depth_far, one_depth_near, result = together(one_depth_far, one_depth_near, result)
    ((keep_one, send_one),) = sums(
        place, (depth_sums_kernel, (one_far, one_depth_far, one_depth_near))
    )
    received_one = lax.ppermute(send_one, "c", swap)
    vectors_plane = spread(vectors)
    received_one, vectors_plane, sums_far = together(received_one, vectors_plane, sums_far)
    (parts,), (vectors,) = sums(
        place,
        (last_sums_kernel, (keep_one, received_one, *sums_far, keep_two, received_two)),
        (total_kernel, vectors_plane),
    )
    mine = spread(over_outer(parts))
    turns = [
        lax.ppermute(vectors, "t", [(z, (z + k) % groups) for z in range(groups)])
        for k in range(1, groups)
    ]
    vectors = sum(turns, vectors)
    if outer > 1:
        vectors = lax.psum(vectors, "o")
    grad_up_bias = lax.dynamic_slice_in_dim(vectors, 6 + t, 1)[0]
    grad_input_bias = lax.dynamic_slice_in_dim(vectors, 6 + groups + t, 1).reshape(-1, cols)[:2]
    rows_out = [vectors[index] for index in range(6)]
    mine, rows_out, grad_up_bias, grad_input_bias = together(
        mine, rows_out, grad_up_bias, grad_input_bias
    )
    other = tuple(lax.ppermute(part, "c", swap) for part in mine)
    grad_input, grad_mixer, grad_up, grad_down = finish(place, mine, other)
    grad_input = grad_input.reshape(3, cols, width).transpose(2, 0, 1)
    return (
        result,
        grad_tokens,
        rows_out[0],
        rows_out[1],
        grad_input,
        grad_input_bias,
        grad_mixer,
        rows_out[4],
        rows_out[2],
        rows_out[3],
        grad_up,
        grad_up_bias,
        grad_down,
        rows_out[5],
    )


def solution(mesh):
    dp, groups = mesh.shape["dp"], mesh.shape["tensor"]
    outer = dp // 8
    split = jax.sharding.Mesh(
        mesh.devices.reshape(outer, 2, 2, 2, groups), ("o", "a", "b", "c", "t")
    )
    dp_axes = ("o", "a", "b", "c")
    all_axes = dp_axes + ("t",)
    in_specs = (
        P(all_axes, None),
        P(dp_axes),
        P(),
        P(),
        P(None, None, "t"),
        P(None, "t"),
        P("t", None),
        P(),
        P(),
        P(),
        P(None, "t"),
        P("t"),
        P("t", None),
        P(),
        P(all_axes, None),
    )
    out_specs = (
        P(all_axes, None),
        P(all_axes, None),
        P(),
        P(),
        P(None, None, "t"),
        P(None, "t"),
        P("t", None),
        P(),
        P(),
        P(),
        P(None, "t"),
        P("t"),
        P("t", None),
        P(),
    )
    return jax.shard_map(
        functools.partial(local, groups=groups, outer=outer),
        mesh=split,
        in_specs=in_specs,
        out_specs=out_specs,
        check_vma=False,
    )
```

```python
import functools

import jax
import jax.numpy as jnp
import numpy as np
from jax import lax
from jax.experimental import pallas as pl
from jax.experimental.pallas import tpu as pltpu
from jax.sharding import PartitionSpec as P

HD = 64
SLOTS = 80
LANES = 128
TILE_IMAGES = 4
MASKED = -1000000000.0
EPS = 1e-06
F32 = jnp.float32
BF16 = jnp.bfloat16

ANY = pl.BlockSpec(memory_space=pl.ANY)
SMEM = pl.BlockSpec(memory_space=pltpu.SMEM)
VMEM = pl.BlockSpec(memory_space=pltpu.VMEM)


def shape(dims, kind):
    return jax.ShapeDtypeStruct(tuple(dims), kind)


def kept(dims, kind):
    return pltpu.HBM(tuple(dims), kind)


def from_hbm(*arrays):
    return tuple(pltpu.with_memory_space_constraint(a, pltpu.HBM) for a in arrays)


def params(megabytes, grid_dims=0):
    semantics = ("arbitrary",) * grid_dims if grid_dims else None
    return pltpu.CompilerParams(
        vmem_limit_bytes=megabytes * 1024 * 1024, dimension_semantics=semantics
    )


def cost(flops, moved):
    return pl.CostEstimate(flops=int(flops), bytes_accessed=int(moved), transcendentals=0)


def dot(left, right):
    return lax.dot_general(left, right, (((1,), (0,)), ((), ())), preferred_element_type=F32)


def dot_rows(left, right):
    return lax.dot_general(left, right, (((1,), (1,)), ((), ())), preferred_element_type=F32)


def dot_columns(left, right):
    return lax.dot_general(left, right, (((0,), (0,)), ((), ())), preferred_element_type=F32)


def centred(rows):
    center = rows - jnp.mean(rows, axis=-1, keepdims=True)
    spread = jnp.mean(center * center, axis=-1, keepdims=True)
    return center, lax.rsqrt(spread + EPS)


def norm_back(rows, gain, grad):
    center, rstd = centred(rows)
    xhat = center * rstd
    e = grad * gain
    back = rstd * (
        e - jnp.mean(e, axis=-1, keepdims=True) - xhat * jnp.mean(e * xhat, axis=-1, keepdims=True)
    )
    return (
        back,
        jnp.sum(grad * xhat, axis=0, keepdims=True),
        jnp.sum(grad, axis=0, keepdims=True),
    )


def norm_one_kernel(images, chunk, place, counts, tokens, gain, shift, out):
    rows = tokens.shape[0]

    @pl.loop(0, rows // chunk)
    def _(step):
        at = pl.ds(pl.multiple_of(step * chunk, chunk), chunk)
        center, rstd = centred(tokens[at, :].astype(F32))
        out[at, :] = (
            center * rstd * gain[...].reshape(1, -1) + shift[...].reshape(1, -1)
        ).astype(BF16)

    extra = out.shape[0] - rows
    row = lax.broadcasted_iota(jnp.int32, (extra, out.shape[1]), 0)
    table = jnp.zeros((extra, out.shape[1]), F32)
    first = place[2] * images
    for image in range(images):
        table = jnp.where(row == image, counts[first + image].astype(F32), table)
    out[rows:, :] = table.astype(BF16)


def norm_one(place, counts, tokens, gain, shift):
    rows, width = tokens.shape
    images = rows // SLOTS
    return pl.pallas_call(
        functools.partial(norm_one_kernel, images, SLOTS),
        out_shape=shape((rows + 16, width), BF16),
        in_specs=[SMEM, SMEM, VMEM, VMEM, VMEM],
        out_specs=VMEM,
        compiler_params=params(16),
        cost_estimate=cost(rows * width * 10, rows * width * 4),
    )(place, counts, tokens, gain, shift)


def norm_two_kernel(tokens, mine, received, bias, gain, shift, first_sum, normed):
    total = tokens[...].astype(F32) + (mine[...] + received[...].astype(F32)) + bias[...]
    first_sum[...] = total
    center, rstd = centred(total)
    normed[...] = (center * rstd * gain[...] + shift[...]).astype(BF16)


def rows_spec(tile, width):
    return pl.BlockSpec((tile, width), lambda i: (i, 0))


def fixed_spec(*dims):
    return pl.BlockSpec(dims, lambda i: (0,) * len(dims))


def norm_two(tokens, mine, received, bias, gain, shift):
    rows, width = tokens.shape
    tile = 2 * SLOTS
    row = rows_spec(tile, width)
    vector = fixed_spec(1, width)
    return pl.pallas_call(
        norm_two_kernel,
        grid=(rows // tile,),
        out_shape=(kept((rows, width), F32), shape((rows, width), BF16)),
        in_specs=[row, row, row, vector, vector, vector],
        out_specs=(row, row),
        compiler_params=params(16, 1),
        cost_estimate=cost(rows * width * 12, rows * width * 14),
    )(*from_hbm(tokens), mine, received, bias, gain, shift)


def added(*refs):
    total = refs[0][...].astype(F32)
    for ref in refs[1:]:
        total = total + ref[...].astype(F32)
    return total


def norm_two_back_kernel(
    part0, part1, part2, part3, first_sum, gain, output_grad, low, sums
):
    grad = added(part0, part1, part2, part3)
    back, grad_gain, grad_shift = norm_back(first_sum[...], gain[...], grad)
    out_grad = output_grad[...].astype(F32)
    total = out_grad + back
    low[...] = total.astype(BF16)

    @pl.when(pl.program_id(0) == 0)
    def _():
        sums[...] = jnp.zeros_like(sums)

    sums[0:1, :] += grad_gain
    sums[1:2, :] += grad_shift
    sums[2:3, :] += jnp.sum(total, axis=0, keepdims=True)
    sums[3:4, :] += jnp.sum(out_grad, axis=0, keepdims=True)


def norm_two_back(parts, first_sum, gain, output_grad):
    rows, width = parts[0].shape
    tile = 2 * SLOTS
    row = rows_spec(tile, width)
    return pl.pallas_call(
        norm_two_back_kernel,
        grid=(rows // tile,),
        out_shape=(shape((rows, width), BF16), shape((8, width), F32)),
        in_specs=[row] * 5 + [fixed_spec(1, width), row],
        out_specs=(row, fixed_spec(8, width)),
        compiler_params=params(16, 1),
        cost_estimate=cost(rows * width * 25, rows * width * 18),
    )(*parts, *from_hbm(first_sum), gain, *from_hbm(output_grad))


def norm_one_back_kernel(
    groups,
    place,
    part0,
    part1,
    part2,
    part3,
    tokens,
    gain,
    grad_first,
    sums_two,
    bias_near,
    bias_far,
    input_near,
    input_far,
    grad_tokens,
    vectors,
):
    grad = added(part0, part1, part2, part3)
    back, grad_gain, grad_shift = norm_back(tokens[...].astype(F32), gain[...], grad)
    grad_tokens[...] = grad_first[...].astype(F32) + back

    @pl.when(pl.program_id(0) == 0)
    def _():
        near = lax.rem(place[2] - 1 - place[1] + groups, groups)
        far = lax.rem(place[2] - 3 * place[1] + groups, groups)
        row = lax.broadcasted_iota(jnp.int32, vectors.shape, 0)
        table = jnp.zeros(vectors.shape, F32)
        for index in range(4):
            table = jnp.where(row == 2 + index, sums_two[index : index + 1, :], table)
        table = jnp.where(row == 6 + near, bias_near[0:1, :], table)
        vectors[...] = jnp.where(row == 6 + far, bias_far[0:1, :], table)
        columns = input_near.shape[1]
        few = lax.broadcasted_iota(jnp.int32, (vectors.shape[0], columns), 0)
        for index in range(2):
            table = jnp.where(
                few == 6 + groups + near, input_near[index : index + 1, :], 0.0
            ) + jnp.where(few == 6 + groups + far, input_far[index : index + 1, :], 0.0)
            vectors[:, index * columns : (index + 1) * columns] += table

    vectors[0:1, :] += grad_gain
    vectors[1:2, :] += grad_shift


def norm_one_back(groups, place, parts, tokens, gain, grad_first, *small):
    rows, width = parts[0].shape
    tile = 2 * SLOTS
    row = rows_spec(tile, width)
    return pl.pallas_call(
        functools.partial(norm_one_back_kernel, groups),
        grid=(rows // tile,),
        out_shape=(kept((rows, width), F32), shape((16, width), F32)),
        in_specs=[SMEM] + [row] * 5 + [fixed_spec(1, width), row]
        + [fixed_spec(*array.shape) for array in small],
        out_specs=(row, fixed_spec(16, width)),
        compiler_params=params(16, 1),
        cost_estimate=cost(rows * width * 25, rows * width * 16),
    )(place, *parts, *from_hbm(tokens), gain, *from_hbm(grad_first), *small)


def pack_attention_kernel(place, projection, mixer, bias, up_bias, out, tail, sem, tail_sem):
    quarter = place[0]
    tail_copy = pltpu.make_async_copy(mixer, tail.at[pl.ds(0, mixer.shape[0])], tail_sem)
    tail_copy.start()
    size = out.shape[0] - 16
    feature_rows = projection.shape[0]
    first = pl.multiple_of(quarter * size, 16)
    from_projection = quarter * size < feature_rows

    @pl.when(from_projection)
    def _():
        copy = pltpu.make_async_copy(
            projection.at[pl.ds(first, size)], out.at[pl.ds(0, size)], sem
        )
        copy.start()
        copy.wait()

    @pl.when(jnp.logical_not(from_projection))
    def _():
        copy = pltpu.make_async_copy(mixer, out.at[pl.ds(0, size)], sem)
        copy.start()
        copy.wait()

    columns = bias.shape[1]
    row = lax.broadcasted_iota(jnp.int32, (16, columns), 0)
    both = bias[...].astype(F32)
    rows = jnp.where(row == 0, both[0:1, :], jnp.where(row == 1, both[1:2, :], 0.0))
    row_all = lax.broadcasted_iota(jnp.int32, (16, out.shape[1]), 0)
    out[size:, :] = jnp.where(row_all == 2, up_bias[...].astype(F32), 0.0).astype(BF16)
    row_two = jnp.where(row == 2, up_bias[:, 0:columns].astype(F32), rows)
    out[size:, 0:columns] = row_two.astype(BF16)
    tail[size:, :] = out[size:, :]
    tail_copy.wait()


def pack_attention(place, projection, mixer, bias, up_bias):
    size, width = mixer.shape
    return pl.pallas_call(
        pack_attention_kernel,
        out_shape=(shape((size + 16, width), BF16),) * 2,
        in_specs=[SMEM, ANY, ANY, VMEM, VMEM],
        out_specs=(VMEM, VMEM),
        scratch_shapes=[pltpu.SemaphoreType.DMA(()), pltpu.SemaphoreType.DMA(())],
        compiler_params=params(16),
        cost_estimate=cost(0, 2 * size * width),
    )(place, *from_hbm(projection, mixer), bias, up_bias)


def pack_hidden_kernel(place, up, down, out, sems):
    size = out.shape[0] // 2
    first = pl.multiple_of(place[0] * size, 16)
    copies = [
        pltpu.make_async_copy(
            source.at[pl.ds(first, size)], out.at[pl.ds(index * size, size)], sems.at[index]
        )
        for index, source in enumerate((up, down))
    ]
    run_copies(copies)


def pack_hidden(place, up, down):
    size, width = up.shape[0] // 4, up.shape[1]
    return pl.pallas_call(
        pack_hidden_kernel,
        out_shape=shape((2 * size, width), BF16),
        in_specs=[SMEM, ANY, ANY],
        out_specs=VMEM,
        scratch_shapes=[pltpu.SemaphoreType.DMA((2,))],
        compiler_params=params(16),
        cost_estimate=cost(0, 4 * size * width),
    )(place, *from_hbm(up, down))


def run_copies(copies):
    for copy in copies:
        copy.start()
    for copy in copies:
        copy.wait()


def make_copies(copies, sems):
    return [
        pltpu.make_async_copy(source, to, sems.at[index])
        for index, (source, to) in enumerate(copies)
    ]


def piece_copies(place, pieces, target, sems):
    size = pieces[0].shape[0] - 16
    copies = []
    for flip, piece in enumerate(pieces):
        to = pl.multiple_of(lax.bitwise_xor(place[0], flip) * size, 16)
        copies.append((piece.at[pl.ds(0, size)], target.at[pl.ds(to, size)]))
    copies.append((pieces[0].at[pl.ds(size, 16)], target.at[pl.ds(4 * size, 16)]))
    return make_copies(copies, sems)


def hidden_copies(place, pieces, bias_piece, target, sems):
    size = pieces[0].shape[0] // 2
    copies = []
    for flip in range(4):
        quarter = lax.bitwise_xor(place[0], flip)
        for matrix in range(2):
            to = pl.multiple_of((4 * matrix + quarter) * size, 16)
            source = pieces[3 + matrix] if flip == 3 else pieces[flip].at[pl.ds(matrix * size, size)]
            copies.append((source, target.at[pl.ds(to, size)]))
    first = bias_piece.shape[0] - 16
    copies.append((bias_piece.at[pl.ds(first, 16)], target.at[pl.ds(8 * size, 16)]))
    return make_copies(copies, sems)


def head_lanes(rows, width):
    return lax.broadcasted_iota(jnp.int32, (rows, width), 1) // HD


def spread_heads(block, lanes, heads):
    gap = jnp.zeros((LANES - SLOTS, block.shape[1]), block.dtype)
    parts = []
    for head in range(heads):
        parts.append(jnp.where(lanes == head, block, jnp.zeros_like(block)))
        parts.append(gap)
    return jnp.concatenate(parts, axis=0)


def gather_heads(product, lanes, heads):
    total = product[0:SLOTS]
    for head in range(1, heads):
        total = jnp.where(lanes == head, product[head * LANES : head * LANES + SLOTS], total)
    return total


def start_on_core(place, own, far, cut, sems):
    copies = [make_copies(cut(parts), sems) for parts in (own, far)]
    for core, some in enumerate(copies):

        @pl.when(place[1] == core)
        def _():
            for copy in some:
                copy.start()

    return copies[0]


def start_far(place, own, far, target, sems):
    def cut(parts):
        size = parts[0].shape[0]
        return [
            (parts[0], target.at[pl.ds(0, size)]),
            (parts[1], target.at[pl.ds(size, parts[1].shape[0])]),
        ]

    return start_on_core(place, own, far, cut, sems)


def start_matrices(place, own, far, target, sems):
    def cut(parts):
        size = parts[0].shape[0]
        bias = parts[2].at[pl.ds(parts[2].shape[0] - 16, 16)]
        return [
            (parts[0], target.at[pl.ds(0, size)]),
            (parts[1], target.at[pl.ds(size, size)]),
            (bias, target.at[pl.ds(2 * size, 16)]),
        ]

    return start_on_core(place, own, far, cut, sems)


def attention_kernel(
    heads,
    place,
    projection,
    tail,
    near0,
    near1,
    near2,
    near3,
    far0,
    far1,
    normed,
    counts,
    *rest,
):
    saved, soft, part, weights, table, sems = rest[-6:]

    @pl.when(pl.program_id(0) == 0)
    def _():
        copies = piece_copies(place, (near0, near1, near2, near3), weights.at[1], sems)
        for copy in copies:
            copy.start()
        far_sems = sems.at[pl.ds(8, 8)]
        copies += start_far(place, (projection, tail), (far0, far1), weights.at[0], far_sems)
        for copy in copies:
            copy.wait()

    cols = heads * HD
    visible_rows = counts[:, 0:LANES].astype(F32)
    for image in range(visible_rows.shape[0]):
        table[image, :, :] = visible_rows[image : image + 1, :]
    rows = normed[...]
    for slot in range(2):
        for index in range(3):
            value = dot_rows(rows, weights[slot, index * cols : (index + 1) * cols, :])
            if index != 1:
                bias_row = 0 if index == 0 else 1
                bias = weights[slot, 4 * cols : 4 * cols + 16, 0:cols].astype(F32)
                value = value + bias[bias_row : bias_row + 1, :]
            saved[4 * slot + index, :, :] = value.astype(BF16)

    lanes = head_lanes(SLOTS, cols)
    key_index = lax.broadcasted_iota(jnp.int32, (SLOTS, LANES), 1).astype(F32)
    first = pl.program_id(0) * TILE_IMAGES

    def one_image(image, carry):
        at = pl.ds(pl.multiple_of(image * SLOTS, 16), SLOTS)
        visible = key_index < table[first + image]
        for slot in range(2):
            queries = saved[4 * slot, at, :]
            keys = spread_heads(saved[4 * slot + 1, at, :], lanes, heads)
            values = spread_heads(saved[4 * slot + 2, at, :], lanes, heads)
            scores = dot_rows(queries, keys) * (HD**-0.5)
            lows = []
            for head in range(heads):
                one = jnp.where(visible, scores[:, head * LANES : (head + 1) * LANES], MASKED)
                exponent = jnp.exp(one - jnp.max(one, axis=-1, keepdims=True))
                total = jnp.sum(exponent, axis=-1, keepdims=True)
                lows.append((exponent / total).astype(BF16))
            low = jnp.concatenate(lows, axis=1)
            soft[at, slot * heads * LANES : (slot + 1) * heads * LANES] = low
            saved[4 * slot + 3, at, :] = dot(low, values).astype(BF16)
        return carry

    lax.fori_loop(0, TILE_IMAGES, one_image, 0, unroll=True)
    total = dot(saved[3, :, :], weights[0, 3 * cols : 4 * cols, :])
    total = total + dot(saved[7, :, :], weights[1, 3 * cols : 4 * cols, :])
    part[...] = total.astype(part.dtype)


def attention(place, own, near, far, normed, before, kind):
    projection, tail = own
    cols, width = projection.shape[0] // 3, projection.shape[1]
    heads = cols // HD
    rows = normed.shape[0] - 16
    tile = TILE_IMAGES * SLOTS
    tiles = rows // tile
    base = tiles if before is None else 0
    extra = () if before is None else from_hbm(*before)
    args = (place, projection, tail, *near, *far, normed, normed, *extra)
    return pl.pallas_call(
        functools.partial(attention_kernel, heads),
        grid=(tiles,),
        out_shape=(
            kept((8, 2 * rows, cols), BF16),
            kept((2 * rows, 2 * heads * LANES), BF16),
            shape((rows, width), kind),
        ),
        in_specs=[SMEM]
        + [ANY] * 8
        + [
            pl.BlockSpec((tile, width), lambda i: (i, 0)),
            pl.BlockSpec((16, width), lambda i: (rows // 16, 0)),
        ]
        + [ANY] * len(extra),
        out_specs=(
            pl.BlockSpec((8, tile, cols), lambda i: (0, base + i, 0)),
            pl.BlockSpec((tile, 2 * heads * LANES), lambda i: (base + i, 0)),
            pl.BlockSpec((tile, width), lambda i: (i, 0)),
        ),
        scratch_shapes=[
            pltpu.VMEM((2, 4 * cols + 16, width), BF16),
            pltpu.VMEM((16, 1, LANES), F32),
            pltpu.SemaphoreType.DMA((16,)),
        ],
        input_output_aliases={11: 0, 12: 1} if extra else {},
        compiler_params=params(20, 1),
        cost_estimate=cost(rows * width * cols * 16 + rows * 400000, rows * width * 10 + 5e6),
    )(*args)


def attention_back_kernel(heads, far, place, *rest):
    count = 4
    pieces, rest = rest[:count], rest[count:]
    normed_mine, normed_other, grad_mine, grad_other, saved, soft = rest[:6]
    rest = rest[6:]
    keep, send_x, send_y, send_xy, bias_sums = rest[:5]
    rest = rest[5:]
    back_mine, back_other, weights, sums, grads, sems = rest
    step = pl.program_id(0)
    steps = pl.num_programs(0)
    cols = heads * HD
    mine = step < steps // 2

    @pl.when(step == 0)
    def _():
        if far:
            copies = start_far(place, pieces[:2], pieces[2:], weights, sems)
        else:
            copies = piece_copies(place, pieces, weights, sems)
            for copy in copies:
                copy.start()
        for copy in copies:
            copy.wait()
        sums[...] = jnp.zeros_like(sums)
        bias_sums[...] = jnp.zeros_like(bias_sums)

    normed = jnp.where(mine, normed_mine[...], normed_other[...])
    grad = jnp.where(mine, grad_mine[...], grad_other[...])
    grads[3, :, :] = dot_rows(grad, weights[3 * cols : 4 * cols, :]).astype(BF16)
    lanes = head_lanes(SLOTS, cols)

    def one_image(image, carry):
        at = pl.ds(pl.multiple_of(image * SLOTS, 16), SLOTS)
        queries = saved[0, at, :]
        keys = spread_heads(saved[1, at, :], lanes, heads)
        values = spread_heads(saved[2, at, :], lanes, heads)
        grad_mixed = grads[3, at, :]
        low = soft[at, :]
        grad_soft = dot_rows(grad_mixed, values)
        lows = []
        for head in range(heads):
            one = low[:, head * LANES : (head + 1) * LANES].astype(F32)
            grad_one = grad_soft[:, head * LANES : (head + 1) * LANES]
            inner = jnp.sum(grad_one * one, axis=-1, keepdims=True)
            lows.append((one * (grad_one - inner) * (HD**-0.5)).astype(BF16))
        grad_scores = jnp.concatenate(lows, axis=1)
        grad_queries = dot(grad_scores, keys)
        grad_values = gather_heads(dot_columns(low, grad_mixed), lanes, heads)
        grad_keys = gather_heads(dot_columns(grad_scores, queries), lanes, heads)
        bias_sums[0:1, :] += jnp.sum(grad_queries, axis=0, keepdims=True)
        bias_sums[1:2, :] += jnp.sum(grad_values, axis=0, keepdims=True)
        grads[0, at, :] = grad_queries.astype(BF16)
        grads[1, at, :] = grad_keys.astype(BF16)
        grads[2, at, :] = grad_values.astype(BF16)
        return carry

    lax.fori_loop(0, TILE_IMAGES, one_image, 0, unroll=True)
    back = None
    for index in range(3):
        at = slice(index * cols, (index + 1) * cols)
        value = grads[index, :, :]
        term = dot(value, weights[at, :])
        back = term if back is None else back + term
        sums[at, :] += dot_columns(value, normed)
    sums[3 * cols : 4 * cols, :] += dot_columns(saved[3, :, :], grad)

    @pl.when(mine)
    def _():
        back_mine[...] = back.astype(BF16)

    @pl.when(jnp.logical_not(mine))
    def _():
        back_other[...] = back.astype(BF16)

    @pl.when(step == steps - 1)
    def _():
        size = keep.shape[2]
        for flip, ref in enumerate((keep, send_x, send_y, send_xy)):
            quarter = lax.bitwise_xor(place[0], flip)
            for half in range(2):
                at = pl.ds(pl.multiple_of((2 * quarter + half) * size, 16), size)
                ref[half, 0, :, :] = sums[at, :].astype(BF16)


def half_spec(tile, width, tiles, second):
    if second:
        return pl.BlockSpec((tile, width), lambda i: (jnp.maximum(i - tiles, 0), 0))
    return pl.BlockSpec((tile, width), lambda i: (jnp.minimum(i, tiles - 1), 0))


def attention_back(place, slot, own, pieces, normed, grads, saved, soft):
    rows, width = grads[0].shape
    cols = saved.shape[2]
    heads = cols // HD
    tile = TILE_IMAGES * SLOTS
    tiles = rows // tile
    far = own is not None
    mine, other = half_spec(tile, width, tiles, False), half_spec(tile, width, tiles, True)
    dims = (2, 1, cols // 2, width)
    weights = (*own, *pieces) if far else pieces
    return pl.pallas_call(
        functools.partial(attention_back_kernel, heads, far),
        grid=(2 * tiles,),
        out_shape=(
            *(shape(dims, BF16),) * 4,
            shape((8, cols), F32),
            shape((rows, width), BF16),
            shape((rows, width), BF16),
        ),
        in_specs=[SMEM]
        + [ANY] * 4
        + [
            mine,
            other,
            mine,
            other,
            pl.BlockSpec((4, tile, cols), lambda i: (slot, i, 0)),
            pl.BlockSpec((tile, heads * LANES), lambda i: (i, slot)),
        ],
        out_specs=(*(fixed_spec(*dims),) * 4, fixed_spec(8, cols), mine, other),
        scratch_shapes=[
            pltpu.VMEM((4 * cols + 16, width), BF16),
            pltpu.VMEM((4 * cols, width), F32),
            pltpu.VMEM((4, tile, cols), BF16),
            pltpu.SemaphoreType.DMA((16,)),
        ],
        compiler_params=params(24, 1),
        cost_estimate=cost(rows * width * cols * 30 + rows * 6e5, rows * width * 20 + 4e6),
    )(place, *weights, *normed, *grads, *from_hbm(saved, soft))


def hidden_kernel(last, place, *rest):
    pieces, rest = rest[:6], rest[6:]
    normed_parts, grad_parts, rest = rest[:2], rest[2:4], rest[4:]
    if last:
        whole_grads, rest = rest[0], rest[1:]
    else:
        (send_x, send_y, keep_x, keep_y), rest = rest[:4], rest[4:]
    bias_sums, out_mine, out_other, back_mine, back_other = rest[:5]
    rest = rest[5:]
    weights, normed, grad, active, grad_low, sums_up, sums_down, summed = rest[:8]
    piece_sems, sems, out_sems = rest[8:]
    rows, width = normed.shape
    half = rows // 2

    def load(first, parts, target):
        return [
            pltpu.make_async_copy(part, target.at[pl.ds(index * half, half)], sems.at[first + index])
            for index, part in enumerate(parts)
        ]

    normed_copies, grad_copies = load(0, normed_parts, normed), load(2, grad_parts, grad)
    for copy in normed_copies:
        copy.start()
    if last:
        starts = start_matrices(place, pieces[:3], pieces[3:], weights, piece_sems)
        first_needed, then_needed = [starts[0], starts[2]], [starts[1]]
    else:
        starts = hidden_copies(place, pieces[:5], pieces[5], weights, piece_sems)
        first_needed, then_needed = starts[0:8:2] + [starts[8]], starts[1:8:2]
        for copy in first_needed + then_needed:
            copy.start()
    for copy in grad_copies:
        copy.start()
    for copy in normed_copies + first_needed:
        copy.wait()

    bias = weights[2 * width : 2 * width + 16, :].astype(F32)[2:3, :]
    chunk = 256
    chunks = [slice(first, first + chunk) for first in range(0, width, chunk)]

    def weight_sums(at):
        sums_up[:, at] = dot_columns(normed[...], grad_low[:, at]).astype(BF16)
        sums_down[at, :] = dot_columns(active[:, at], grad[...]).astype(BF16)

    for index, at in enumerate(chunks):
        hidden = dot(normed[...], weights[0:width, at]) + bias[:, at]
        if index == 0:
            for copy in grad_copies + then_needed:
                copy.wait()
        phi = 0.5 + 0.5 * lax.erf(hidden * (0.5**0.5))
        slope = phi + hidden * (jnp.exp(-0.5 * hidden * hidden) * ((2.0 * np.pi) ** -0.5))
        active[:, at] = (hidden * phi).astype(BF16)
        down_rows = weights[width + at.start : width + at.stop, :]
        grad_pre = dot_rows(grad[...], down_rows) * slope
        bias_sums[0:1, at] = jnp.sum(grad_pre, axis=0, keepdims=True)
        grad_low[:, at] = grad_pre.astype(BF16)
        if index:
            weight_sums(chunks[index - 1])
    weight_sums(chunks[-1])

    size = sums_up.shape[0] // 8
    copies = []
    for flip in range(4):
        quarter = lax.bitwise_xor(place[0], flip)
        for part in range(2):
            at = pl.ds(pl.multiple_of((2 * quarter + part) * size, 16), size)
            for matrix, source in enumerate((sums_up, sums_down)):
                if last:
                    target = whole_grads.at[part, flip, matrix]
                elif part == 0:
                    target = (keep_x if flip % 2 == 0 else send_x).at[flip // 2, matrix]
                else:
                    target = (keep_y if flip < 2 else send_y).at[flip % 2, matrix]
                sem = piece_sems.at[len(copies)]
                copies.append(pltpu.make_async_copy(source.at[at], target, sem))
    for copy in copies:
        copy.start()
    targets = ((out_mine, out_other), (back_mine, back_other))

    def out_copy(index, part, first, sem):
        target = targets[index][part]
        source = summed.at[index, pl.ds(part * half, target.shape[0]), pl.ds(first, chunk)]
        return pltpu.make_async_copy(source, target.at[:, pl.ds(first, chunk)], sem)

    def finish_chunk(step, carry):
        first = pl.multiple_of(step * chunk, chunk)
        at = pl.ds(first, chunk)
        back = dot_rows(grad_low[...], weights[at, :])
        out = dot(active[...], weights[width : 2 * width, at])
        for index, value in enumerate((out, back)):
            summed[index, :, at] = value.astype(BF16)
            for part in range(2):
                out_copy(index, part, first, out_sems.at[step, index, part]).start()
        return carry

    lax.fori_loop(0, len(chunks), finish_chunk, 0)
    for step in range(len(chunks)):
        for index in range(2):
            for part in range(2):
                out_copy(index, part, step * chunk, out_sems.at[step, index, part]).wait()
    for copy in copies:
        copy.wait()


def hidden_block(place, pieces, normed, grads, last):
    rows, width = normed[0].shape
    size = width // 8
    if last:
        grad_shapes = (kept((2, 4, 2, size, width), BF16),)
    else:
        grad_shapes = (kept((2, 2, size, width), BF16),) * 4
    return pl.pallas_call(
        functools.partial(hidden_kernel, last),
        out_shape=(
            *grad_shapes,
            shape((8, width), F32),
            kept((rows, width), BF16),
            kept((rows, width), BF16),
            kept((rows, width), BF16),
            kept((rows, width), BF16),
        ),
        in_specs=[SMEM] + [ANY] * 10,
        out_specs=(ANY,) * len(grad_shapes) + (VMEM,) + (ANY,) * 4,
        scratch_shapes=[
            pltpu.VMEM((2 * width + 16, width), BF16),
            pltpu.VMEM((2 * rows, width), BF16),
            pltpu.VMEM((2 * rows, width), BF16),
            pltpu.VMEM((2 * rows, width), BF16),
            pltpu.VMEM((2 * rows, width), BF16),
            pltpu.VMEM((width, width), BF16),
            pltpu.VMEM((width, width), BF16),
            pltpu.VMEM((2, 2 * rows, width), BF16),
            pltpu.SemaphoreType.DMA((16,)),
            pltpu.SemaphoreType.DMA((4,)),
            pltpu.SemaphoreType.DMA((width // 256, 2, 2)),
        ],
        compiler_params=params(44),
        cost_estimate=cost(rows * width * width * 24, rows * width * 24 + 8e6),
    )(place, *pieces, *from_hbm(*normed, *grads))


def first_sums_kernel(keep_x, keep_y, got_x, got_y, send_y, send_x, base):
    add = lambda u, v: u.astype(F32) + v.astype(F32)
    base[0] = add(keep_x[0], got_x[0])
    base[1] = add(keep_y[0], got_y[0])
    send_y[...] = add(keep_x[1], got_x[1]).astype(BF16)
    send_x[...] = add(keep_y[1], got_y[1]).astype(BF16)


def plane_sums_kernel(base, next_y, next_x, plane):
    plane[0] = (base[0] + next_y[...].astype(F32)).astype(BF16)
    plane[1] = (base[1] + next_x[...].astype(F32)).astype(BF16)


def depth_sums_kernel(core, local_far, far, near, keep, send):
    halves = []
    for half in range(2):
        first = jnp.where(core == 0, local_far[half], far[half])
        halves.append(first.astype(F32) + near[half].astype(F32))
    keep[...] = jnp.where(core == 0, halves[0], halves[1])
    send[...] = jnp.where(core == 0, halves[1], halves[0]).astype(BF16)


def pair_send_kernel(core, own, got, send):
    send[...] = jnp.where(core == 0, own[1], got[0])


def pair_sums_kernel(core, own, got, received, keep, send_x, send_y, send_xy):
    for flip, ref in enumerate((keep, send_x, send_y, send_xy)):
        half = jnp.where(core == 0, own[0, flip], got[1, flip])
        ref[...] = (half.astype(F32) + received[flip].astype(F32)).astype(BF16)


def half_split_kernel(core, both, keep, send):
    keep[...] = jnp.where(core == 0, both[0], both[1])
    send[...] = jnp.where(core == 0, both[1], both[0])


def last_sums_kernel(keep, received, *rest):
    total = rest[-1]
    total[0:1] = (keep[...] + received[...].astype(F32)).astype(BF16)
    both = rest[0][...].astype(F32)
    for ref in rest[1:-1]:
        both = both + ref[...].astype(F32)
    total[1:3] = both.astype(BF16)


def total_kernel(*refs):
    total = refs[0][...].astype(F32)
    for ref in refs[1:-1]:
        total = total + ref[...].astype(F32)
    refs[-1][...] = total.astype(refs[-1].dtype)


def sums_kernel(parts, place, *refs):
    ins = sum(count for _, count, _ in parts)
    in_refs, out_refs = refs[:ins], refs[ins:]
    for body, count, outs in parts:
        mine, in_refs = in_refs[:count], in_refs[count:]
        results, out_refs = out_refs[:outs], out_refs[outs:]
        with_core = (depth_sums_kernel, pair_send_kernel, pair_sums_kernel, half_split_kernel)
        lead = (place[1],) if body in with_core else ()
        rows = mine[0].shape[-2]
        chunk = 32 if rows % 32 == 0 else 16

        @pl.loop(0, rows // chunk)
        def _(step):
            at = pl.ds(pl.multiple_of(step * chunk, chunk), chunk)
            views = [
                ref.at[(slice(None),) * (len(ref.shape) - 2) + (at, slice(None))]
                for ref in (*mine, *results)
            ]
            body(*lead, *views)


def sums(place, *work):
    parts, args, out_shapes = [], [], []
    for body, arrays in work:
        like = arrays[0].shape
        if body is first_sums_kernel:
            outs = [shape(like[1:], BF16), shape(like[1:], BF16), shape(like, F32)]
        elif body is plane_sums_kernel:
            outs = [shape(like, BF16)]
        elif body is pair_send_kernel:
            outs = [shape(like[1:], BF16)]
        elif body is pair_sums_kernel:
            outs = [shape(like[2:], BF16)] * 4
        elif body is half_split_kernel:
            outs = [shape(like[1:], BF16)] * 2
        elif body is depth_sums_kernel:
            outs = [shape(like[1:], F32), shape(like[1:], BF16)]
        else:
            dims = (3, *like[1:]) if body is last_sums_kernel else like
            outs = [shape(dims, arrays[0].dtype if body is total_kernel else BF16)]
        parts.append((body, len(arrays), len(outs)))
        args += arrays
        out_shapes += outs
    moved = sum(4 * np.prod(o.shape) for o in out_shapes)
    results = pl.pallas_call(
        functools.partial(sums_kernel, tuple(parts)),
        out_shape=tuple(out_shapes),
        in_specs=[SMEM] + [VMEM] * len(args),
        out_specs=(VMEM,) * len(out_shapes),
        compiler_params=params(16),
        cost_estimate=cost(0, moved),
    )(place, *args)
    grouped = []
    for _, _, count in parts:
        grouped.append(tuple(results[:count]))
        results = results[count:]
    return grouped


def finish_kernel(side, place, *refs):
    parts, outs, wide, sems = refs[:4], refs[-6:-2], refs[-2], refs[-1]
    matrices, half = parts[0].shape[:2]
    grad_input, grad_mixer = outs[:2]
    part = place[1] if side == 0 else 1 - place[1]
    copies = []
    for flip in range(4):
        quarter = lax.bitwise_xor(place[0], flip)
        at = pl.ds(pl.multiple_of((2 * quarter + part) * half, 8), half)
        for matrix in range(matrices):
            source, sem = wide.at[flip, matrix], sems.at[flip, matrix]

            @pl.loop(0, half // 16)
            def _(step):
                rows = pl.ds(pl.multiple_of(step * 16, 16), 16)
                wide[flip, matrix, rows, :] = parts[flip][matrix, rows, :].astype(F32)

            if matrix:
                copies.append(pltpu.make_async_copy(source, outs[1 + matrix].at[at], sem))
                copies[-1].start()
                continue
            rows = pl.ds(pl.multiple_of(part * half, 8), half)
            copies.append(pltpu.make_async_copy(source, grad_mixer.at[rows], sem))

            @pl.when(quarter < 3)
            def _():
                pltpu.make_async_copy(source, grad_input.at[at], sem).start()

            @pl.when(quarter == 3)
            def _():
                copies[-1].start()

    for copy in copies:
        copy.wait()


def finish(place, parts, side, before):
    matrices, half, width = parts[0].shape
    extra = before or ()
    return pl.pallas_call(
        functools.partial(finish_kernel, side),
        out_shape=tuple(kept((count * half, width), F32) for count in (6, 2, 8, 8)),
        in_specs=[SMEM] + [VMEM] * 4 + [ANY] * len(extra),
        out_specs=(ANY,) * 4,
        scratch_shapes=[
            pltpu.VMEM((4, matrices, half, width), F32),
            pltpu.SemaphoreType.DMA((4, matrices)),
        ],
        input_output_aliases={5 + index: index for index in range(len(extra))},
        compiler_params=params(12),
        cost_estimate=cost(0, half * width * 72),
    )(place, *parts, *extra)


def local(
    tokens,
    visible_counts,
    norm_one_gain,
    norm_one_shift,
    input_weight,
    input_bias,
    mixer_weight,
    mixer_bias,
    norm_two_gain,
    norm_two_shift,
    up_weight,
    up_bias,
    down_weight,
    down_bias,
    output_grad,
    groups,
    outer,
):
    width = tokens.shape[1]
    rows = tokens.shape[0]
    cols = mixer_weight.shape[0]
    t = lax.axis_index("t")
    core = lax.axis_index("c")
    place = jnp.stack([2 * lax.axis_index("a") + lax.axis_index("b"), core, t]).astype(jnp.int32)
    one_row = lambda v: v.reshape(1, -1)

    swap = [(0, 1), (1, 0)]
    cross = [(0, 3), (1, 2), (2, 1), (3, 0)]
    to_near = [(z, (z + 1) % groups) for z in range(groups)] + [
        (groups + z, groups + (z + 2) % groups) for z in range(groups)
    ]
    to_far = [(groups + z, groups + (z + 3) % groups) for z in range(groups)]
    home_near = [(j, i) for i, j in to_near]
    home_far = [(j, i) for i, j in to_far]

    def spread(piece):
        return (
            piece,
            lax.ppermute(piece, "b", swap),
            lax.ppermute(piece, "a", swap),
            lax.ppermute(piece, ("a", "b"), cross),
        )

    def together(*groups):
        return lax.optimization_barrier(groups)

    def after(value, *others):
        return lax.optimization_barrier((value, *others))[0]

    def first_exchange(send_x, send_y, keep_x, keep_y):
        got_x = lax.ppermute(send_x, "b", swap)
        got_y = lax.ppermute(send_y, "a", swap)
        return keep_x, keep_y, got_x, got_y

    def second_exchange(send_y, send_x, base):
        return base, lax.ppermute(send_y, "a", swap), lax.ppermute(send_x, "b", swap)

    def direct(keep, send_x, send_y, send_xy):
        return (
            keep,
            lax.ppermute(send_x, "b", swap),
            lax.ppermute(send_y, "a", swap),
            lax.ppermute(send_xy, ("a", "b"), cross),
        )

    def over_outer(value):
        return lax.psum(value.astype(F32), "o").astype(BF16) if outer > 1 else value

    projection = input_weight.transpose(1, 2, 0).reshape(3 * cols, width)
    normed_one = norm_one(
        place,
        visible_counts,
        tokens,
        norm_one_gain,
        norm_one_shift,
    )
    piece_one, tail_one = pack_attention(
        place, projection, mixer_weight, after(input_bias, normed_one), one_row(up_bias)
    )
    depth_near_one = lax.ppermute(piece_one, ("c", "t"), to_near)
    normed_other = lax.ppermute(normed_one, "c", swap)
    piece_two = pack_hidden(place, up_weight, down_weight)
    depth_near_one, normed_other, piece_two = together(depth_near_one, normed_other, piece_two)
    near_one = spread(depth_near_one)
    far_projection = lax.ppermute(after(projection, depth_near_one), ("c", "t"), to_far)
    far_mixer = lax.ppermute(after(tail_one, depth_near_one), ("c", "t"), to_far)
    near_two = lax.ppermute(after(piece_two, far_mixer, *near_one), ("c", "t"), to_near)

    own_one = (projection, tail_one)
    far_one = (far_projection, far_mixer)
    saved, soft, part = attention(place, own_one, near_one, far_one, normed_other, None, BF16)
    saved, soft, part, near_two = together(saved, soft, part, near_two)
    grad_other = lax.ppermute(after(output_grad, part), "c", swap)
    part_received = lax.ppermute(part, "c", swap)
    near_x = lax.ppermute(near_two, "b", swap)
    near_y = lax.ppermute(near_two, "a", swap)
    far_up = lax.ppermute(after(up_weight, near_two), ("c", "t"), to_far)
    saved, soft, part = attention(
        place, own_one, near_one, far_one, normed_one, (saved, soft), F32
    )
    part, part_received, near_x, near_y, far_up, grad_other = together(
        part, part_received, near_x, near_y, far_up, grad_other
    )
    quarter = near_two.shape[0] // 2
    near_up = lax.ppermute(near_y[:quarter], "b", swap)
    near_down = lax.ppermute(near_x[quarter:], "a", swap)
    first_sum, normed_two = norm_two(
        tokens,
        part,
        part_received,
        one_row(mixer_bias),
        one_row(norm_two_gain),
        one_row(norm_two_shift),
    )
    normed_two, first_sum, near_up, near_down = together(
        normed_two, first_sum, near_up, near_down
    )
    normed_two_other = lax.ppermute(normed_two, "c", swap)
    far_down = lax.ppermute(after(down_weight, far_up), ("c", "t"), to_far)
    normed_two_both = (normed_two, normed_two_other)

    grad_both = (output_grad, grad_other)
    pieces = (near_two, near_x, near_y, near_up, near_down, depth_near_one)
    near_outs = hidden_block(place, pieces, normed_two_both, grad_both, False)
    near_outs, far_down = together(near_outs, far_down)
    *grads_near, bias_near, out_near, out_send, back_near, back_send = near_outs
    stage_near = first_exchange(*grads_near)
    back_near_received = lax.ppermute(back_send, "c", swap)
    out_near_received = lax.ppermute(out_send, "c", swap)
    shards = (up_weight, down_weight, tail_one, far_up, far_down, far_mixer)
    far_outs = hidden_block(place, shards, normed_two_both, grad_both, True)
    far_outs, stage_near, back_near_received, out_near_received = together(
        far_outs, stage_near, back_near_received, out_near_received
    )
    grads_far, bias_far, out_far, out_send, back_far_mine, back_send = far_outs

    got_far = lax.ppermute(grads_far, ("c", "t"), home_far)
    back_received = lax.ppermute(back_send, "c", swap)
    (stage_near,) = sums(place, (first_sums_kernel, stage_near))
    back_received = after(back_received, *stage_near)
    stage_near = second_exchange(*stage_near)
    grad_first_low, sums_two = norm_two_back(
        (back_near, back_near_received, back_far_mine, back_received),
        first_sum,
        one_row(norm_two_gain),
        output_grad,
    )
    first_other = lax.ppermute(grad_first_low, "c", swap)
    out_received = lax.ppermute(after(out_send, first_other), "c", swap)

    normed_both = (normed_one, normed_other)
    first_both = (grad_first_low, first_other)
    *grads_one_near, bias_one_near, back_near, back_send = attention_back(
        place, 1, None, near_one, normed_both, first_both, saved, soft
    )
    grads_one_near, back_near, back_send, stage_near, got_far, out_received = together(
        grads_one_near, back_near, back_send, stage_near, got_far, out_received
    )
    one_near = direct(*grads_one_near)
    (plane_near,), (send_far,) = sums(
        place, (plane_sums_kernel, stage_near), (pair_send_kernel, (grads_far, got_far))
    )
    depth_near = lax.ppermute(plane_near, ("c", "t"), home_near)
    received_far = lax.ppermute(send_far, "c", swap)
    back_near_send = after(back_send, received_far)
    grad_low_late = after(grad_first_low, plane_near)
    *grads_one_far, bias_one_far, back_far_mine, back_send = attention_back(
        place, 0, own_one, far_one, normed_both, (grad_low_late, first_other), saved, soft
    )
    grads_one_far, back_far_mine, back_send, one_near, received_far, depth_near = together(
        grads_one_far, back_far_mine, back_send, one_near, received_far, depth_near
    )
    back_near_received = lax.ppermute(back_near_send, "c", swap)

    one_far = direct(*grads_one_far)
    back_received = lax.ppermute(back_send, "c", swap)
    (one_near,), sums_far, (keep_two, send_two) = sums(
        place,
        (total_kernel, one_near),
        (pair_sums_kernel, (grads_far, got_far, received_far)),
        (half_split_kernel, (depth_near,)),
    )
    one_depth_near = lax.ppermute(one_near, ("c", "t"), home_near)
    received_two = lax.ppermute(send_two, "c", swap)
    grad_tokens, vectors = norm_one_back(
        groups,
        place,
        (back_near, back_near_received, back_far_mine, back_received),
        tokens,
        one_row(norm_one_gain),
        grad_first_low,
        sums_two,
        bias_near,
        bias_far,
        bias_one_near,
        bias_one_far,
    )
    vectors_core = lax.ppermute(vectors, "c", swap)
    vectors_core, one_far, received_two = together(vectors_core, one_far, received_two)
    (one_far,), (vectors,) = sums(
        place, (total_kernel, one_far), (total_kernel, (vectors, vectors_core))
    )
    one_depth_far = lax.ppermute(one_far, ("c", "t"), home_far)
    sums_far = direct(*sums_far)
    result = (
        first_sum
        + (out_near.astype(F32) + out_near_received.astype(F32))
        + (out_far.astype(F32) + out_received.astype(F32))
        + down_bias
    ).astype(BF16)
    one_depth_far, one_depth_near, result = together(one_depth_far, one_depth_near, result)
    ((keep_one, send_one),) = sums(
        place, (depth_sums_kernel, (one_far, one_depth_far, one_depth_near))
    )
    received_one = lax.ppermute(send_one, "c", swap)
    vectors_plane = spread(vectors)
    received_one, vectors_plane, sums_far = together(received_one, vectors_plane, sums_far)
    (parts,), (vectors,) = sums(
        place,
        (last_sums_kernel, (keep_one, received_one, *sums_far, keep_two, received_two)),
        (total_kernel, vectors_plane),
    )
    mine = spread(over_outer(parts))
    turns = [
        lax.ppermute(vectors, "t", [(z, (z + k) % groups) for z in range(groups)])
        for k in range(1, groups)
    ]
    vectors = sum(turns, vectors)
    if outer > 1:
        vectors = lax.psum(vectors, "o")
    grad_up_bias = lax.dynamic_slice_in_dim(vectors, 6 + t, 1)[0]
    grad_input_bias = lax.dynamic_slice_in_dim(vectors, 6 + groups + t, 1).reshape(-1, cols)[:2]
    rows_out = [vectors[index] for index in range(6)]
    mine, rows_out, grad_up_bias, grad_input_bias = together(
        mine, rows_out, grad_up_bias, grad_input_bias
    )
    other = tuple(lax.ppermute(part, "c", swap) for part in mine)
    half_done = finish(place, mine, 0, None)
    other, half_done = together(other, half_done)
    grad_input, grad_mixer, grad_up, grad_down = finish(place, other, 1, half_done)
    grad_input = grad_input.reshape(3, cols, width).transpose(2, 0, 1)
    return (
        result,
        grad_tokens,
        rows_out[0],
        rows_out[1],
        grad_input,
        grad_input_bias,
        grad_mixer,
        rows_out[4],
        rows_out[2],
        rows_out[3],
        grad_up,
        grad_up_bias,
        grad_down,
        rows_out[5],
    )


def solution(mesh):
    dp, groups = mesh.shape["dp"], mesh.shape["tensor"]
    outer = dp // 8
    split = jax.sharding.Mesh(
        mesh.devices.reshape(outer, 2, 2, 2, groups), ("o", "a", "b", "c", "t")
    )
    dp_axes = ("o", "a", "b", "c")
    all_axes = dp_axes + ("t",)
    in_specs = (
        P(all_axes, None),
        P(dp_axes),
        P(),
        P(),
        P(None, None, "t"),
        P(None, "t"),
        P("t", None),
        P(),
        P(),
        P(),
        P(None, "t"),
        P("t"),
        P("t", None),
        P(),
        P(all_axes, None),
    )
    out_specs = (
        P(all_axes, None),
        P(all_axes, None),
        P(),
        P(),
        P(None, None, "t"),
        P(None, "t"),
        P("t", None),
        P(),
        P(),
        P(),
        P(None, "t"),
        P("t"),
        P("t", None),
        P(),
    )
    return jax.shard_map(
        functools.partial(local, groups=groups, outer=outer),
        mesh=split,
        in_specs=in_specs,
        out_specs=out_specs,
        check_vma=False,
    )
```

```python
import functools

import jax
import jax.numpy as jnp
import numpy as np
from jax import lax
from jax.experimental import pallas as pl
from jax.experimental.pallas import tpu as pltpu
from jax.sharding import PartitionSpec as P

HD = 64
SLOTS = 80
LANES = 128
TILE_IMAGES = 4
MASKED = -1000000000.0
EPS = 1e-06
F32 = jnp.float32
BF16 = jnp.bfloat16

ANY = pl.BlockSpec(memory_space=pl.ANY)
SMEM = pl.BlockSpec(memory_space=pltpu.SMEM)
VMEM = pl.BlockSpec(memory_space=pltpu.VMEM)


def shape(dims, kind):
    return jax.ShapeDtypeStruct(tuple(dims), kind)


def kept(dims, kind):
    return pltpu.HBM(tuple(dims), kind)


def from_hbm(*arrays):
    return tuple(pltpu.with_memory_space_constraint(a, pltpu.HBM) for a in arrays)


def params(megabytes, grid_dims=0):
    semantics = ("arbitrary",) * grid_dims if grid_dims else None
    return pltpu.CompilerParams(
        vmem_limit_bytes=megabytes * 1024 * 1024, dimension_semantics=semantics
    )


def cost(flops, moved):
    return pl.CostEstimate(flops=int(flops), bytes_accessed=int(moved), transcendentals=0)


def dot(left, right):
    return lax.dot_general(left, right, (((1,), (0,)), ((), ())), preferred_element_type=F32)


def dot_rows(left, right):
    return lax.dot_general(left, right, (((1,), (1,)), ((), ())), preferred_element_type=F32)


def dot_columns(left, right):
    return lax.dot_general(left, right, (((0,), (0,)), ((), ())), preferred_element_type=F32)


def centred(rows):
    center = rows - jnp.mean(rows, axis=-1, keepdims=True)
    spread = jnp.mean(center * center, axis=-1, keepdims=True)
    return center, lax.rsqrt(spread + EPS)


def norm_back(rows, gain, grad):
    center, rstd = centred(rows)
    xhat = center * rstd
    e = grad * gain
    back = rstd * (
        e - jnp.mean(e, axis=-1, keepdims=True) - xhat * jnp.mean(e * xhat, axis=-1, keepdims=True)
    )
    return (
        back,
        jnp.sum(grad * xhat, axis=0, keepdims=True),
        jnp.sum(grad, axis=0, keepdims=True),
    )


def norm_one_kernel(images, chunk, place, counts, tokens, gain, shift, out):
    rows = tokens.shape[0]

    @pl.loop(0, rows // chunk)
    def _(step):
        at = pl.ds(pl.multiple_of(step * chunk, chunk), chunk)
        center, rstd = centred(tokens[at, :].astype(F32))
        out[at, :] = (
            center * rstd * gain[...].reshape(1, -1) + shift[...].reshape(1, -1)
        ).astype(BF16)

    extra = out.shape[0] - rows
    row = lax.broadcasted_iota(jnp.int32, (extra, out.shape[1]), 0)
    table = jnp.zeros((extra, out.shape[1]), F32)
    first = place[2] * images
    for image in range(images):
        table = jnp.where(row == image, counts[first + image].astype(F32), table)
    out[rows:, :] = table.astype(BF16)


def norm_one(place, counts, tokens, gain, shift):
    rows, width = tokens.shape
    images = rows // SLOTS
    return pl.pallas_call(
        functools.partial(norm_one_kernel, images, SLOTS),
        out_shape=shape((rows + 16, width), BF16),
        in_specs=[SMEM, SMEM, VMEM, VMEM, VMEM],
        out_specs=VMEM,
        compiler_params=params(16),
        cost_estimate=cost(rows * width * 10, rows * width * 4),
    )(place, counts, tokens, gain, shift)


def norm_two_kernel(tokens, mine, received, bias, gain, shift, first_sum, normed):
    total = tokens[...].astype(F32) + (mine[...] + received[...].astype(F32)) + bias[...]
    first_sum[...] = total
    center, rstd = centred(total)
    normed[...] = (center * rstd * gain[...] + shift[...]).astype(BF16)


def rows_spec(tile, width):
    return pl.BlockSpec((tile, width), lambda i: (i, 0))


def fixed_spec(*dims):
    return pl.BlockSpec(dims, lambda i: (0,) * len(dims))


def norm_two(tokens, mine, received, bias, gain, shift):
    rows, width = tokens.shape
    tile = 2 * SLOTS
    row = rows_spec(tile, width)
    vector = fixed_spec(1, width)
    return pl.pallas_call(
        norm_two_kernel,
        grid=(rows // tile,),
        out_shape=(kept((rows, width), F32), shape((rows, width), BF16)),
        in_specs=[row, row, row, vector, vector, vector],
        out_specs=(row, row),
        compiler_params=params(16, 1),
        cost_estimate=cost(rows * width * 12, rows * width * 14),
    )(*from_hbm(tokens), mine, received, bias, gain, shift)


def added(*refs):
    total = refs[0][...].astype(F32)
    for ref in refs[1:]:
        total = total + ref[...].astype(F32)
    return total


def norm_two_back_kernel(
    part0, part1, part2, part3, first_sum, gain, output_grad, low, sums
):
    grad = added(part0, part1, part2, part3)
    back, grad_gain, grad_shift = norm_back(first_sum[...], gain[...], grad)
    out_grad = output_grad[...].astype(F32)
    total = out_grad + back
    low[...] = total.astype(BF16)

    @pl.when(pl.program_id(0) == 0)
    def _():
        sums[...] = jnp.zeros_like(sums)

    sums[0:1, :] += grad_gain
    sums[1:2, :] += grad_shift
    sums[2:3, :] += jnp.sum(total, axis=0, keepdims=True)
    sums[3:4, :] += jnp.sum(out_grad, axis=0, keepdims=True)


def norm_two_back(parts, first_sum, gain, output_grad):
    rows, width = parts[0].shape
    tile = 2 * SLOTS
    row = rows_spec(tile, width)
    return pl.pallas_call(
        norm_two_back_kernel,
        grid=(rows // tile,),
        out_shape=(shape((rows, width), BF16), shape((8, width), F32)),
        in_specs=[row] * 5 + [fixed_spec(1, width), row],
        out_specs=(row, fixed_spec(8, width)),
        compiler_params=params(16, 1),
        cost_estimate=cost(rows * width * 25, rows * width * 18),
    )(*parts, *from_hbm(first_sum), gain, *from_hbm(output_grad))


def norm_one_back_kernel(
    groups,
    place,
    part0,
    part1,
    part2,
    part3,
    tokens,
    gain,
    grad_first,
    sums_two,
    bias_near,
    bias_far,
    input_near,
    input_far,
    grad_tokens,
    vectors,
):
    grad = added(part0, part1, part2, part3)
    back, grad_gain, grad_shift = norm_back(tokens[...].astype(F32), gain[...], grad)
    grad_tokens[...] = grad_first[...].astype(F32) + back

    @pl.when(pl.program_id(0) == 0)
    def _():
        near = lax.rem(place[2] - 1 - place[1] + groups, groups)
        far = lax.rem(place[2] - 3 * place[1] + groups, groups)
        row = lax.broadcasted_iota(jnp.int32, vectors.shape, 0)
        table = jnp.zeros(vectors.shape, F32)
        for index in range(4):
            table = jnp.where(row == 2 + index, sums_two[index : index + 1, :], table)
        table = jnp.where(row == 6 + near, bias_near[0:1, :], table)
        vectors[...] = jnp.where(row == 6 + far, bias_far[0:1, :], table)
        columns = input_near.shape[1]
        few = lax.broadcasted_iota(jnp.int32, (vectors.shape[0], columns), 0)
        for index in range(2):
            table = jnp.where(
                few == 6 + groups + near, input_near[index : index + 1, :], 0.0
            ) + jnp.where(few == 6 + groups + far, input_far[index : index + 1, :], 0.0)
            vectors[:, index * columns : (index + 1) * columns] += table

    vectors[0:1, :] += grad_gain
    vectors[1:2, :] += grad_shift


def norm_one_back(groups, place, parts, tokens, gain, grad_first, *small):
    rows, width = parts[0].shape
    tile = 2 * SLOTS
    row = rows_spec(tile, width)
    return pl.pallas_call(
        functools.partial(norm_one_back_kernel, groups),
        grid=(rows // tile,),
        out_shape=(kept((rows, width), F32), shape((16, width), F32)),
        in_specs=[SMEM] + [row] * 5 + [fixed_spec(1, width), row]
        + [fixed_spec(*array.shape) for array in small],
        out_specs=(row, fixed_spec(16, width)),
        compiler_params=params(16, 1),
        cost_estimate=cost(rows * width * 25, rows * width * 16),
    )(place, *parts, *from_hbm(tokens), gain, *from_hbm(grad_first), *small)


def pack_attention_kernel(place, projection, mixer, bias, up_bias, out, tail, sem, tail_sem):
    quarter = place[0]
    tail_copy = pltpu.make_async_copy(mixer, tail.at[pl.ds(0, mixer.shape[0])], tail_sem)
    tail_copy.start()
    size = out.shape[0] - 16
    feature_rows = projection.shape[0]
    first = pl.multiple_of(quarter * size, 16)
    from_projection = quarter * size < feature_rows

    @pl.when(from_projection)
    def _():
        copy = pltpu.make_async_copy(
            projection.at[pl.ds(first, size)], out.at[pl.ds(0, size)], sem
        )
        copy.start()
        copy.wait()

    @pl.when(jnp.logical_not(from_projection))
    def _():
        copy = pltpu.make_async_copy(mixer, out.at[pl.ds(0, size)], sem)
        copy.start()
        copy.wait()

    columns = bias.shape[1]
    row = lax.broadcasted_iota(jnp.int32, (16, columns), 0)
    both = bias[...].astype(F32)
    rows = jnp.where(row == 0, both[0:1, :], jnp.where(row == 1, both[1:2, :], 0.0))
    row_all = lax.broadcasted_iota(jnp.int32, (16, out.shape[1]), 0)
    out[size:, :] = jnp.where(row_all == 2, up_bias[...].astype(F32), 0.0).astype(BF16)
    row_two = jnp.where(row == 2, up_bias[:, 0:columns].astype(F32), rows)
    out[size:, 0:columns] = row_two.astype(BF16)
    tail[size:, :] = out[size:, :]
    tail_copy.wait()


def pack_attention(place, projection, mixer, bias, up_bias):
    size, width = mixer.shape
    return pl.pallas_call(
        pack_attention_kernel,
        out_shape=(shape((size + 16, width), BF16),) * 2,
        in_specs=[SMEM, ANY, ANY, VMEM, VMEM],
        out_specs=(VMEM, VMEM),
        scratch_shapes=[pltpu.SemaphoreType.DMA(()), pltpu.SemaphoreType.DMA(())],
        compiler_params=params(16),
        cost_estimate=cost(0, 2 * size * width),
    )(place, *from_hbm(projection, mixer), bias, up_bias)


def pack_hidden_kernel(place, up, down, out, sems):
    size = out.shape[0] // 2
    first = pl.multiple_of(place[0] * size, 16)
    copies = [
        pltpu.make_async_copy(
            source.at[pl.ds(first, size)], out.at[pl.ds(index * size, size)], sems.at[index]
        )
        for index, source in enumerate((up, down))
    ]
    run_copies(copies)


def pack_hidden(place, up, down):
    size, width = up.shape[0] // 4, up.shape[1]
    return pl.pallas_call(
        pack_hidden_kernel,
        out_shape=shape((2 * size, width), BF16),
        in_specs=[SMEM, ANY, ANY],
        out_specs=VMEM,
        scratch_shapes=[pltpu.SemaphoreType.DMA((2,))],
        compiler_params=params(16),
        cost_estimate=cost(0, 4 * size * width),
    )(place, *from_hbm(up, down))


def run_copies(copies):
    for copy in copies:
        copy.start()
    for copy in copies:
        copy.wait()


def make_copies(copies, sems):
    return [
        pltpu.make_async_copy(source, to, sems.at[index])
        for index, (source, to) in enumerate(copies)
    ]


def piece_copies(place, pieces, target, sems):
    size = pieces[0].shape[0] - 16
    copies = []
    for flip, piece in enumerate(pieces):
        to = pl.multiple_of(lax.bitwise_xor(place[0], flip) * size, 16)
        copies.append((piece.at[pl.ds(0, size)], target.at[pl.ds(to, size)]))
    copies.append((pieces[0].at[pl.ds(size, 16)], target.at[pl.ds(4 * size, 16)]))
    return make_copies(copies, sems)


def hidden_copies(place, pieces, bias_piece, target, sems):
    size = pieces[0].shape[0] // 2
    copies = []
    for flip in range(4):
        quarter = lax.bitwise_xor(place[0], flip)
        for matrix in range(2):
            to = pl.multiple_of((4 * matrix + quarter) * size, 16)
            source = pieces[3 + matrix] if flip == 3 else pieces[flip].at[pl.ds(matrix * size, size)]
            copies.append((source, target.at[pl.ds(to, size)]))
    first = bias_piece.shape[0] - 16
    copies.append((bias_piece.at[pl.ds(first, 16)], target.at[pl.ds(8 * size, 16)]))
    return make_copies(copies, sems)


def head_lanes(rows, width):
    return lax.broadcasted_iota(jnp.int32, (rows, width), 1) // HD


def spread_heads(block, lanes, heads):
    gap = jnp.zeros((LANES - SLOTS, block.shape[1]), block.dtype)
    parts = []
    for head in range(heads):
        parts.append(jnp.where(lanes == head, block, jnp.zeros_like(block)))
        parts.append(gap)
    return jnp.concatenate(parts, axis=0)


def gather_heads(product, lanes, heads):
    total = product[0:SLOTS]
    for head in range(1, heads):
        total = jnp.where(lanes == head, product[head * LANES : head * LANES + SLOTS], total)
    return total


def start_on_core(place, own, far, cut, sems):
    copies = [make_copies(cut(parts), sems) for parts in (own, far)]
    for core, some in enumerate(copies):

        @pl.when(place[1] == core)
        def _():
            for copy in some:
                copy.start()

    return copies[0]


def start_far(place, own, far, target, sems):
    def cut(parts):
        size = parts[0].shape[0]
        return [
            (parts[0], target.at[pl.ds(0, size)]),
            (parts[1], target.at[pl.ds(size, parts[1].shape[0])]),
        ]

    return start_on_core(place, own, far, cut, sems)


def start_matrices(place, own, far, target, sems):
    def cut(parts):
        size = parts[0].shape[0]
        bias = parts[1].at[pl.ds(parts[1].shape[0] - 16, 16)]
        return [(parts[0], target.at[pl.ds(0, size)]), (bias, target.at[pl.ds(size, 16)])]

    return start_on_core(place, own, far, cut, sems)


def attention_kernel(
    heads,
    place,
    projection,
    tail,
    near0,
    near1,
    near2,
    near3,
    far0,
    far1,
    normed,
    counts,
    *rest,
):
    saved, soft, part, weights, table, sems = rest[-6:]

    @pl.when(pl.program_id(0) == 0)
    def _():
        copies = piece_copies(place, (near0, near1, near2, near3), weights.at[1], sems)
        for copy in copies:
            copy.start()
        far_sems = sems.at[pl.ds(8, 8)]
        copies += start_far(place, (projection, tail), (far0, far1), weights.at[0], far_sems)
        for copy in copies:
            copy.wait()

    cols = heads * HD
    visible_rows = counts[:, 0:LANES].astype(F32)
    for image in range(visible_rows.shape[0]):
        table[image, :, :] = visible_rows[image : image + 1, :]
    rows = normed[...]
    for slot in range(2):
        for index in range(3):
            value = dot_rows(rows, weights[slot, index * cols : (index + 1) * cols, :])
            if index != 1:
                bias_row = 0 if index == 0 else 1
                bias = weights[slot, 4 * cols : 4 * cols + 16, 0:cols].astype(F32)
                value = value + bias[bias_row : bias_row + 1, :]
            saved[4 * slot + index, :, :] = value.astype(BF16)

    lanes = head_lanes(SLOTS, cols)
    key_index = lax.broadcasted_iota(jnp.int32, (SLOTS, LANES), 1).astype(F32)
    first = pl.program_id(0) * TILE_IMAGES

    def one_image(image, carry):
        at = pl.ds(pl.multiple_of(image * SLOTS, 16), SLOTS)
        visible = key_index < table[first + image]
        for slot in range(2):
            queries = saved[4 * slot, at, :]
            keys = spread_heads(saved[4 * slot + 1, at, :], lanes, heads)
            values = spread_heads(saved[4 * slot + 2, at, :], lanes, heads)
            scores = dot_rows(queries, keys) * (HD**-0.5)
            lows = []
            for head in range(heads):
                one = jnp.where(visible, scores[:, head * LANES : (head + 1) * LANES], MASKED)
                exponent = jnp.exp(one - jnp.max(one, axis=-1, keepdims=True))
                total = jnp.sum(exponent, axis=-1, keepdims=True)
                lows.append((exponent / total).astype(BF16))
            low = jnp.concatenate(lows, axis=1)
            soft[at, slot * heads * LANES : (slot + 1) * heads * LANES] = low
            saved[4 * slot + 3, at, :] = dot(low, values).astype(BF16)
        return carry

    lax.fori_loop(0, TILE_IMAGES, one_image, 0, unroll=True)
    total = dot(saved[3, :, :], weights[0, 3 * cols : 4 * cols, :])
    total = total + dot(saved[7, :, :], weights[1, 3 * cols : 4 * cols, :])
    part[...] = total.astype(part.dtype)


def attention(place, own, near, far, normed, before, kind):
    projection, tail = own
    cols, width = projection.shape[0] // 3, projection.shape[1]
    heads = cols // HD
    rows = normed.shape[0] - 16
    tile = TILE_IMAGES * SLOTS
    tiles = rows // tile
    base = tiles if before is None else 0
    extra = () if before is None else from_hbm(*before)
    args = (place, projection, tail, *near, *far, normed, normed, *extra)
    return pl.pallas_call(
        functools.partial(attention_kernel, heads),
        grid=(tiles,),
        out_shape=(
            kept((8, 2 * rows, cols), BF16),
            kept((2 * rows, 2 * heads * LANES), BF16),
            shape((rows, width), kind),
        ),
        in_specs=[SMEM]
        + [ANY] * 8
        + [
            pl.BlockSpec((tile, width), lambda i: (i, 0)),
            pl.BlockSpec((16, width), lambda i: (rows // 16, 0)),
        ]
        + [ANY] * len(extra),
        out_specs=(
            pl.BlockSpec((8, tile, cols), lambda i: (0, base + i, 0)),
            pl.BlockSpec((tile, 2 * heads * LANES), lambda i: (base + i, 0)),
            pl.BlockSpec((tile, width), lambda i: (i, 0)),
        ),
        scratch_shapes=[
            pltpu.VMEM((2, 4 * cols + 16, width), BF16),
            pltpu.VMEM((16, 1, LANES), F32),
            pltpu.SemaphoreType.DMA((16,)),
        ],
        input_output_aliases={11: 0, 12: 1} if extra else {},
        compiler_params=params(20, 1),
        cost_estimate=cost(rows * width * cols * 16 + rows * 400000, rows * width * 10 + 5e6),
    )(*args)


def attention_back_kernel(heads, far, place, *rest):
    count = 4
    pieces, rest = rest[:count], rest[count:]
    normed_mine, normed_other, grad_mine, grad_other, saved, soft = rest[:6]
    rest = rest[6:]
    keep, send_x, send_y, send_xy, bias_sums = rest[:5]
    rest = rest[5:]
    back_mine, back_other, weights, sums, grads, sems = rest
    step = pl.program_id(0)
    steps = pl.num_programs(0)
    cols = heads * HD
    mine = step < steps // 2

    @pl.when(step == 0)
    def _():
        if far:
            copies = start_far(place, pieces[:2], pieces[2:], weights, sems)
        else:
            copies = piece_copies(place, pieces, weights, sems)
            for copy in copies:
                copy.start()
        for copy in copies:
            copy.wait()
        sums[...] = jnp.zeros_like(sums)
        bias_sums[...] = jnp.zeros_like(bias_sums)

    normed = jnp.where(mine, normed_mine[...], normed_other[...])
    grad = jnp.where(mine, grad_mine[...], grad_other[...])
    grads[3, :, :] = dot_rows(grad, weights[3 * cols : 4 * cols, :]).astype(BF16)
    lanes = head_lanes(SLOTS, cols)

    def one_image(image, carry):
        at = pl.ds(pl.multiple_of(image * SLOTS, 16), SLOTS)
        queries = saved[0, at, :]
        keys = spread_heads(saved[1, at, :], lanes, heads)
        values = spread_heads(saved[2, at, :], lanes, heads)
        grad_mixed = grads[3, at, :]
        low = soft[at, :]
        grad_soft = dot_rows(grad_mixed, values)
        lows = []
        for head in range(heads):
            one = low[:, head * LANES : (head + 1) * LANES].astype(F32)
            grad_one = grad_soft[:, head * LANES : (head + 1) * LANES]
            inner = jnp.sum(grad_one * one, axis=-1, keepdims=True)
            lows.append((one * (grad_one - inner) * (HD**-0.5)).astype(BF16))
        grad_scores = jnp.concatenate(lows, axis=1)
        grad_queries = dot(grad_scores, keys)
        grad_values = gather_heads(dot_columns(low, grad_mixed), lanes, heads)
        grad_keys = gather_heads(dot_columns(grad_scores, queries), lanes, heads)
        bias_sums[0:1, :] += jnp.sum(grad_queries, axis=0, keepdims=True)
        bias_sums[1:2, :] += jnp.sum(grad_values, axis=0, keepdims=True)
        grads[0, at, :] = grad_queries.astype(BF16)
        grads[1, at, :] = grad_keys.astype(BF16)
        grads[2, at, :] = grad_values.astype(BF16)
        return carry

    lax.fori_loop(0, TILE_IMAGES, one_image, 0, unroll=True)
    back = None
    for index in range(3):
        at = slice(index * cols, (index + 1) * cols)
        value = grads[index, :, :]
        term = dot(value, weights[at, :])
        back = term if back is None else back + term
        sums[at, :] += dot_columns(value, normed)
    sums[3 * cols : 4 * cols, :] += dot_columns(saved[3, :, :], grad)

    @pl.when(mine)
    def _():
        back_mine[...] = back.astype(BF16)

    @pl.when(jnp.logical_not(mine))
    def _():
        back_other[...] = back.astype(BF16)

    @pl.when(step == steps - 1)
    def _():
        size = keep.shape[2]
        for flip, ref in enumerate((keep, send_x, send_y, send_xy)):
            quarter = lax.bitwise_xor(place[0], flip)
            for half in range(2):
                at = pl.ds(pl.multiple_of((2 * quarter + half) * size, 16), size)
                ref[half, 0, :, :] = sums[at, :].astype(BF16)


def half_spec(tile, width, tiles, second):
    if second:
        return pl.BlockSpec((tile, width), lambda i: (jnp.maximum(i - tiles, 0), 0))
    return pl.BlockSpec((tile, width), lambda i: (jnp.minimum(i, tiles - 1), 0))


def attention_back(place, slot, own, pieces, normed, grads, saved, soft):
    rows, width = grads[0].shape
    cols = saved.shape[2]
    heads = cols // HD
    tile = TILE_IMAGES * SLOTS
    tiles = rows // tile
    far = own is not None
    mine, other = half_spec(tile, width, tiles, False), half_spec(tile, width, tiles, True)
    dims = (2, 1, cols // 2, width)
    weights = (*own, *pieces) if far else pieces
    return pl.pallas_call(
        functools.partial(attention_back_kernel, heads, far),
        grid=(2 * tiles,),
        out_shape=(
            *(shape(dims, BF16),) * 4,
            shape((8, cols), F32),
            shape((rows, width), BF16),
            shape((rows, width), BF16),
        ),
        in_specs=[SMEM]
        + [ANY] * 4
        + [
            mine,
            other,
            mine,
            other,
            pl.BlockSpec((4, tile, cols), lambda i: (slot, i, 0)),
            pl.BlockSpec((tile, heads * LANES), lambda i: (i, slot)),
        ],
        out_specs=(*(fixed_spec(*dims),) * 4, fixed_spec(8, cols), mine, other),
        scratch_shapes=[
            pltpu.VMEM((4 * cols + 16, width), BF16),
            pltpu.VMEM((4 * cols, width), F32),
            pltpu.VMEM((4, tile, cols), BF16),
            pltpu.SemaphoreType.DMA((16,)),
        ],
        compiler_params=params(24, 1),
        cost_estimate=cost(rows * width * cols * 30 + rows * 6e5, rows * width * 20 + 4e6),
    )(place, *weights, *normed, *grads, *from_hbm(saved, soft))


def hidden_kernel(last, place, *rest):
    count = 4 if last else 6
    pieces, rest = rest[:count], rest[count:]
    normed_parts, grad_parts, rest = rest[:2], rest[2:4], rest[4:]
    if last:
        whole_grads, rest = rest[0], rest[1:]
    else:
        (send_x, send_y, keep_x, keep_y), rest = rest[:4], rest[4:]
    bias_sums, out_mine, out_other, back_mine, back_other = rest[:5]
    rest = rest[5:]
    weights, normed, grad, active, grad_low, sums_up, sums_down, summed = rest[:8]
    piece_sems, sems, out_sems = rest[8:]
    rows, width = normed.shape
    half = rows // 2

    def load(first, parts, target):
        return [
            pltpu.make_async_copy(part, target.at[pl.ds(index * half, half)], sems.at[first + index])
            for index, part in enumerate(parts)
        ]

    normed_copies, grad_copies = load(0, normed_parts, normed), load(2, grad_parts, grad)
    for copy in normed_copies:
        copy.start()
    if last:
        first_needed = start_matrices(place, pieces[:2], pieces[2:], weights, piece_sems)
        then_needed = []
    else:
        starts = hidden_copies(place, pieces[:5], pieces[5], weights, piece_sems)
        first_needed, then_needed = starts[0:8:2] + [starts[8]], starts[1:8:2]
        for copy in first_needed + then_needed:
            copy.start()
    for copy in grad_copies:
        copy.start()
    for copy in normed_copies + first_needed:
        copy.wait()

    bias = weights[2 * width : 2 * width + 16, :].astype(F32)[2:3, :]
    chunk = 256
    chunks = [slice(first, first + chunk) for first in range(0, width, chunk)]

    def weight_sums(at):
        sums_up[:, at] = dot_columns(normed[...], grad_low[:, at]).astype(BF16)
        sums_down[at, :] = dot_columns(active[:, at], grad[...]).astype(BF16)

    for index, at in enumerate(chunks):
        hidden = dot(normed[...], weights[0:width, at]) + bias[:, at]
        if index == 0:
            for copy in grad_copies + then_needed:
                copy.wait()
        phi = 0.5 + 0.5 * lax.erf(hidden * (0.5**0.5))
        slope = phi + hidden * (jnp.exp(-0.5 * hidden * hidden) * ((2.0 * np.pi) ** -0.5))
        active[:, at] = (hidden * phi).astype(BF16)
        down_rows = weights[width + at.start : width + at.stop, :]
        grad_pre = dot_rows(grad[...], down_rows) * slope
        bias_sums[0:1, at] = jnp.sum(grad_pre, axis=0, keepdims=True)
        grad_low[:, at] = grad_pre.astype(BF16)
        if index:
            weight_sums(chunks[index - 1])
    weight_sums(chunks[-1])

    size = sums_up.shape[0] // 8
    copies = []
    for flip in range(4):
        quarter = lax.bitwise_xor(place[0], flip)
        for part in range(2):
            at = pl.ds(pl.multiple_of((2 * quarter + part) * size, 16), size)
            for matrix, source in enumerate((sums_up, sums_down)):
                if last:
                    target = whole_grads.at[part, flip, matrix]
                elif part == 0:
                    target = (keep_x if flip % 2 == 0 else send_x).at[flip // 2, matrix]
                else:
                    target = (keep_y if flip < 2 else send_y).at[flip % 2, matrix]
                sem = piece_sems.at[len(copies)]
                copies.append(pltpu.make_async_copy(source.at[at], target, sem))
    for copy in copies:
        copy.start()
    targets = ((out_mine, out_other), (back_mine, back_other))

    def out_copy(index, part, first, sem):
        target = targets[index][part]
        source = summed.at[index, pl.ds(part * half, target.shape[0]), pl.ds(first, chunk)]
        return pltpu.make_async_copy(source, target.at[:, pl.ds(first, chunk)], sem)

    def finish_chunk(step, carry):
        first = pl.multiple_of(step * chunk, chunk)
        at = pl.ds(first, chunk)
        back = dot_rows(grad_low[...], weights[at, :])
        out = dot(active[...], weights[width : 2 * width, at])
        for index, value in enumerate((out, back)):
            summed[index, :, at] = value.astype(BF16)
            for part in range(2):
                out_copy(index, part, first, out_sems.at[step, index, part]).start()
        return carry

    lax.fori_loop(0, len(chunks), finish_chunk, 0)
    for step in range(len(chunks)):
        for index in range(2):
            for part in range(2):
                out_copy(index, part, step * chunk, out_sems.at[step, index, part]).wait()
    for copy in copies:
        copy.wait()


def hidden_block(place, pieces, normed, grads, last):
    rows, width = normed[0].shape
    size = width // 8
    if last:
        grad_shapes = (kept((2, 4, 2, size, width), BF16),)
    else:
        grad_shapes = (kept((2, 2, size, width), BF16),) * 4
    return pl.pallas_call(
        functools.partial(hidden_kernel, last),
        out_shape=(
            *grad_shapes,
            shape((8, width), F32),
            kept((rows, width), BF16),
            kept((rows, width), BF16),
            kept((rows, width), BF16),
            kept((rows, width), BF16),
        ),
        in_specs=[SMEM] + [ANY] * (len(pieces) + 4),
        out_specs=(ANY,) * len(grad_shapes) + (VMEM,) + (ANY,) * 4,
        scratch_shapes=[
            pltpu.VMEM((2 * width + 16, width), BF16),
            pltpu.VMEM((2 * rows, width), BF16),
            pltpu.VMEM((2 * rows, width), BF16),
            pltpu.VMEM((2 * rows, width), BF16),
            pltpu.VMEM((2 * rows, width), BF16),
            pltpu.VMEM((width, width), BF16),
            pltpu.VMEM((width, width), BF16),
            pltpu.VMEM((2, 2 * rows, width), BF16),
            pltpu.SemaphoreType.DMA((16,)),
            pltpu.SemaphoreType.DMA((4,)),
            pltpu.SemaphoreType.DMA((width // 256, 2, 2)),
        ],
        compiler_params=params(44),
        cost_estimate=cost(rows * width * width * 24, rows * width * 24 + 8e6),
    )(place, *pieces, *from_hbm(*normed, *grads))


def first_sums_kernel(keep_x, keep_y, got_x, got_y, send_y, send_x, base):
    add = lambda u, v: u.astype(F32) + v.astype(F32)
    base[0] = add(keep_x[0], got_x[0])
    base[1] = add(keep_y[0], got_y[0])
    send_y[...] = add(keep_x[1], got_x[1]).astype(BF16)
    send_x[...] = add(keep_y[1], got_y[1]).astype(BF16)


def plane_sums_kernel(base, next_y, next_x, plane):
    plane[0] = (base[0] + next_y[...].astype(F32)).astype(BF16)
    plane[1] = (base[1] + next_x[...].astype(F32)).astype(BF16)


def depth_sums_kernel(core, local_far, far, near, keep, send):
    halves = []
    for half in range(2):
        first = jnp.where(core == 0, local_far[half], far[half])
        halves.append(first.astype(F32) + near[half].astype(F32))
    keep[...] = jnp.where(core == 0, halves[0], halves[1])
    send[...] = jnp.where(core == 0, halves[1], halves[0]).astype(BF16)


def pair_send_kernel(core, own, got, send):
    send[...] = jnp.where(core == 0, own[1], got[0])


def pair_sums_kernel(core, own, got, received, keep, send_x, send_y, send_xy):
    for flip, ref in enumerate((keep, send_x, send_y, send_xy)):
        half = jnp.where(core == 0, own[0, flip], got[1, flip])
        ref[...] = (half.astype(F32) + received[flip].astype(F32)).astype(BF16)


def half_split_kernel(core, both, keep, send):
    keep[...] = jnp.where(core == 0, both[0], both[1])
    send[...] = jnp.where(core == 0, both[1], both[0])


def last_sums_kernel(keep, received, *rest):
    total = rest[-1]
    total[0:1] = (keep[...] + received[...].astype(F32)).astype(BF16)
    both = rest[0][...].astype(F32)
    for ref in rest[1:-1]:
        both = both + ref[...].astype(F32)
    total[1:3] = both.astype(BF16)


def total_kernel(*refs):
    total = refs[0][...].astype(F32)
    for ref in refs[1:-1]:
        total = total + ref[...].astype(F32)
    refs[-1][...] = total.astype(refs[-1].dtype)


def sums_kernel(parts, place, *refs):
    ins = sum(count for _, count, _ in parts)
    in_refs, out_refs = refs[:ins], refs[ins:]
    for body, count, outs in parts:
        mine, in_refs = in_refs[:count], in_refs[count:]
        results, out_refs = out_refs[:outs], out_refs[outs:]
        with_core = (depth_sums_kernel, pair_send_kernel, pair_sums_kernel, half_split_kernel)
        lead = (place[1],) if body in with_core else ()
        rows = mine[0].shape[-2]
        chunk = 32 if rows % 32 == 0 else 16

        @pl.loop(0, rows // chunk)
        def _(step):
            at = pl.ds(pl.multiple_of(step * chunk, chunk), chunk)
            views = [
                ref.at[(slice(None),) * (len(ref.shape) - 2) + (at, slice(None))]
                for ref in (*mine, *results)
            ]
            body(*lead, *views)


def sums(place, *work):
    parts, args, out_shapes = [], [], []
    for body, arrays in work:
        like = arrays[0].shape
        if body is first_sums_kernel:
            outs = [shape(like[1:], BF16), shape(like[1:], BF16), shape(like, F32)]
        elif body is plane_sums_kernel:
            outs = [shape(like, BF16)]
        elif body is pair_send_kernel:
            outs = [shape(like[1:], BF16)]
        elif body is pair_sums_kernel:
            outs = [shape(like[2:], BF16)] * 4
        elif body is half_split_kernel:
            outs = [shape(like[1:], BF16)] * 2
        elif body is depth_sums_kernel:
            outs = [shape(like[1:], F32), shape(like[1:], BF16)]
        else:
            dims = (3, *like[1:]) if body is last_sums_kernel else like
            outs = [shape(dims, arrays[0].dtype if body is total_kernel else BF16)]
        parts.append((body, len(arrays), len(outs)))
        args += arrays
        out_shapes += outs
    moved = sum(4 * np.prod(o.shape) for o in out_shapes)
    results = pl.pallas_call(
        functools.partial(sums_kernel, tuple(parts)),
        out_shape=tuple(out_shapes),
        in_specs=[SMEM] + [VMEM] * len(args),
        out_specs=(VMEM,) * len(out_shapes),
        compiler_params=params(16),
        cost_estimate=cost(0, moved),
    )(place, *args)
    grouped = []
    for _, _, count in parts:
        grouped.append(tuple(results[:count]))
        results = results[count:]
    return grouped


def finish_kernel(side, place, *refs):
    parts, outs, wide, sems = refs[:4], refs[-6:-2], refs[-2], refs[-1]
    matrices, half = parts[0].shape[:2]
    grad_input, grad_mixer = outs[:2]
    part = place[1] if side == 0 else 1 - place[1]
    copies = []
    for flip in range(4):
        quarter = lax.bitwise_xor(place[0], flip)
        at = pl.ds(pl.multiple_of((2 * quarter + part) * half, 8), half)
        for matrix in range(matrices):
            source, sem = wide.at[flip, matrix], sems.at[flip, matrix]

            @pl.loop(0, half // 16)
            def _(step):
                rows = pl.ds(pl.multiple_of(step * 16, 16), 16)
                wide[flip, matrix, rows, :] = parts[flip][matrix, rows, :].astype(F32)

            if matrix:
                copies.append(pltpu.make_async_copy(source, outs[1 + matrix].at[at], sem))
                copies[-1].start()
                continue
            rows = pl.ds(pl.multiple_of(part * half, 8), half)
            copies.append(pltpu.make_async_copy(source, grad_mixer.at[rows], sem))

            @pl.when(quarter < 3)
            def _():
                pltpu.make_async_copy(source, grad_input.at[at], sem).start()

            @pl.when(quarter == 3)
            def _():
                copies[-1].start()

    for copy in copies:
        copy.wait()


def finish(place, parts, side, before):
    matrices, half, width = parts[0].shape
    extra = before or ()
    return pl.pallas_call(
        functools.partial(finish_kernel, side),
        out_shape=tuple(kept((count * half, width), F32) for count in (6, 2, 8, 8)),
        in_specs=[SMEM] + [VMEM] * 4 + [ANY] * len(extra),
        out_specs=(ANY,) * 4,
        scratch_shapes=[
            pltpu.VMEM((4, matrices, half, width), F32),
            pltpu.SemaphoreType.DMA((4, matrices)),
        ],
        input_output_aliases={5 + index: index for index in range(len(extra))},
        compiler_params=params(12),
        cost_estimate=cost(0, half * width * 72),
    )(place, *parts, *extra)


def local(
    tokens,
    visible_counts,
    norm_one_gain,
    norm_one_shift,
    input_weight,
    input_bias,
    mixer_weight,
    mixer_bias,
    norm_two_gain,
    norm_two_shift,
    up_weight,
    up_bias,
    down_weight,
    down_bias,
    output_grad,
    groups,
    outer,
):
    width = tokens.shape[1]
    rows = tokens.shape[0]
    cols = mixer_weight.shape[0]
    t = lax.axis_index("t")
    core = lax.axis_index("c")
    place = jnp.stack([2 * lax.axis_index("a") + lax.axis_index("b"), core, t]).astype(jnp.int32)
    one_row = lambda v: v.reshape(1, -1)

    swap = [(0, 1), (1, 0)]
    cross = [(0, 3), (1, 2), (2, 1), (3, 0)]
    to_near = [(z, (z + 1) % groups) for z in range(groups)] + [
        (groups + z, groups + (z + 2) % groups) for z in range(groups)
    ]
    to_far = [(groups + z, groups + (z + 3) % groups) for z in range(groups)]
    home_near = [(j, i) for i, j in to_near]
    home_far = [(j, i) for i, j in to_far]

    def spread(piece):
        return (
            piece,
            lax.ppermute(piece, "b", swap),
            lax.ppermute(piece, "a", swap),
            lax.ppermute(piece, ("a", "b"), cross),
        )

    def together(*groups):
        return lax.optimization_barrier(groups)

    def after(value, *others):
        return lax.optimization_barrier((value, *others))[0]

    def first_exchange(send_x, send_y, keep_x, keep_y):
        got_x = lax.ppermute(send_x, "b", swap)
        got_y = lax.ppermute(send_y, "a", swap)
        return keep_x, keep_y, got_x, got_y

    def second_exchange(send_y, send_x, base):
        return base, lax.ppermute(send_y, "a", swap), lax.ppermute(send_x, "b", swap)

    def direct(keep, send_x, send_y, send_xy):
        return (
            keep,
            lax.ppermute(send_x, "b", swap),
            lax.ppermute(send_y, "a", swap),
            lax.ppermute(send_xy, ("a", "b"), cross),
        )

    def over_outer(value):
        return lax.psum(value.astype(F32), "o").astype(BF16) if outer > 1 else value

    projection = input_weight.transpose(1, 2, 0).reshape(3 * cols, width)
    normed_one = norm_one(
        place,
        visible_counts,
        tokens,
        norm_one_gain,
        norm_one_shift,
    )
    piece_one, tail_one = pack_attention(
        place, projection, mixer_weight, after(input_bias, normed_one), one_row(up_bias)
    )
    depth_near_one = lax.ppermute(piece_one, ("c", "t"), to_near)
    normed_other = lax.ppermute(normed_one, "c", swap)
    piece_two = pack_hidden(place, up_weight, down_weight)
    both_two = jnp.concatenate([up_weight, down_weight])
    depth_near_one, normed_other, piece_two, both_two = together(
        depth_near_one, normed_other, piece_two, both_two
    )
    near_one = spread(depth_near_one)
    far_projection = lax.ppermute(after(projection, depth_near_one), ("c", "t"), to_far)
    far_mixer = lax.ppermute(after(tail_one, depth_near_one), ("c", "t"), to_far)
    near_two = lax.ppermute(after(piece_two, far_mixer, *near_one), ("c", "t"), to_near)

    own_one = (projection, tail_one)
    far_one = (far_projection, far_mixer)
    saved, soft, part = attention(place, own_one, near_one, far_one, normed_other, None, BF16)
    saved, soft, part, near_two = together(saved, soft, part, near_two)
    grad_other = lax.ppermute(after(output_grad, part), "c", swap)
    part_received = lax.ppermute(part, "c", swap)
    near_x = lax.ppermute(near_two, "b", swap)
    near_y = lax.ppermute(near_two, "a", swap)
    far_two = lax.ppermute(after(both_two, near_two), ("c", "t"), to_far)
    saved, soft, part = attention(
        place, own_one, near_one, far_one, normed_one, (saved, soft), F32
    )
    part, part_received, near_x, near_y, grad_other = together(
        part, part_received, near_x, near_y, grad_other
    )
    quarter = near_two.shape[0] // 2
    near_up = lax.ppermute(near_y[:quarter], "b", swap)
    near_down = lax.ppermute(near_x[quarter:], "a", swap)
    first_sum, normed_two = norm_two(
        tokens,
        part,
        part_received,
        one_row(mixer_bias),
        one_row(norm_two_gain),
        one_row(norm_two_shift),
    )
    normed_two, first_sum, near_up, near_down = together(
        normed_two, first_sum, near_up, near_down
    )
    normed_two_other = lax.ppermute(normed_two, "c", swap)
    normed_two_both = (normed_two, normed_two_other)

    grad_both = (output_grad, grad_other)
    pieces = (near_two, near_x, near_y, near_up, near_down, depth_near_one)
    near_outs = hidden_block(place, pieces, normed_two_both, grad_both, False)
    near_outs, far_two = together(near_outs, far_two)
    *grads_near, bias_near, out_near, out_send, back_near, back_send = near_outs
    stage_near = first_exchange(*grads_near)
    back_near_received = lax.ppermute(back_send, "c", swap)
    out_near_received = lax.ppermute(out_send, "c", swap)
    shards = (both_two, tail_one, far_two, far_mixer)
    far_outs = hidden_block(place, shards, normed_two_both, grad_both, True)
    far_outs, stage_near, back_near_received, out_near_received = together(
        far_outs, stage_near, back_near_received, out_near_received
    )
    grads_far, bias_far, out_far, out_send, back_far_mine, back_send = far_outs

    got_far = lax.ppermute(grads_far, ("c", "t"), home_far)
    back_received = lax.ppermute(back_send, "c", swap)
    (stage_near,) = sums(place, (first_sums_kernel, stage_near))
    back_received = after(back_received, *stage_near)
    stage_near = second_exchange(*stage_near)
    grad_first_low, sums_two = norm_two_back(
        (back_near, back_near_received, back_far_mine, back_received),
        first_sum,
        one_row(norm_two_gain),
        output_grad,
    )
    first_other = lax.ppermute(grad_first_low, "c", swap)
    out_received = lax.ppermute(after(out_send, first_other), "c", swap)

    normed_both = (normed_one, normed_other)
    first_both = (grad_first_low, first_other)
    *grads_one_near, bias_one_near, back_near, back_send = attention_back(
        place, 1, None, near_one, normed_both, first_both, saved, soft
    )
    grads_one_near, back_near, back_send, stage_near, got_far, out_received = together(
        grads_one_near, back_near, back_send, stage_near, got_far, out_received
    )
    one_near = direct(*grads_one_near)
    (plane_near,), (send_far,) = sums(
        place, (plane_sums_kernel, stage_near), (pair_send_kernel, (grads_far, got_far))
    )
    depth_near = lax.ppermute(plane_near, ("c", "t"), home_near)
    received_far = lax.ppermute(send_far, "c", swap)
    back_near_send = after(back_send, received_far)
    grad_low_late = after(grad_first_low, plane_near)
    *grads_one_far, bias_one_far, back_far_mine, back_send = attention_back(
        place, 0, own_one, far_one, normed_both, (grad_low_late, first_other), saved, soft
    )
    grads_one_far, back_far_mine, back_send, one_near, received_far, depth_near = together(
        grads_one_far, back_far_mine, back_send, one_near, received_far, depth_near
    )
    back_near_received = lax.ppermute(back_near_send, "c", swap)

    one_far = direct(*grads_one_far)
    back_received = lax.ppermute(back_send, "c", swap)
    (one_near,), sums_far, (keep_two, send_two) = sums(
        place,
        (total_kernel, one_near),
        (pair_sums_kernel, (grads_far, got_far, received_far)),
        (half_split_kernel, (depth_near,)),
    )
    one_depth_near = lax.ppermute(one_near, ("c", "t"), home_near)
    received_two = lax.ppermute(send_two, "c", swap)
    grad_tokens, vectors = norm_one_back(
        groups,
        place,
        (back_near, back_near_received, back_far_mine, back_received),
        tokens,
        one_row(norm_one_gain),
        grad_first_low,
        sums_two,
        bias_near,
        bias_far,
        bias_one_near,
        bias_one_far,
    )
    vectors_core = lax.ppermute(vectors, "c", swap)
    vectors_core, one_far, received_two = together(vectors_core, one_far, received_two)
    (one_far,), (vectors,) = sums(
        place, (total_kernel, one_far), (total_kernel, (vectors, vectors_core))
    )
    one_depth_far = lax.ppermute(one_far, ("c", "t"), home_far)
    sums_far = direct(*sums_far)
    result = (
        first_sum
        + (out_near.astype(F32) + out_near_received.astype(F32))
        + (out_far.astype(F32) + out_received.astype(F32))
        + down_bias
    ).astype(BF16)
    one_depth_far, one_depth_near, result = together(one_depth_far, one_depth_near, result)
    ((keep_one, send_one),) = sums(
        place, (depth_sums_kernel, (one_far, one_depth_far, one_depth_near))
    )
    received_one = lax.ppermute(send_one, "c", swap)
    vectors_plane = spread(vectors)
    received_one, vectors_plane, sums_far = together(received_one, vectors_plane, sums_far)
    (parts,), (vectors,) = sums(
        place,
        (last_sums_kernel, (keep_one, received_one, *sums_far, keep_two, received_two)),
        (total_kernel, vectors_plane),
    )
    mine = spread(over_outer(parts))
    turns = [
        lax.ppermute(vectors, "t", [(z, (z + k) % groups) for z in range(groups)])
        for k in range(1, groups)
    ]
    vectors = sum(turns, vectors)
    if outer > 1:
        vectors = lax.psum(vectors, "o")
    grad_up_bias = lax.dynamic_slice_in_dim(vectors, 6 + t, 1)[0]
    grad_input_bias = lax.dynamic_slice_in_dim(vectors, 6 + groups + t, 1).reshape(-1, cols)[:2]
    rows_out = [vectors[index] for index in range(6)]
    mine, rows_out, grad_up_bias, grad_input_bias = together(
        mine, rows_out, grad_up_bias, grad_input_bias
    )
    other = tuple(lax.ppermute(part, "c", swap) for part in mine)
    half_done = finish(place, mine, 0, None)
    other, half_done = together(other, half_done)
    grad_input, grad_mixer, grad_up, grad_down = finish(place, other, 1, half_done)
    grad_input = grad_input.reshape(3, cols, width).transpose(2, 0, 1)
    return (
        result,
        grad_tokens,
        rows_out[0],
        rows_out[1],
        grad_input,
        grad_input_bias,
        grad_mixer,
        rows_out[4],
        rows_out[2],
        rows_out[3],
        grad_up,
        grad_up_bias,
        grad_down,
        rows_out[5],
    )


def solution(mesh):
    dp, groups = mesh.shape["dp"], mesh.shape["tensor"]
    outer = dp // 8
    split = jax.sharding.Mesh(
        mesh.devices.reshape(outer, 2, 2, 2, groups), ("o", "a", "b", "c", "t")
    )
    dp_axes = ("o", "a", "b", "c")
    all_axes = dp_axes + ("t",)
    in_specs = (
        P(all_axes, None),
        P(dp_axes),
        P(),
        P(),
        P(None, None, "t"),
        P(None, "t"),
        P("t", None),
        P(),
        P(),
        P(),
        P(None, "t"),
        P("t"),
        P("t", None),
        P(),
        P(all_axes, None),
    )
    out_specs = (
        P(all_axes, None),
        P(all_axes, None),
        P(),
        P(),
        P(None, None, "t"),
        P(None, "t"),
        P("t", None),
        P(),
        P(),
        P(),
        P(None, "t"),
        P("t"),
        P("t", None),
        P(),
    )
    return jax.shard_map(
        functools.partial(local, groups=groups, outer=outer),
        mesh=split,
        in_specs=in_specs,
        out_specs=out_specs,
        check_vma=False,
    )
```

```python
import functools

import jax
import jax.numpy as jnp
import numpy as np
from jax import lax
from jax.experimental import pallas as pl
from jax.experimental.pallas import tpu as pltpu
from jax.sharding import PartitionSpec as P

HD = 64
SLOTS = 80
LANES = 128
TILE_IMAGES = 4
MASKED = -1000000000.0
EPS = 1e-06
F32 = jnp.float32
BF16 = jnp.bfloat16

ANY = pl.BlockSpec(memory_space=pl.ANY)
SMEM = pl.BlockSpec(memory_space=pltpu.SMEM)
VMEM = pl.BlockSpec(memory_space=pltpu.VMEM)


def shape(dims, kind):
    return jax.ShapeDtypeStruct(tuple(dims), kind)


def kept(dims, kind):
    return pltpu.HBM(tuple(dims), kind)


def from_hbm(*arrays):
    return tuple(pltpu.with_memory_space_constraint(a, pltpu.HBM) for a in arrays)


def params(megabytes, grid_dims=0):
    semantics = ("arbitrary",) * grid_dims if grid_dims else None
    return pltpu.CompilerParams(
        vmem_limit_bytes=megabytes * 1024 * 1024, dimension_semantics=semantics
    )


def cost(flops, moved):
    return pl.CostEstimate(flops=int(flops), bytes_accessed=int(moved), transcendentals=0)


def dot(left, right):
    return lax.dot_general(left, right, (((1,), (0,)), ((), ())), preferred_element_type=F32)


def dot_rows(left, right):
    return lax.dot_general(left, right, (((1,), (1,)), ((), ())), preferred_element_type=F32)


def dot_columns(left, right):
    return lax.dot_general(left, right, (((0,), (0,)), ((), ())), preferred_element_type=F32)


def centred(rows):
    center = rows - jnp.mean(rows, axis=-1, keepdims=True)
    spread = jnp.mean(center * center, axis=-1, keepdims=True)
    return center, lax.rsqrt(spread + EPS)


def norm_back(rows, gain, grad):
    center, rstd = centred(rows)
    xhat = center * rstd
    e = grad * gain
    back = rstd * (
        e - jnp.mean(e, axis=-1, keepdims=True) - xhat * jnp.mean(e * xhat, axis=-1, keepdims=True)
    )
    return (
        back,
        jnp.sum(grad * xhat, axis=0, keepdims=True),
        jnp.sum(grad, axis=0, keepdims=True),
    )


def norm_one_kernel(images, chunk, place, counts, tokens, gain, shift, out):
    rows = tokens.shape[0]

    @pl.loop(0, rows // chunk)
    def _(step):
        at = pl.ds(pl.multiple_of(step * chunk, chunk), chunk)
        center, rstd = centred(tokens[at, :].astype(F32))
        out[at, :] = (
            center * rstd * gain[...].reshape(1, -1) + shift[...].reshape(1, -1)
        ).astype(BF16)

    extra = out.shape[0] - rows
    row = lax.broadcasted_iota(jnp.int32, (extra, out.shape[1]), 0)
    table = jnp.zeros((extra, out.shape[1]), F32)
    first = place[2] * images
    for image in range(images):
        table = jnp.where(row == image, counts[first + image].astype(F32), table)
    out[rows:, :] = table.astype(BF16)


def norm_one(place, counts, tokens, gain, shift):
    rows, width = tokens.shape
    images = rows // SLOTS
    return pl.pallas_call(
        functools.partial(norm_one_kernel, images, SLOTS),
        out_shape=shape((rows + 16, width), BF16),
        in_specs=[SMEM, SMEM, VMEM, VMEM, VMEM],
        out_specs=VMEM,
        compiler_params=params(16),
        cost_estimate=cost(rows * width * 10, rows * width * 4),
    )(place, counts, *from_hbm(tokens, gain, shift))


def norm_two_kernel(tokens, mine, received, bias, gain, shift, first_sum, normed):
    total = tokens[...].astype(F32) + (mine[...] + received[...].astype(F32)) + bias[...]
    first_sum[...] = total
    center, rstd = centred(total)
    normed[...] = (center * rstd * gain[...] + shift[...]).astype(BF16)


def rows_spec(tile, width):
    return pl.BlockSpec((tile, width), lambda i: (i, 0))


def fixed_spec(*dims):
    return pl.BlockSpec(dims, lambda i: (0,) * len(dims))


def norm_two(tokens, mine, received, bias, gain, shift):
    rows, width = tokens.shape
    tile = 2 * SLOTS
    row = rows_spec(tile, width)
    vector = fixed_spec(1, width)
    return pl.pallas_call(
        norm_two_kernel,
        grid=(rows // tile,),
        out_shape=(kept((rows, width), F32), shape((rows, width), BF16)),
        in_specs=[row, row, row, vector, vector, vector],
        out_specs=(row, row),
        compiler_params=params(16, 1),
        cost_estimate=cost(rows * width * 12, rows * width * 14),
    )(*from_hbm(tokens), mine, received, bias, gain, shift)


def added(*refs):
    total = refs[0][...].astype(F32)
    for ref in refs[1:]:
        total = total + ref[...].astype(F32)
    return total


def norm_two_back_kernel(
    part0, part1, part2, part3, first_sum, gain, output_grad, low, sums
):
    grad = added(part0, part1, part2, part3)
    back, grad_gain, grad_shift = norm_back(first_sum[...], gain[...], grad)
    out_grad = output_grad[...].astype(F32)
    total = out_grad + back
    low[...] = total.astype(BF16)

    @pl.when(pl.program_id(0) == 0)
    def _():
        sums[...] = jnp.zeros_like(sums)

    sums[0:1, :] += grad_gain
    sums[1:2, :] += grad_shift
    sums[2:3, :] += jnp.sum(total, axis=0, keepdims=True)
    sums[3:4, :] += jnp.sum(out_grad, axis=0, keepdims=True)


def norm_two_back(parts, first_sum, gain, output_grad):
    rows, width = parts[0].shape
    tile = 2 * SLOTS
    row = rows_spec(tile, width)
    return pl.pallas_call(
        norm_two_back_kernel,
        grid=(rows // tile,),
        out_shape=(shape((rows, width), BF16), shape((8, width), F32)),
        in_specs=[row] * 5 + [fixed_spec(1, width), row],
        out_specs=(row, fixed_spec(8, width)),
        compiler_params=params(16, 1),
        cost_estimate=cost(rows * width * 25, rows * width * 18),
    )(*parts, *from_hbm(first_sum), gain, *from_hbm(output_grad))


def norm_one_back_kernel(
    groups,
    place,
    part0,
    part1,
    part2,
    part3,
    tokens,
    gain,
    grad_first,
    sums_two,
    bias_near,
    bias_far,
    input_near,
    input_far,
    grad_tokens,
    vectors,
):
    grad = added(part0, part1, part2, part3)
    back, grad_gain, grad_shift = norm_back(tokens[...].astype(F32), gain[...], grad)
    grad_tokens[...] = grad_first[...].astype(F32) + back

    @pl.when(pl.program_id(0) == 0)
    def _():
        near = lax.rem(place[2] - 1 - place[1] + groups, groups)
        far = lax.rem(place[2] - 3 * place[1] + groups, groups)
        row = lax.broadcasted_iota(jnp.int32, vectors.shape, 0)
        table = jnp.zeros(vectors.shape, F32)
        for index in range(4):
            table = jnp.where(row == 2 + index, sums_two[index : index + 1, :], table)
        table = jnp.where(row == 6 + near, bias_near[0:1, :], table)
        vectors[...] = jnp.where(row == 6 + far, bias_far[0:1, :], table)
        columns = input_near.shape[1]
        few = lax.broadcasted_iota(jnp.int32, (vectors.shape[0], columns), 0)
        for index in range(2):
            table = jnp.where(
                few == 6 + groups + near, input_near[index : index + 1, :], 0.0
            ) + jnp.where(few == 6 + groups + far, input_far[index : index + 1, :], 0.0)
            vectors[:, index * columns : (index + 1) * columns] += table

    vectors[0:1, :] += grad_gain
    vectors[1:2, :] += grad_shift


def norm_one_back(groups, place, parts, tokens, gain, grad_first, *small):
    rows, width = parts[0].shape
    tile = 2 * SLOTS
    row = rows_spec(tile, width)
    return pl.pallas_call(
        functools.partial(norm_one_back_kernel, groups),
        grid=(rows // tile,),
        out_shape=(kept((rows, width), F32), shape((16, width), F32)),
        in_specs=[SMEM] + [row] * 5 + [fixed_spec(1, width), row]
        + [fixed_spec(*array.shape) for array in small],
        out_specs=(row, fixed_spec(16, width)),
        compiler_params=params(16, 1),
        cost_estimate=cost(rows * width * 25, rows * width * 16),
    )(place, *parts, *from_hbm(tokens), gain, *from_hbm(grad_first), *small)


def pack_attention_kernel(place, projection, mixer, bias, up_bias, out, tail, sem, tail_sem):
    quarter = place[0]
    tail_copy = pltpu.make_async_copy(mixer, tail.at[pl.ds(0, mixer.shape[0])], tail_sem)
    tail_copy.start()
    size = out.shape[0] - 16
    feature_rows = projection.shape[0]
    first = pl.multiple_of(quarter * size, 16)
    from_projection = quarter * size < feature_rows

    @pl.when(from_projection)
    def _():
        copy = pltpu.make_async_copy(
            projection.at[pl.ds(first, size)], out.at[pl.ds(0, size)], sem
        )
        copy.start()
        copy.wait()

    @pl.when(jnp.logical_not(from_projection))
    def _():
        copy = pltpu.make_async_copy(mixer, out.at[pl.ds(0, size)], sem)
        copy.start()
        copy.wait()

    columns = bias.shape[1]
    row = lax.broadcasted_iota(jnp.int32, (16, columns), 0)
    both = bias[...].astype(F32)
    rows = jnp.where(row == 0, both[0:1, :], jnp.where(row == 1, both[1:2, :], 0.0))
    row_all = lax.broadcasted_iota(jnp.int32, (16, out.shape[1]), 0)
    out[size:, :] = jnp.where(row_all == 2, up_bias[...].astype(F32), 0.0).astype(BF16)
    row_two = jnp.where(row == 2, up_bias[:, 0:columns].astype(F32), rows)
    out[size:, 0:columns] = row_two.astype(BF16)
    tail[size:, :] = out[size:, :]
    tail_copy.wait()


def pack_attention(place, projection, mixer, bias, up_bias):
    size, width = mixer.shape
    return pl.pallas_call(
        pack_attention_kernel,
        out_shape=(shape((size + 16, width), BF16),) * 2,
        in_specs=[SMEM, ANY, ANY, VMEM, VMEM],
        out_specs=(VMEM, VMEM),
        scratch_shapes=[pltpu.SemaphoreType.DMA(()), pltpu.SemaphoreType.DMA(())],
        compiler_params=params(16),
        cost_estimate=cost(0, 2 * size * width),
    )(place, *from_hbm(projection, mixer, bias, up_bias))


def pack_hidden_kernel(place, up, down, out, sems):
    size = out.shape[0] // 2
    first = pl.multiple_of(place[0] * size, 16)
    copies = [
        pltpu.make_async_copy(
            source.at[pl.ds(first, size)], out.at[pl.ds(index * size, size)], sems.at[index]
        )
        for index, source in enumerate((up, down))
    ]
    run_copies(copies)


def pack_hidden(place, up, down):
    size, width = up.shape[0] // 4, up.shape[1]
    return pl.pallas_call(
        pack_hidden_kernel,
        out_shape=shape((2 * size, width), BF16),
        in_specs=[SMEM, ANY, ANY],
        out_specs=VMEM,
        scratch_shapes=[pltpu.SemaphoreType.DMA((2,))],
        compiler_params=params(16),
        cost_estimate=cost(0, 4 * size * width),
    )(place, *from_hbm(up, down))


def run_copies(copies):
    for copy in copies:
        copy.start()
    for copy in copies:
        copy.wait()


def make_copies(copies, sems):
    return [
        pltpu.make_async_copy(source, to, sems.at[index])
        for index, (source, to) in enumerate(copies)
    ]


def piece_copies(place, pieces, target, sems):
    size = pieces[0].shape[0] - 16
    copies = []
    for flip, piece in enumerate(pieces):
        to = pl.multiple_of(lax.bitwise_xor(place[0], flip) * size, 16)
        copies.append((piece.at[pl.ds(0, size)], target.at[pl.ds(to, size)]))
    copies.append((pieces[0].at[pl.ds(size, 16)], target.at[pl.ds(4 * size, 16)]))
    return make_copies(copies, sems)


def hidden_copies(place, pieces, bias_piece, target, sems):
    size = pieces[0].shape[0] // 2
    copies = []
    for flip in range(4):
        quarter = lax.bitwise_xor(place[0], flip)
        for matrix in range(2):
            to = pl.multiple_of((4 * matrix + quarter) * size, 16)
            source = pieces[3 + matrix] if flip == 3 else pieces[flip].at[pl.ds(matrix * size, size)]
            copies.append((source, target.at[pl.ds(to, size)]))
    first = bias_piece.shape[0] - 16
    copies.append((bias_piece.at[pl.ds(first, 16)], target.at[pl.ds(8 * size, 16)]))
    return make_copies(copies, sems)


def head_lanes(rows, width):
    return lax.broadcasted_iota(jnp.int32, (rows, width), 1) // HD


def spread_heads(block, lanes, heads):
    gap = jnp.zeros((LANES - SLOTS, block.shape[1]), block.dtype)
    parts = []
    for head in range(heads):
        parts.append(jnp.where(lanes == head, block, jnp.zeros_like(block)))
        parts.append(gap)
    return jnp.concatenate(parts, axis=0)


def gather_heads(product, lanes, heads):
    total = product[0:SLOTS]
    for head in range(1, heads):
        total = jnp.where(lanes == head, product[head * LANES : head * LANES + SLOTS], total)
    return total


def start_on_core(place, own, far, cut, sems):
    copies = [make_copies(cut(parts), sems) for parts in (own, far)]
    for core, some in enumerate(copies):

        @pl.when(place[1] == core)
        def _():
            for copy in some:
                copy.start()

    return copies[0]


def start_far(place, own, far, target, sems):
    def cut(parts):
        size = parts[0].shape[0]
        return [
            (parts[0], target.at[pl.ds(0, size)]),
            (parts[1], target.at[pl.ds(size, parts[1].shape[0])]),
        ]

    return start_on_core(place, own, far, cut, sems)


def start_matrices(place, own, far, target, sems):
    def cut(parts):
        size = parts[0].shape[0]
        bias = parts[1].at[pl.ds(parts[1].shape[0] - 16, 16)]
        return [(parts[0], target.at[pl.ds(0, size)]), (bias, target.at[pl.ds(size, 16)])]

    return start_on_core(place, own, far, cut, sems)


def attention_kernel(
    heads,
    place,
    projection,
    tail,
    near0,
    near1,
    near2,
    near3,
    far0,
    far1,
    normed,
    counts,
    *rest,
):
    saved, soft, part, weights, table, sems = rest[-6:]

    @pl.when(pl.program_id(0) == 0)
    def _():
        copies = piece_copies(place, (near0, near1, near2, near3), weights.at[1], sems)
        for copy in copies:
            copy.start()
        far_sems = sems.at[pl.ds(8, 8)]
        copies += start_far(place, (projection, tail), (far0, far1), weights.at[0], far_sems)
        for copy in copies:
            copy.wait()

    cols = heads * HD
    visible_rows = counts[:, 0:LANES].astype(F32)
    for image in range(visible_rows.shape[0]):
        table[image, :, :] = visible_rows[image : image + 1, :]
    rows = normed[...]
    for slot in range(2):
        for index in range(3):
            value = dot_rows(rows, weights[slot, index * cols : (index + 1) * cols, :])
            if index != 1:
                bias_row = 0 if index == 0 else 1
                bias = weights[slot, 4 * cols : 4 * cols + 16, 0:cols].astype(F32)
                value = value + bias[bias_row : bias_row + 1, :]
            saved[4 * slot + index, :, :] = value.astype(BF16)

    lanes = head_lanes(SLOTS, cols)
    key_index = lax.broadcasted_iota(jnp.int32, (SLOTS, LANES), 1).astype(F32)
    first = pl.program_id(0) * TILE_IMAGES

    def one_image(image, carry):
        at = pl.ds(pl.multiple_of(image * SLOTS, 16), SLOTS)
        visible = key_index < table[first + image]
        for slot in range(2):
            queries = saved[4 * slot, at, :]
            keys = spread_heads(saved[4 * slot + 1, at, :], lanes, heads)
            values = spread_heads(saved[4 * slot + 2, at, :], lanes, heads)
            scores = dot_rows(queries, keys) * (HD**-0.5)
            lows = []
            for head in range(heads):
                one = jnp.where(visible, scores[:, head * LANES : (head + 1) * LANES], MASKED)
                exponent = jnp.exp(one - jnp.max(one, axis=-1, keepdims=True))
                total = jnp.sum(exponent, axis=-1, keepdims=True)
                lows.append((exponent / total).astype(BF16))
            low = jnp.concatenate(lows, axis=1)
            soft[at, slot * heads * LANES : (slot + 1) * heads * LANES] = low
            saved[4 * slot + 3, at, :] = dot(low, values).astype(BF16)
        return carry

    lax.fori_loop(0, TILE_IMAGES, one_image, 0, unroll=True)
    total = dot(saved[3, :, :], weights[0, 3 * cols : 4 * cols, :])
    total = total + dot(saved[7, :, :], weights[1, 3 * cols : 4 * cols, :])
    part[...] = total.astype(part.dtype)


def attention(place, own, near, far, normed, before, kind):
    projection, tail = own
    cols, width = projection.shape[0] // 3, projection.shape[1]
    heads = cols // HD
    rows = normed.shape[0] - 16
    tile = TILE_IMAGES * SLOTS
    tiles = rows // tile
    base = tiles if before is None else 0
    extra = () if before is None else from_hbm(*before)
    args = (place, projection, tail, *near, *far, normed, normed, *extra)
    return pl.pallas_call(
        functools.partial(attention_kernel, heads),
        grid=(tiles,),
        out_shape=(
            kept((8, 2 * rows, cols), BF16),
            kept((2 * rows, 2 * heads * LANES), BF16),
            shape((rows, width), kind),
        ),
        in_specs=[SMEM]
        + [ANY] * 8
        + [
            pl.BlockSpec((tile, width), lambda i: (i, 0)),
            pl.BlockSpec((16, width), lambda i: (rows // 16, 0)),
        ]
        + [ANY] * len(extra),
        out_specs=(
            pl.BlockSpec((8, tile, cols), lambda i: (0, base + i, 0)),
            pl.BlockSpec((tile, 2 * heads * LANES), lambda i: (base + i, 0)),
            pl.BlockSpec((tile, width), lambda i: (i, 0)),
        ),
        scratch_shapes=[
            pltpu.VMEM((2, 4 * cols + 16, width), BF16),
            pltpu.VMEM((16, 1, LANES), F32),
            pltpu.SemaphoreType.DMA((16,)),
        ],
        input_output_aliases={11: 0, 12: 1} if extra else {},
        compiler_params=params(20, 1),
        cost_estimate=cost(rows * width * cols * 16 + rows * 400000, rows * width * 10 + 5e6),
    )(*args)


def attention_back_kernel(heads, far, place, *rest):
    count = 4
    pieces, rest = rest[:count], rest[count:]
    normed_mine, normed_other, grad_mine, grad_other, saved, soft = rest[:6]
    rest = rest[6:]
    keep, send_x, send_y, send_xy, bias_sums = rest[:5]
    rest = rest[5:]
    back_mine, back_other, weights, sums, grads, sems = rest
    step = pl.program_id(0)
    steps = pl.num_programs(0)
    cols = heads * HD
    mine = step < steps // 2

    @pl.when(step == 0)
    def _():
        if far:
            copies = start_far(place, pieces[:2], pieces[2:], weights, sems)
        else:
            copies = piece_copies(place, pieces, weights, sems)
            for copy in copies:
                copy.start()
        for copy in copies:
            copy.wait()
        sums[...] = jnp.zeros_like(sums)
        bias_sums[...] = jnp.zeros_like(bias_sums)

    normed = jnp.where(mine, normed_mine[...], normed_other[...])
    grad = jnp.where(mine, grad_mine[...], grad_other[...])
    grads[3, :, :] = dot_rows(grad, weights[3 * cols : 4 * cols, :]).astype(BF16)
    lanes = head_lanes(SLOTS, cols)

    def one_image(image, carry):
        at = pl.ds(pl.multiple_of(image * SLOTS, 16), SLOTS)
        queries = saved[0, at, :]
        keys = spread_heads(saved[1, at, :], lanes, heads)
        values = spread_heads(saved[2, at, :], lanes, heads)
        grad_mixed = grads[3, at, :]
        low = soft[at, :]
        grad_soft = dot_rows(grad_mixed, values)
        lows = []
        for head in range(heads):
            one = low[:, head * LANES : (head + 1) * LANES].astype(F32)
            grad_one = grad_soft[:, head * LANES : (head + 1) * LANES]
            inner = jnp.sum(grad_one * one, axis=-1, keepdims=True)
            lows.append((one * (grad_one - inner) * (HD**-0.5)).astype(BF16))
        grad_scores = jnp.concatenate(lows, axis=1)
        grad_queries = dot(grad_scores, keys)
        grad_values = gather_heads(dot_columns(low, grad_mixed), lanes, heads)
        grad_keys = gather_heads(dot_columns(grad_scores, queries), lanes, heads)
        bias_sums[0:1, :] += jnp.sum(grad_queries, axis=0, keepdims=True)
        bias_sums[1:2, :] += jnp.sum(grad_values, axis=0, keepdims=True)
        grads[0, at, :] = grad_queries.astype(BF16)
        grads[1, at, :] = grad_keys.astype(BF16)
        grads[2, at, :] = grad_values.astype(BF16)
        return carry

    lax.fori_loop(0, TILE_IMAGES, one_image, 0, unroll=True)
    back = None
    for index in range(3):
        at = slice(index * cols, (index + 1) * cols)
        value = grads[index, :, :]
        term = dot(value, weights[at, :])
        back = term if back is None else back + term
        sums[at, :] += dot_columns(value, normed)
    sums[3 * cols : 4 * cols, :] += dot_columns(saved[3, :, :], grad)

    @pl.when(mine)
    def _():
        back_mine[...] = back.astype(BF16)

    @pl.when(jnp.logical_not(mine))
    def _():
        back_other[...] = back.astype(BF16)

    @pl.when(step == steps - 1)
    def _():
        size = keep.shape[2]
        for flip, ref in enumerate((keep, send_x, send_y, send_xy)):
            quarter = lax.bitwise_xor(place[0], flip)
            for half in range(2):
                at = pl.ds(pl.multiple_of((2 * quarter + half) * size, 16), size)
                ref[half, 0, :, :] = sums[at, :].astype(BF16)


def half_spec(tile, width, tiles, second):
    if second:
        return pl.BlockSpec((tile, width), lambda i: (jnp.maximum(i - tiles, 0), 0))
    return pl.BlockSpec((tile, width), lambda i: (jnp.minimum(i, tiles - 1), 0))


def attention_back(place, slot, own, pieces, normed, grads, saved, soft):
    rows, width = grads[0].shape
    cols = saved.shape[2]
    heads = cols // HD
    tile = TILE_IMAGES * SLOTS
    tiles = rows // tile
    far = own is not None
    mine, other = half_spec(tile, width, tiles, False), half_spec(tile, width, tiles, True)
    dims = (2, 1, cols // 2, width)
    weights = (*own, *pieces) if far else pieces
    return pl.pallas_call(
        functools.partial(attention_back_kernel, heads, far),
        grid=(2 * tiles,),
        out_shape=(
            *(shape(dims, BF16),) * 4,
            shape((8, cols), F32),
            shape((rows, width), BF16),
            shape((rows, width), BF16),
        ),
        in_specs=[SMEM]
        + [ANY] * 4
        + [
            mine,
            other,
            mine,
            other,
            pl.BlockSpec((4, tile, cols), lambda i: (slot, i, 0)),
            pl.BlockSpec((tile, heads * LANES), lambda i: (i, slot)),
        ],
        out_specs=(*(fixed_spec(*dims),) * 4, fixed_spec(8, cols), mine, other),
        scratch_shapes=[
            pltpu.VMEM((4 * cols + 16, width), BF16),
            pltpu.VMEM((4 * cols, width), F32),
            pltpu.VMEM((4, tile, cols), BF16),
            pltpu.SemaphoreType.DMA((16,)),
        ],
        compiler_params=params(24, 1),
        cost_estimate=cost(rows * width * cols * 30 + rows * 6e5, rows * width * 20 + 4e6),
    )(place, *weights, *normed, *grads, *from_hbm(saved, soft))


def hidden_kernel(last, place, *rest):
    count = 4 if last else 6
    pieces, rest = rest[:count], rest[count:]
    normed_parts, grad_parts, rest = rest[:2], rest[2:4], rest[4:]
    if last:
        whole_grads, rest = rest[0], rest[1:]
    else:
        (send_x, send_y, keep_x, keep_y), rest = rest[:4], rest[4:]
    bias_sums, out_mine, out_other, back_mine, back_other = rest[:5]
    rest = rest[5:]
    weights, normed, grad, active, grad_low, sums_up, sums_down, summed = rest[:8]
    piece_sems, sems, out_sems = rest[8:]
    rows, width = normed.shape
    half = rows // 2

    def load(first, parts, target):
        return [
            pltpu.make_async_copy(part, target.at[pl.ds(index * half, half)], sems.at[first + index])
            for index, part in enumerate(parts)
        ]

    normed_copies, grad_copies = load(0, normed_parts, normed), load(2, grad_parts, grad)
    for copy in normed_copies:
        copy.start()
    if last:
        first_needed = start_matrices(place, pieces[:2], pieces[2:], weights, piece_sems)
        then_needed = []
    else:
        starts = hidden_copies(place, pieces[:5], pieces[5], weights, piece_sems)
        first_needed, then_needed = starts[0:8:2] + [starts[8]], starts[1:8:2]
        for copy in first_needed + then_needed:
            copy.start()
    for copy in grad_copies:
        copy.start()
    for copy in normed_copies + first_needed:
        copy.wait()

    bias = weights[2 * width : 2 * width + 16, :].astype(F32)[2:3, :]
    chunk = 256
    chunks = [slice(first, first + chunk) for first in range(0, width, chunk)]

    def weight_sums(at):
        sums_up[:, at] = dot_columns(normed[...], grad_low[:, at]).astype(BF16)
        sums_down[at, :] = dot_columns(active[:, at], grad[...]).astype(BF16)

    for index, at in enumerate(chunks):
        hidden = dot(normed[...], weights[0:width, at]) + bias[:, at]
        if index == 0:
            for copy in grad_copies + then_needed:
                copy.wait()
        phi = 0.5 + 0.5 * lax.erf(hidden * (0.5**0.5))
        slope = phi + hidden * (jnp.exp(-0.5 * hidden * hidden) * ((2.0 * np.pi) ** -0.5))
        active[:, at] = (hidden * phi).astype(BF16)
        down_rows = weights[width + at.start : width + at.stop, :]
        grad_pre = dot_rows(grad[...], down_rows) * slope
        bias_sums[0:1, at] = jnp.sum(grad_pre, axis=0, keepdims=True)
        grad_low[:, at] = grad_pre.astype(BF16)
        if index:
            weight_sums(chunks[index - 1])
    weight_sums(chunks[-1])

    size = sums_up.shape[0] // 8
    copies = []
    for flip in range(4):
        quarter = lax.bitwise_xor(place[0], flip)
        for part in range(2):
            at = pl.ds(pl.multiple_of((2 * quarter + part) * size, 16), size)
            for matrix, source in enumerate((sums_up, sums_down)):
                if last:
                    target = whole_grads.at[part, flip, matrix]
                elif part == 0:
                    target = (keep_x if flip % 2 == 0 else send_x).at[flip // 2, matrix]
                else:
                    target = (keep_y if flip < 2 else send_y).at[flip % 2, matrix]
                sem = piece_sems.at[len(copies)]
                copies.append(pltpu.make_async_copy(source.at[at], target, sem))
    for copy in copies:
        copy.start()
    targets = ((out_mine, out_other), (back_mine, back_other))

    def out_copy(index, part, first, sem):
        target = targets[index][part]
        source = summed.at[index, pl.ds(part * half, target.shape[0]), pl.ds(first, chunk)]
        return pltpu.make_async_copy(source, target.at[:, pl.ds(first, chunk)], sem)

    def finish_chunk(step, carry):
        first = pl.multiple_of(step * chunk, chunk)
        at = pl.ds(first, chunk)
        back = dot_rows(grad_low[...], weights[at, :])
        out = dot(active[...], weights[width : 2 * width, at])
        for index, value in enumerate((out, back)):
            summed[index, :, at] = value.astype(BF16)
            for part in range(2):
                out_copy(index, part, first, out_sems.at[step, index, part]).start()
        return carry

    lax.fori_loop(0, len(chunks), finish_chunk, 0)
    for step in range(len(chunks)):
        for index in range(2):
            for part in range(2):
                out_copy(index, part, step * chunk, out_sems.at[step, index, part]).wait()
    for copy in copies:
        copy.wait()


def hidden_block(place, pieces, normed, grads, last):
    rows, width = normed[0].shape
    size = width // 8
    if last:
        grad_shapes = (kept((2, 4, 2, size, width), BF16),)
    else:
        grad_shapes = (kept((2, 2, size, width), BF16),) * 4
    return pl.pallas_call(
        functools.partial(hidden_kernel, last),
        out_shape=(
            *grad_shapes,
            shape((8, width), F32),
            kept((rows, width), BF16),
            kept((rows, width), BF16),
            kept((rows, width), BF16),
            kept((rows, width), BF16),
        ),
        in_specs=[SMEM] + [ANY] * (len(pieces) + 4),
        out_specs=(ANY,) * len(grad_shapes) + (VMEM,) + (ANY,) * 4,
        scratch_shapes=[
            pltpu.VMEM((2 * width + 16, width), BF16),
            pltpu.VMEM((2 * rows, width), BF16),
            pltpu.VMEM((2 * rows, width), BF16),
            pltpu.VMEM((2 * rows, width), BF16),
            pltpu.VMEM((2 * rows, width), BF16),
            pltpu.VMEM((width, width), BF16),
            pltpu.VMEM((width, width), BF16),
            pltpu.VMEM((2, 2 * rows, width), BF16),
            pltpu.SemaphoreType.DMA((16,)),
            pltpu.SemaphoreType.DMA((4,)),
            pltpu.SemaphoreType.DMA((width // 256, 2, 2)),
        ],
        compiler_params=params(44),
        cost_estimate=cost(rows * width * width * 24, rows * width * 24 + 8e6),
    )(place, *pieces, *from_hbm(*normed, *grads))


def first_sums_kernel(keep_x, keep_y, got_x, got_y, send_y, send_x, base):
    add = lambda u, v: u.astype(F32) + v.astype(F32)
    base[0] = add(keep_x[0], got_x[0])
    base[1] = add(keep_y[0], got_y[0])
    send_y[...] = add(keep_x[1], got_x[1]).astype(BF16)
    send_x[...] = add(keep_y[1], got_y[1]).astype(BF16)


def plane_sums_kernel(base, next_y, next_x, plane):
    plane[0] = (base[0] + next_y[...].astype(F32)).astype(BF16)
    plane[1] = (base[1] + next_x[...].astype(F32)).astype(BF16)


def depth_sums_kernel(core, local_far, far, near, keep, send):
    halves = []
    for half in range(2):
        first = jnp.where(core == 0, local_far[half], far[half])
        halves.append(first.astype(F32) + near[half].astype(F32))
    keep[...] = jnp.where(core == 0, halves[0], halves[1])
    send[...] = jnp.where(core == 0, halves[1], halves[0]).astype(BF16)


def pair_send_kernel(core, own, got, send):
    send[...] = jnp.where(core == 0, own[1], got[0])


def pair_sums_kernel(core, own, got, received, keep, send_x, send_y, send_xy):
    for flip, ref in enumerate((keep, send_x, send_y, send_xy)):
        half = jnp.where(core == 0, own[0, flip], got[1, flip])
        ref[...] = (half.astype(F32) + received[flip].astype(F32)).astype(BF16)


def half_split_kernel(core, both, keep, send):
    keep[...] = jnp.where(core == 0, both[0], both[1])
    send[...] = jnp.where(core == 0, both[1], both[0])


def last_sums_kernel(keep, received, *rest):
    total = rest[-1]
    total[0:1] = (keep[...] + received[...].astype(F32)).astype(BF16)
    both = rest[0][...].astype(F32)
    for ref in rest[1:-1]:
        both = both + ref[...].astype(F32)
    total[1:3] = both.astype(BF16)


def total_kernel(*refs):
    total = refs[0][...].astype(F32)
    for ref in refs[1:-1]:
        total = total + ref[...].astype(F32)
    refs[-1][...] = total.astype(refs[-1].dtype)


def sums_kernel(parts, place, *refs):
    ins = sum(count for _, count, _ in parts)
    in_refs, out_refs = refs[:ins], refs[ins:]
    for body, count, outs in parts:
        mine, in_refs = in_refs[:count], in_refs[count:]
        results, out_refs = out_refs[:outs], out_refs[outs:]
        with_core = (depth_sums_kernel, pair_send_kernel, pair_sums_kernel, half_split_kernel)
        lead = (place[1],) if body in with_core else ()
        rows = mine[0].shape[-2]
        chunk = 32 if rows % 32 == 0 else 16

        @pl.loop(0, rows // chunk)
        def _(step):
            at = pl.ds(pl.multiple_of(step * chunk, chunk), chunk)
            views = [
                ref.at[(slice(None),) * (len(ref.shape) - 2) + (at, slice(None))]
                for ref in (*mine, *results)
            ]
            body(*lead, *views)


def sums(place, *work):
    parts, args, out_shapes = [], [], []
    for body, arrays in work:
        like = arrays[0].shape
        if body is first_sums_kernel:
            outs = [shape(like[1:], BF16), shape(like[1:], BF16), shape(like, F32)]
        elif body is plane_sums_kernel:
            outs = [shape(like, BF16)]
        elif body is pair_send_kernel:
            outs = [shape(like[1:], BF16)]
        elif body is pair_sums_kernel:
            outs = [shape(like[2:], BF16)] * 4
        elif body is half_split_kernel:
            outs = [shape(like[1:], BF16)] * 2
        elif body is depth_sums_kernel:
            outs = [shape(like[1:], F32), shape(like[1:], BF16)]
        else:
            dims = (3, *like[1:]) if body is last_sums_kernel else like
            outs = [shape(dims, arrays[0].dtype if body is total_kernel else BF16)]
        parts.append((body, len(arrays), len(outs)))
        args += arrays
        out_shapes += outs
    moved = sum(4 * np.prod(o.shape) for o in out_shapes)
    results = pl.pallas_call(
        functools.partial(sums_kernel, tuple(parts)),
        out_shape=tuple(out_shapes),
        in_specs=[SMEM] + [VMEM] * len(args),
        out_specs=(VMEM,) * len(out_shapes),
        compiler_params=params(16),
        cost_estimate=cost(0, moved),
    )(place, *args)
    grouped = []
    for _, _, count in parts:
        grouped.append(tuple(results[:count]))
        results = results[count:]
    return grouped


def finish_kernel(side, place, *refs):
    parts, outs, wide, sems = refs[:4], refs[-6:-2], refs[-2], refs[-1]
    matrices, half = parts[0].shape[:2]
    grad_input, grad_mixer = outs[:2]
    part = place[1] if side == 0 else 1 - place[1]
    copies = []
    for flip in range(4):
        quarter = lax.bitwise_xor(place[0], flip)
        at = pl.ds(pl.multiple_of((2 * quarter + part) * half, 8), half)
        for matrix in range(matrices):
            source, sem = wide.at[flip, matrix], sems.at[flip, matrix]

            @pl.loop(0, half // 16)
            def _(step):
                rows = pl.ds(pl.multiple_of(step * 16, 16), 16)
                wide[flip, matrix, rows, :] = parts[flip][matrix, rows, :].astype(F32)

            if matrix:
                copies.append(pltpu.make_async_copy(source, outs[1 + matrix].at[at], sem))
                copies[-1].start()
                continue
            rows = pl.ds(pl.multiple_of(part * half, 8), half)
            copies.append(pltpu.make_async_copy(source, grad_mixer.at[rows], sem))

            @pl.when(quarter < 3)
            def _():
                pltpu.make_async_copy(source, grad_input.at[at], sem).start()

            @pl.when(quarter == 3)
            def _():
                copies[-1].start()

    for copy in copies:
        copy.wait()


def finish(place, parts, side, before):
    matrices, half, width = parts[0].shape
    extra = before or ()
    return pl.pallas_call(
        functools.partial(finish_kernel, side),
        out_shape=tuple(kept((count * half, width), F32) for count in (6, 2, 8, 8)),
        in_specs=[SMEM] + [VMEM] * 4 + [ANY] * len(extra),
        out_specs=(ANY,) * 4,
        scratch_shapes=[
            pltpu.VMEM((4, matrices, half, width), F32),
            pltpu.SemaphoreType.DMA((4, matrices)),
        ],
        input_output_aliases={5 + index: index for index in range(len(extra))},
        compiler_params=params(12),
        cost_estimate=cost(0, half * width * 72),
    )(place, *parts, *extra)


def local(
    tokens,
    visible_counts,
    norm_one_gain,
    norm_one_shift,
    input_weight,
    input_bias,
    mixer_weight,
    mixer_bias,
    norm_two_gain,
    norm_two_shift,
    up_weight,
    up_bias,
    down_weight,
    down_bias,
    output_grad,
    groups,
    outer,
):
    width = tokens.shape[1]
    rows = tokens.shape[0]
    cols = mixer_weight.shape[0]
    t = lax.axis_index("t")
    core = lax.axis_index("c")
    place = jnp.stack([2 * lax.axis_index("a") + lax.axis_index("b"), core, t]).astype(jnp.int32)
    one_row = lambda v: v.reshape(1, -1)

    swap = [(0, 1), (1, 0)]
    cross = [(0, 3), (1, 2), (2, 1), (3, 0)]
    to_near = [(z, (z + 1) % groups) for z in range(groups)] + [
        (groups + z, groups + (z + 2) % groups) for z in range(groups)
    ]
    to_far = [(groups + z, groups + (z + 3) % groups) for z in range(groups)]
    home_near = [(j, i) for i, j in to_near]
    home_far = [(j, i) for i, j in to_far]

    def spread(piece):
        return (
            piece,
            lax.ppermute(piece, "b", swap),
            lax.ppermute(piece, "a", swap),
            lax.ppermute(piece, ("a", "b"), cross),
        )

    def together(*groups):
        return lax.optimization_barrier(groups)

    def after(value, *others):
        return lax.optimization_barrier((value, *others))[0]

    def first_exchange(send_x, send_y, keep_x, keep_y):
        got_x = lax.ppermute(send_x, "b", swap)
        got_y = lax.ppermute(send_y, "a", swap)
        return keep_x, keep_y, got_x, got_y

    def second_exchange(send_y, send_x, base):
        return base, lax.ppermute(send_y, "a", swap), lax.ppermute(send_x, "b", swap)

    def direct(keep, send_x, send_y, send_xy):
        return (
            keep,
            lax.ppermute(send_x, "b", swap),
            lax.ppermute(send_y, "a", swap),
            lax.ppermute(send_xy, ("a", "b"), cross),
        )

    def over_outer(value):
        return lax.psum(value.astype(F32), "o").astype(BF16) if outer > 1 else value

    projection = input_weight.transpose(1, 2, 0).reshape(3 * cols, width)
    normed_one = norm_one(
        place,
        visible_counts,
        tokens,
        norm_one_gain,
        norm_one_shift,
    )
    piece_one, tail_one = pack_attention(
        place, projection, mixer_weight, after(input_bias, normed_one), one_row(up_bias)
    )
    depth_near_one = lax.ppermute(piece_one, ("c", "t"), to_near)
    normed_other = lax.ppermute(normed_one, "c", swap)
    piece_two = pack_hidden(place, up_weight, down_weight)
    both_two = jnp.concatenate([up_weight, down_weight])
    depth_near_one, normed_other, piece_two, both_two = together(
        depth_near_one, normed_other, piece_two, both_two
    )
    near_one = spread(depth_near_one)
    far_projection = lax.ppermute(after(projection, depth_near_one), ("c", "t"), to_far)
    far_mixer = lax.ppermute(after(tail_one, depth_near_one), ("c", "t"), to_far)
    near_two = lax.ppermute(after(piece_two, far_mixer, *near_one), ("c", "t"), to_near)

    own_one = (projection, tail_one)
    far_one = (far_projection, far_mixer)
    saved, soft, part = attention(place, own_one, near_one, far_one, normed_other, None, BF16)
    saved, soft, part, near_two = together(saved, soft, part, near_two)
    grad_other = lax.ppermute(after(output_grad, part), "c", swap)
    part_received = lax.ppermute(part, "c", swap)
    near_x = lax.ppermute(near_two, "b", swap)
    near_y = lax.ppermute(near_two, "a", swap)
    far_two = lax.ppermute(after(both_two, near_two), ("c", "t"), to_far)
    saved, soft, part = attention(
        place, own_one, near_one, far_one, normed_one, (saved, soft), F32
    )
    part, part_received, near_x, near_y, grad_other = together(
        part, part_received, near_x, near_y, grad_other
    )
    quarter = near_two.shape[0] // 2
    near_up = lax.ppermute(near_y[:quarter], "b", swap)
    near_down = lax.ppermute(near_x[quarter:], "a", swap)
    first_sum, normed_two = norm_two(
        tokens,
        part,
        part_received,
        one_row(mixer_bias),
        one_row(norm_two_gain),
        one_row(norm_two_shift),
    )
    normed_two, first_sum, near_up, near_down = together(
        normed_two, first_sum, near_up, near_down
    )
    normed_two_other = lax.ppermute(normed_two, "c", swap)
    normed_two_both = (normed_two, normed_two_other)

    grad_both = (output_grad, grad_other)
    pieces = (near_two, near_x, near_y, near_up, near_down, depth_near_one)
    near_outs = hidden_block(place, pieces, normed_two_both, grad_both, False)
    near_outs, far_two = together(near_outs, far_two)
    *grads_near, bias_near, out_near, out_send, back_near, back_send = near_outs
    stage_near = first_exchange(*grads_near)
    back_near_received = lax.ppermute(back_send, "c", swap)
    out_near_received = lax.ppermute(out_send, "c", swap)
    shards = (both_two, tail_one, far_two, far_mixer)
    far_outs = hidden_block(place, shards, normed_two_both, grad_both, True)
    far_outs, stage_near, back_near_received, out_near_received = together(
        far_outs, stage_near, back_near_received, out_near_received
    )
    grads_far, bias_far, out_far, out_send, back_far_mine, back_send = far_outs

    got_far = lax.ppermute(grads_far, ("c", "t"), home_far)
    back_received = lax.ppermute(back_send, "c", swap)
    (stage_near,) = sums(place, (first_sums_kernel, stage_near))
    back_received = after(back_received, *stage_near)
    stage_near = second_exchange(*stage_near)
    grad_first_low, sums_two = norm_two_back(
        (back_near, back_near_received, back_far_mine, back_received),
        first_sum,
        one_row(norm_two_gain),
        output_grad,
    )
    first_other = lax.ppermute(grad_first_low, "c", swap)
    out_received = lax.ppermute(after(out_send, first_other), "c", swap)

    normed_both = (normed_one, normed_other)
    first_both = (grad_first_low, first_other)
    *grads_one_near, bias_one_near, back_near, back_send = attention_back(
        place, 1, None, near_one, normed_both, first_both, saved, soft
    )
    grads_one_near, back_near, back_send, stage_near, got_far, out_received = together(
        grads_one_near, back_near, back_send, stage_near, got_far, out_received
    )
    one_near = direct(*grads_one_near)
    (plane_near,), (send_far,) = sums(
        place, (plane_sums_kernel, stage_near), (pair_send_kernel, (grads_far, got_far))
    )
    depth_near = lax.ppermute(plane_near, ("c", "t"), home_near)
    received_far = lax.ppermute(send_far, "c", swap)
    back_near_send = after(back_send, received_far)
    grad_low_late = after(grad_first_low, plane_near)
    *grads_one_far, bias_one_far, back_far_mine, back_send = attention_back(
        place, 0, own_one, far_one, normed_both, (grad_low_late, first_other), saved, soft
    )
    grads_one_far, back_far_mine, back_send, one_near, received_far, depth_near = together(
        grads_one_far, back_far_mine, back_send, one_near, received_far, depth_near
    )
    back_near_received = lax.ppermute(back_near_send, "c", swap)

    one_far = direct(*grads_one_far)
    back_received = lax.ppermute(back_send, "c", swap)
    (one_near,), sums_far, (keep_two, send_two) = sums(
        place,
        (total_kernel, one_near),
        (pair_sums_kernel, (grads_far, got_far, received_far)),
        (half_split_kernel, (depth_near,)),
    )
    one_depth_near = lax.ppermute(one_near, ("c", "t"), home_near)
    received_two = lax.ppermute(send_two, "c", swap)
    grad_tokens, vectors = norm_one_back(
        groups,
        place,
        (back_near, back_near_received, back_far_mine, back_received),
        tokens,
        one_row(norm_one_gain),
        grad_first_low,
        sums_two,
        bias_near,
        bias_far,
        bias_one_near,
        bias_one_far,
    )
    vectors_core = lax.ppermute(vectors, "c", swap)
    vectors_core, one_far, received_two = together(vectors_core, one_far, received_two)
    (one_far,), (vectors,) = sums(
        place, (total_kernel, one_far), (total_kernel, (vectors, vectors_core))
    )
    one_depth_far = lax.ppermute(one_far, ("c", "t"), home_far)
    sums_far = direct(*sums_far)
    result = (
        first_sum
        + (out_near.astype(F32) + out_near_received.astype(F32))
        + (out_far.astype(F32) + out_received.astype(F32))
        + down_bias
    ).astype(BF16)
    one_depth_far, one_depth_near, result = together(one_depth_far, one_depth_near, result)
    ((keep_one, send_one),) = sums(
        place, (depth_sums_kernel, (one_far, one_depth_far, one_depth_near))
    )
    received_one = lax.ppermute(send_one, "c", swap)
    vectors_plane = spread(vectors)
    received_one, vectors_plane, sums_far = together(received_one, vectors_plane, sums_far)
    (parts,), (vectors,) = sums(
        place,
        (last_sums_kernel, (keep_one, received_one, *sums_far, keep_two, received_two)),
        (total_kernel, vectors_plane),
    )
    mine = spread(over_outer(parts))
    turns = [
        lax.ppermute(vectors, "t", [(z, (z + k) % groups) for z in range(groups)])
        for k in range(1, groups)
    ]
    vectors = sum(turns, vectors)
    if outer > 1:
        vectors = lax.psum(vectors, "o")
    grad_up_bias = lax.dynamic_slice_in_dim(vectors, 6 + t, 1)[0]
    grad_input_bias = lax.dynamic_slice_in_dim(vectors, 6 + groups + t, 1).reshape(-1, cols)[:2]
    rows_out = [vectors[index] for index in range(6)]
    mine, rows_out, grad_up_bias, grad_input_bias = together(
        mine, rows_out, grad_up_bias, grad_input_bias
    )
    other = tuple(lax.ppermute(part, "c", swap) for part in mine)
    half_done = finish(place, mine, 0, None)
    other, half_done = together(other, half_done)
    grad_input, grad_mixer, grad_up, grad_down = finish(place, other, 1, half_done)
    grad_input = grad_input.reshape(3, cols, width).transpose(2, 0, 1)
    return (
        result,
        grad_tokens,
        rows_out[0],
        rows_out[1],
        grad_input,
        grad_input_bias,
        grad_mixer,
        rows_out[4],
        rows_out[2],
        rows_out[3],
        grad_up,
        grad_up_bias,
        grad_down,
        rows_out[5],
    )


def solution(mesh):
    dp, groups = mesh.shape["dp"], mesh.shape["tensor"]
    outer = dp // 8
    split = jax.sharding.Mesh(
        mesh.devices.reshape(outer, 2, 2, 2, groups), ("o", "a", "b", "c", "t")
    )
    dp_axes = ("o", "a", "b", "c")
    all_axes = dp_axes + ("t",)
    in_specs = (
        P(all_axes, None),
        P(dp_axes),
        P(),
        P(),
        P(None, None, "t"),
        P(None, "t"),
        P("t", None),
        P(),
        P(),
        P(),
        P(None, "t"),
        P("t"),
        P("t", None),
        P(),
        P(all_axes, None),
    )
    out_specs = (
        P(all_axes, None),
        P(all_axes, None),
        P(),
        P(),
        P(None, None, "t"),
        P(None, "t"),
        P("t", None),
        P(),
        P(),
        P(),
        P(None, "t"),
        P("t"),
        P("t", None),
        P(),
    )
    return jax.shard_map(
        functools.partial(local, groups=groups, outer=outer),
        mesh=split,
        in_specs=in_specs,
        out_specs=out_specs,
        check_vma=False,
    )
```

```python
import functools

import jax
import jax.numpy as jnp
import numpy as np
from jax import lax
from jax.experimental import pallas as pl
from jax.experimental.pallas import tpu as pltpu
from jax.sharding import PartitionSpec as P

HD = 64
SLOTS = 80
LANES = 128
TILE_IMAGES = 4
MASKED = -1000000000.0
EPS = 1e-06
F32 = jnp.float32
BF16 = jnp.bfloat16

ANY = pl.BlockSpec(memory_space=pl.ANY)
SMEM = pl.BlockSpec(memory_space=pltpu.SMEM)
VMEM = pl.BlockSpec(memory_space=pltpu.VMEM)


def shape(dims, kind):
    return jax.ShapeDtypeStruct(tuple(dims), kind)


def kept(dims, kind):
    return pltpu.HBM(tuple(dims), kind)


def from_hbm(*arrays):
    return tuple(pltpu.with_memory_space_constraint(a, pltpu.HBM) for a in arrays)


def params(megabytes, grid_dims=0):
    semantics = ("arbitrary",) * grid_dims if grid_dims else None
    return pltpu.CompilerParams(
        vmem_limit_bytes=megabytes * 1024 * 1024, dimension_semantics=semantics
    )


def cost(flops, moved):
    return pl.CostEstimate(flops=int(flops), bytes_accessed=int(moved), transcendentals=0)


def dot(left, right):
    return lax.dot_general(left, right, (((1,), (0,)), ((), ())), preferred_element_type=F32)


def dot_rows(left, right):
    return lax.dot_general(left, right, (((1,), (1,)), ((), ())), preferred_element_type=F32)


def dot_columns(left, right):
    return lax.dot_general(left, right, (((0,), (0,)), ((), ())), preferred_element_type=F32)


def centred(rows):
    center = rows - jnp.mean(rows, axis=-1, keepdims=True)
    spread = jnp.mean(center * center, axis=-1, keepdims=True)
    return center, lax.rsqrt(spread + EPS)


def norm_back(rows, gain, grad):
    center, rstd = centred(rows)
    xhat = center * rstd
    e = grad * gain
    back = rstd * (
        e - jnp.mean(e, axis=-1, keepdims=True) - xhat * jnp.mean(e * xhat, axis=-1, keepdims=True)
    )
    return (
        back,
        jnp.sum(grad * xhat, axis=0, keepdims=True),
        jnp.sum(grad, axis=0, keepdims=True),
    )


def norm_one_kernel(images, chunk, place, counts, tokens, gain, shift, out):
    rows = tokens.shape[0]

    @pl.loop(0, rows // chunk)
    def _(step):
        at = pl.ds(pl.multiple_of(step * chunk, chunk), chunk)
        center, rstd = centred(tokens[at, :].astype(F32))
        out[at, :] = (
            center * rstd * gain[...].reshape(1, -1) + shift[...].reshape(1, -1)
        ).astype(BF16)

    extra = out.shape[0] - rows
    row = lax.broadcasted_iota(jnp.int32, (extra, out.shape[1]), 0)
    table = jnp.zeros((extra, out.shape[1]), F32)
    first = place[2] * images
    for image in range(images):
        table = jnp.where(row == image, counts[first + image].astype(F32), table)
    out[rows:, :] = table.astype(BF16)


def norm_one(place, counts, tokens, gain, shift):
    rows, width = tokens.shape
    images = rows // SLOTS
    return pl.pallas_call(
        functools.partial(norm_one_kernel, images, SLOTS),
        out_shape=shape((rows + 16, width), BF16),
        in_specs=[SMEM, SMEM, VMEM, VMEM, VMEM],
        out_specs=VMEM,
        compiler_params=params(16),
        cost_estimate=cost(rows * width * 10, rows * width * 4),
    )(place, counts, *from_hbm(tokens, gain, shift))


def norm_two_kernel(tokens, mine, received, bias, gain, shift, first_sum, normed):
    total = tokens[...].astype(F32) + (mine[...].astype(F32) + received[...].astype(F32)) + bias[...]
    first_sum[...] = total
    center, rstd = centred(total)
    normed[...] = (center * rstd * gain[...] + shift[...]).astype(BF16)


def rows_spec(tile, width):
    return pl.BlockSpec((tile, width), lambda i: (i, 0))


def fixed_spec(*dims):
    return pl.BlockSpec(dims, lambda i: (0,) * len(dims))


def norm_two(tokens, mine, received, bias, gain, shift):
    rows, width = tokens.shape
    tile = 2 * SLOTS
    row = rows_spec(tile, width)
    vector = fixed_spec(1, width)
    return pl.pallas_call(
        norm_two_kernel,
        grid=(rows // tile,),
        out_shape=(kept((rows, width), F32), shape((rows, width), BF16)),
        in_specs=[row, row, row, vector, vector, vector],
        out_specs=(row, row),
        compiler_params=params(16, 1),
        cost_estimate=cost(rows * width * 12, rows * width * 14),
    )(*from_hbm(tokens), mine, received, bias, gain, shift)


def added(*refs):
    total = refs[0][...].astype(F32)
    for ref in refs[1:]:
        total = total + ref[...].astype(F32)
    return total


def norm_two_back_kernel(
    part0, part1, part2, part3, first_sum, gain, output_grad, low, sums
):
    grad = added(part0, part1, part2, part3)
    back, grad_gain, grad_shift = norm_back(first_sum[...], gain[...], grad)
    out_grad = output_grad[...].astype(F32)
    total = out_grad + back
    low[...] = total.astype(BF16)

    @pl.when(pl.program_id(0) == 0)
    def _():
        sums[...] = jnp.zeros_like(sums)

    sums[0:1, :] += grad_gain
    sums[1:2, :] += grad_shift
    sums[2:3, :] += jnp.sum(total, axis=0, keepdims=True)
    sums[3:4, :] += jnp.sum(out_grad, axis=0, keepdims=True)


def norm_two_back(parts, first_sum, gain, output_grad):
    rows, width = parts[0].shape
    tile = 2 * SLOTS
    row = rows_spec(tile, width)
    return pl.pallas_call(
        norm_two_back_kernel,
        grid=(rows // tile,),
        out_shape=(shape((rows, width), BF16), shape((8, width), F32)),
        in_specs=[row] * 5 + [fixed_spec(1, width), row],
        out_specs=(row, fixed_spec(8, width)),
        compiler_params=params(16, 1),
        cost_estimate=cost(rows * width * 25, rows * width * 18),
    )(*parts, *from_hbm(first_sum), gain, *from_hbm(output_grad))


def norm_one_back_kernel(
    groups,
    place,
    part0,
    part1,
    part2,
    part3,
    tokens,
    gain,
    grad_first,
    sums_two,
    bias_near,
    bias_far,
    input_near,
    input_far,
    grad_tokens,
    vectors,
):
    grad = added(part0, part1, part2, part3)
    back, grad_gain, grad_shift = norm_back(tokens[...].astype(F32), gain[...], grad)
    grad_tokens[...] = grad_first[...].astype(F32) + back

    @pl.when(pl.program_id(0) == 0)
    def _():
        near = lax.rem(place[2] - 1 - place[1] + groups, groups)
        far = lax.rem(place[2] - 3 * place[1] + groups, groups)
        row = lax.broadcasted_iota(jnp.int32, vectors.shape, 0)
        table = jnp.zeros(vectors.shape, F32)
        for index in range(4):
            table = jnp.where(row == 2 + index, sums_two[index : index + 1, :], table)
        table = jnp.where(row == 6 + near, bias_near[0:1, :], table)
        vectors[...] = jnp.where(row == 6 + far, bias_far[0:1, :], table)
        columns = input_near.shape[1]
        few = lax.broadcasted_iota(jnp.int32, (vectors.shape[0], columns), 0)
        for index in range(2):
            table = jnp.where(
                few == 6 + groups + near, input_near[index : index + 1, :], 0.0
            ) + jnp.where(few == 6 + groups + far, input_far[index : index + 1, :], 0.0)
            vectors[:, index * columns : (index + 1) * columns] += table

    vectors[0:1, :] += grad_gain
    vectors[1:2, :] += grad_shift


def norm_one_back(groups, place, parts, tokens, gain, grad_first, *small):
    rows, width = parts[0].shape
    tile = 2 * SLOTS
    row = rows_spec(tile, width)
    return pl.pallas_call(
        functools.partial(norm_one_back_kernel, groups),
        grid=(rows // tile,),
        out_shape=(kept((rows, width), F32), shape((16, width), F32)),
        in_specs=[SMEM] + [row] * 5 + [fixed_spec(1, width), row]
        + [fixed_spec(*array.shape) for array in small],
        out_specs=(row, fixed_spec(16, width)),
        compiler_params=params(16, 1),
        cost_estimate=cost(rows * width * 25, rows * width * 16),
    )(place, *parts, *from_hbm(tokens), gain, *from_hbm(grad_first), *small)


def pack_attention_kernel(place, projection, mixer, bias, up_bias, out, tail, sem, tail_sem):
    quarter = place[0]
    tail_copy = pltpu.make_async_copy(mixer, tail.at[pl.ds(0, mixer.shape[0])], tail_sem)
    tail_copy.start()
    size = out.shape[0] - 16
    feature_rows = projection.shape[0]
    first = pl.multiple_of(quarter * size, 16)
    from_projection = quarter * size < feature_rows

    @pl.when(from_projection)
    def _():
        copy = pltpu.make_async_copy(
            projection.at[pl.ds(first, size)], out.at[pl.ds(0, size)], sem
        )
        copy.start()
        copy.wait()

    @pl.when(jnp.logical_not(from_projection))
    def _():
        copy = pltpu.make_async_copy(mixer, out.at[pl.ds(0, size)], sem)
        copy.start()
        copy.wait()

    columns = bias.shape[1]
    row = lax.broadcasted_iota(jnp.int32, (16, columns), 0)
    both = bias[...].astype(F32)
    rows = jnp.where(row == 0, both[0:1, :], jnp.where(row == 1, both[1:2, :], 0.0))
    row_all = lax.broadcasted_iota(jnp.int32, (16, out.shape[1]), 0)
    out[size:, :] = jnp.where(row_all == 2, up_bias[...].astype(F32).reshape(1, -1), 0.0).astype(BF16)
    row_two = jnp.where(row == 2, up_bias[...].astype(F32).reshape(1, -1)[:, 0:columns], rows)
    out[size:, 0:columns] = row_two.astype(BF16)
    tail[size:, :] = out[size:, :]
    tail_copy.wait()


def pack_attention(place, projection, mixer, bias, up_bias):
    size, width = mixer.shape
    return pl.pallas_call(
        pack_attention_kernel,
        out_shape=(shape((size + 16, width), BF16),) * 2,
        in_specs=[SMEM, ANY, ANY, VMEM, VMEM],
        out_specs=(VMEM, VMEM),
        scratch_shapes=[pltpu.SemaphoreType.DMA(()), pltpu.SemaphoreType.DMA(())],
        compiler_params=params(16),
        cost_estimate=cost(0, 2 * size * width),
    )(place, *from_hbm(projection, mixer, bias, up_bias))


def pack_hidden_kernel(place, up, down, out, sems):
    size = out.shape[0] // 2
    first = pl.multiple_of(place[0] * size, 16)
    copies = [
        pltpu.make_async_copy(
            source.at[pl.ds(first, size)], out.at[pl.ds(index * size, size)], sems.at[index]
        )
        for index, source in enumerate((up, down))
    ]
    run_copies(copies)


def pack_hidden(place, up, down):
    size, width = up.shape[0] // 4, up.shape[1]
    return pl.pallas_call(
        pack_hidden_kernel,
        out_shape=shape((2 * size, width), BF16),
        in_specs=[SMEM, ANY, ANY],
        out_specs=VMEM,
        scratch_shapes=[pltpu.SemaphoreType.DMA((2,))],
        compiler_params=params(16),
        cost_estimate=cost(0, 4 * size * width),
    )(place, *from_hbm(up, down))


def run_copies(copies):
    for copy in copies:
        copy.start()
    for copy in copies:
        copy.wait()


def make_copies(copies, sems):
    return [
        pltpu.make_async_copy(source, to, sems.at[index])
        for index, (source, to) in enumerate(copies)
    ]


def piece_copies(place, pieces, target, sems):
    size = pieces[0].shape[0] - 16
    copies = []
    for flip, piece in enumerate(pieces):
        to = pl.multiple_of(lax.bitwise_xor(place[0], flip) * size, 16)
        copies.append((piece.at[pl.ds(0, size)], target.at[pl.ds(to, size)]))
    copies.append((pieces[0].at[pl.ds(size, 16)], target.at[pl.ds(4 * size, 16)]))
    return make_copies(copies, sems)


def hidden_copies(place, pieces, bias_piece, target, sems):
    size = pieces[0].shape[0] // 2
    copies = []
    for flip in range(4):
        quarter = lax.bitwise_xor(place[0], flip)
        for matrix in range(2):
            to = pl.multiple_of((4 * matrix + quarter) * size, 16)
            source = pieces[3 + matrix] if flip == 3 else pieces[flip].at[pl.ds(matrix * size, size)]
            copies.append((source, target.at[pl.ds(to, size)]))
    first = bias_piece.shape[0] - 16
    copies.append((bias_piece.at[pl.ds(first, 16)], target.at[pl.ds(8 * size, 16)]))
    return make_copies(copies, sems)


def head_lanes(rows, width):
    return lax.broadcasted_iota(jnp.int32, (rows, width), 1) // HD


def spread_heads(block, lanes, heads):
    gap = jnp.zeros((LANES - SLOTS, block.shape[1]), block.dtype)
    parts = []
    for head in range(heads):
        parts.append(jnp.where(lanes == head, block, jnp.zeros_like(block)))
        parts.append(gap)
    return jnp.concatenate(parts, axis=0)


def gather_heads(product, lanes, heads):
    total = product[0:SLOTS]
    for head in range(1, heads):
        total = jnp.where(lanes == head, product[head * LANES : head * LANES + SLOTS], total)
    return total


def start_on_core(place, own, far, cut, sems):
    copies = [make_copies(cut(parts), sems) for parts in (own, far)]
    for core, some in enumerate(copies):

        @pl.when(place[1] == core)
        def _():
            for copy in some:
                copy.start()

    return copies[0]


def start_far(place, own, far, target, sems):
    def cut(parts):
        size = parts[0].shape[0]
        return [
            (parts[0], target.at[pl.ds(0, size)]),
            (parts[1], target.at[pl.ds(size, parts[1].shape[0])]),
        ]

    return start_on_core(place, own, far, cut, sems)


def start_matrices(place, own, far, target, sems):
    def cut(parts):
        size = parts[0].shape[0]
        bias = parts[1].at[pl.ds(parts[1].shape[0] - 16, 16)]
        return [(parts[0], target.at[pl.ds(0, size)]), (bias, target.at[pl.ds(size, 16)])]

    return start_on_core(place, own, far, cut, sems)


def attention_kernel(
    heads,
    place,
    projection,
    tail,
    near0,
    near1,
    near2,
    near3,
    far0,
    far1,
    normed,
    counts,
    *rest,
):
    saved, soft, part, weights, table, sems = rest[-6:]

    @pl.when(pl.program_id(0) == 0)
    def _():
        copies = piece_copies(place, (near0, near1, near2, near3), weights.at[1], sems)
        for copy in copies:
            copy.start()
        far_sems = sems.at[pl.ds(8, 8)]
        copies += start_far(place, (projection, tail), (far0, far1), weights.at[0], far_sems)
        for copy in copies:
            copy.wait()

    cols = heads * HD
    visible_rows = counts[:, 0:LANES].astype(F32)
    for image in range(visible_rows.shape[0]):
        table[image, :, :] = visible_rows[image : image + 1, :]
    rows = normed[...]
    for slot in range(2):
        for index in range(3):
            value = dot_rows(rows, weights[slot, index * cols : (index + 1) * cols, :])
            if index != 1:
                bias_row = 0 if index == 0 else 1
                bias = weights[slot, 4 * cols : 4 * cols + 16, 0:cols].astype(F32)
                value = value + bias[bias_row : bias_row + 1, :]
            saved[4 * slot + index, :, :] = value.astype(BF16)

    lanes = head_lanes(SLOTS, cols)
    key_index = lax.broadcasted_iota(jnp.int32, (SLOTS, LANES), 1).astype(F32)
    first = pl.program_id(0) * TILE_IMAGES

    def one_image(image, carry):
        at = pl.ds(pl.multiple_of(image * SLOTS, 16), SLOTS)
        visible = key_index < table[first + image]
        for slot in range(2):
            queries = saved[4 * slot, at, :]
            keys = spread_heads(saved[4 * slot + 1, at, :], lanes, heads)
            values = spread_heads(saved[4 * slot + 2, at, :], lanes, heads)
            scores = dot_rows(queries, keys) * (HD**-0.5)
            lows = []
            for head in range(heads):
                one = jnp.where(visible, scores[:, head * LANES : (head + 1) * LANES], MASKED)
                exponent = jnp.exp(one - jnp.max(one, axis=-1, keepdims=True))
                total = jnp.sum(exponent, axis=-1, keepdims=True)
                lows.append((exponent / total).astype(BF16))
            low = jnp.concatenate(lows, axis=1)
            soft[at, slot * heads * LANES : (slot + 1) * heads * LANES] = low
            saved[4 * slot + 3, at, :] = dot(low, values).astype(BF16)
        return carry

    lax.fori_loop(0, TILE_IMAGES, one_image, 0, unroll=True)
    total = dot(saved[3, :, :], weights[0, 3 * cols : 4 * cols, :])
    total = total + dot(saved[7, :, :], weights[1, 3 * cols : 4 * cols, :])
    part[...] = total.astype(part.dtype)


def attention(place, own, near, far, normed, before, kind):
    projection, tail = own
    cols, width = projection.shape[0] // 3, projection.shape[1]
    heads = cols // HD
    rows = normed.shape[0] - 16
    tile = TILE_IMAGES * SLOTS
    tiles = rows // tile
    base = tiles if before is None else 0
    extra = () if before is None else from_hbm(*before)
    args = (place, projection, tail, *near, *far, normed, normed, *extra)
    return pl.pallas_call(
        functools.partial(attention_kernel, heads),
        grid=(tiles,),
        out_shape=(
            kept((8, 2 * rows, cols), BF16),
            kept((2 * rows, 2 * heads * LANES), BF16),
            shape((rows, width), kind),
        ),
        in_specs=[SMEM]
        + [ANY] * 8
        + [
            pl.BlockSpec((tile, width), lambda i: (i, 0)),
            pl.BlockSpec((16, width), lambda i: (rows // 16, 0)),
        ]
        + [ANY] * len(extra),
        out_specs=(
            pl.BlockSpec((8, tile, cols), lambda i: (0, base + i, 0)),
            pl.BlockSpec((tile, 2 * heads * LANES), lambda i: (base + i, 0)),
            pl.BlockSpec((tile, width), lambda i: (i, 0)),
        ),
        scratch_shapes=[
            pltpu.VMEM((2, 4 * cols + 16, width), BF16),
            pltpu.VMEM((16, 1, LANES), F32),
            pltpu.SemaphoreType.DMA((16,)),
        ],
        input_output_aliases={11: 0, 12: 1} if extra else {},
        compiler_params=params(20, 1),
        cost_estimate=cost(rows * width * cols * 16 + rows * 400000, rows * width * 10 + 5e6),
    )(*args)


def attention_back_kernel(heads, far, place, *rest):
    count = 4
    pieces, rest = rest[:count], rest[count:]
    normed_mine, normed_other, grad_mine, grad_other, saved, soft = rest[:6]
    rest = rest[6:]
    keep, send_x, send_y, send_xy, bias_sums = rest[:5]
    rest = rest[5:]
    back_mine, back_other, weights, sums, grads, sems = rest
    step = pl.program_id(0)
    steps = pl.num_programs(0)
    cols = heads * HD
    mine = step < steps // 2

    @pl.when(step == 0)
    def _():
        if far:
            copies = start_far(place, pieces[:2], pieces[2:], weights, sems)
        else:
            copies = piece_copies(place, pieces, weights, sems)
            for copy in copies:
                copy.start()
        for copy in copies:
            copy.wait()
        sums[...] = jnp.zeros_like(sums)
        bias_sums[...] = jnp.zeros_like(bias_sums)

    normed = jnp.where(mine, normed_mine[...], normed_other[...])
    grad = jnp.where(mine, grad_mine[...], grad_other[...])
    grads[3, :, :] = dot_rows(grad, weights[3 * cols : 4 * cols, :]).astype(BF16)
    lanes = head_lanes(SLOTS, cols)

    def one_image(image, carry):
        at = pl.ds(pl.multiple_of(image * SLOTS, 16), SLOTS)
        queries = saved[0, at, :]
        keys = spread_heads(saved[1, at, :], lanes, heads)
        values = spread_heads(saved[2, at, :], lanes, heads)
        grad_mixed = grads[3, at, :]
        low = soft[at, :]
        grad_soft = dot_rows(grad_mixed, values)
        lows = []
        for head in range(heads):
            one = low[:, head * LANES : (head + 1) * LANES].astype(F32)
            grad_one = grad_soft[:, head * LANES : (head + 1) * LANES]
            inner = jnp.sum(grad_one * one, axis=-1, keepdims=True)
            lows.append((one * (grad_one - inner) * (HD**-0.5)).astype(BF16))
        grad_scores = jnp.concatenate(lows, axis=1)
        grad_queries = dot(grad_scores, keys)
        grad_values = gather_heads(dot_columns(low, grad_mixed), lanes, heads)
        grad_keys = gather_heads(dot_columns(grad_scores, queries), lanes, heads)
        bias_sums[0:1, :] += jnp.sum(grad_queries, axis=0, keepdims=True)
        bias_sums[1:2, :] += jnp.sum(grad_values, axis=0, keepdims=True)
        grads[0, at, :] = grad_queries.astype(BF16)
        grads[1, at, :] = grad_keys.astype(BF16)
        grads[2, at, :] = grad_values.astype(BF16)
        return carry

    lax.fori_loop(0, TILE_IMAGES, one_image, 0, unroll=True)
    back = None
    for index in range(3):
        at = slice(index * cols, (index + 1) * cols)
        value = grads[index, :, :]
        term = dot(value, weights[at, :])
        back = term if back is None else back + term
        sums[at, :] += dot_columns(value, normed)
    sums[3 * cols : 4 * cols, :] += dot_columns(saved[3, :, :], grad)

    @pl.when(mine)
    def _():
        back_mine[...] = back.astype(BF16)

    @pl.when(jnp.logical_not(mine))
    def _():
        back_other[...] = back.astype(BF16)

    @pl.when(step == steps - 1)
    def _():
        size = keep.shape[2]
        for flip, ref in enumerate((keep, send_x, send_y, send_xy)):
            quarter = lax.bitwise_xor(place[0], flip)
            for half in range(2):
                at = pl.ds(pl.multiple_of((2 * quarter + half) * size, 16), size)
                ref[half, 0, :, :] = sums[at, :].astype(BF16)


def half_spec(tile, width, tiles, second):
    if second:
        return pl.BlockSpec((tile, width), lambda i: (jnp.maximum(i - tiles, 0), 0))
    return pl.BlockSpec((tile, width), lambda i: (jnp.minimum(i, tiles - 1), 0))


def attention_back(place, slot, own, pieces, normed, grads, saved, soft):
    rows, width = grads[0].shape
    cols = saved.shape[2]
    heads = cols // HD
    tile = TILE_IMAGES * SLOTS
    tiles = rows // tile
    far = own is not None
    mine, other = half_spec(tile, width, tiles, False), half_spec(tile, width, tiles, True)
    dims = (2, 1, cols // 2, width)
    weights = (*own, *pieces) if far else pieces
    return pl.pallas_call(
        functools.partial(attention_back_kernel, heads, far),
        grid=(2 * tiles,),
        out_shape=(
            *(shape(dims, BF16),) * 4,
            shape((8, cols), F32),
            shape((rows, width), BF16),
            shape((rows, width), BF16),
        ),
        in_specs=[SMEM]
        + [ANY] * 4
        + [
            mine,
            other,
            mine,
            other,
            pl.BlockSpec((4, tile, cols), lambda i: (slot, i, 0)),
            pl.BlockSpec((tile, heads * LANES), lambda i: (i, slot)),
        ],
        out_specs=(*(fixed_spec(*dims),) * 4, fixed_spec(8, cols), mine, other),
        scratch_shapes=[
            pltpu.VMEM((4 * cols + 16, width), BF16),
            pltpu.VMEM((4 * cols, width), F32),
            pltpu.VMEM((4, tile, cols), BF16),
            pltpu.SemaphoreType.DMA((16,)),
        ],
        compiler_params=params(24, 1),
        cost_estimate=cost(rows * width * cols * 30 + rows * 6e5, rows * width * 20 + 4e6),
    )(place, *weights, *normed, *grads, *from_hbm(saved, soft))


def hidden_kernel(last, place, *rest):
    count = 4 if last else 6
    pieces, rest = rest[:count], rest[count:]
    normed_parts, grad_parts, rest = rest[:2], rest[2:4], rest[4:]
    if last:
        whole_grads, rest = rest[0], rest[1:]
    else:
        (send_x, send_y, keep_x, keep_y), rest = rest[:4], rest[4:]
    bias_sums, out_mine, out_other, back_mine, back_other = rest[:5]
    rest = rest[5:]
    weights, normed, grad, active, grad_low, sums_up, sums_down, summed = rest[:8]
    piece_sems, sems, out_sems = rest[8:]
    rows, width = normed.shape
    half = rows // 2

    def load(first, parts, target):
        return [
            pltpu.make_async_copy(part, target.at[pl.ds(index * half, half)], sems.at[first + index])
            for index, part in enumerate(parts)
        ]

    normed_copies, grad_copies = load(0, normed_parts, normed), load(2, grad_parts, grad)
    for copy in normed_copies:
        copy.start()
    if last:
        first_needed = start_matrices(place, pieces[:2], pieces[2:], weights, piece_sems)
        then_needed = []
    else:
        starts = hidden_copies(place, pieces[:5], pieces[5], weights, piece_sems)
        first_needed, then_needed = starts[0:8:2] + [starts[8]], starts[1:8:2]
        for copy in first_needed + then_needed:
            copy.start()
    for copy in grad_copies:
        copy.start()
    for copy in normed_copies + first_needed:
        copy.wait()

    bias = weights[2 * width : 2 * width + 16, :].astype(F32)[2:3, :]
    chunk = 256
    chunks = [slice(first, first + chunk) for first in range(0, width, chunk)]

    def weight_sums(at):
        sums_up[:, at] = dot_columns(normed[...], grad_low[:, at]).astype(BF16)
        sums_down[at, :] = dot_columns(active[:, at], grad[...]).astype(BF16)

    for index, at in enumerate(chunks):
        hidden = dot(normed[...], weights[0:width, at]) + bias[:, at]
        if index == 0:
            for copy in grad_copies + then_needed:
                copy.wait()
        phi = 0.5 + 0.5 * lax.erf(hidden * (0.5**0.5))
        slope = phi + hidden * (jnp.exp(-0.5 * hidden * hidden) * ((2.0 * np.pi) ** -0.5))
        active[:, at] = (hidden * phi).astype(BF16)
        down_rows = weights[width + at.start : width + at.stop, :]
        grad_pre = dot_rows(grad[...], down_rows) * slope
        bias_sums[0:1, at] = jnp.sum(grad_pre, axis=0, keepdims=True)
        grad_low[:, at] = grad_pre.astype(BF16)
        if index:
            weight_sums(chunks[index - 1])
    weight_sums(chunks[-1])

    size = sums_up.shape[0] // 8
    copies = []
    for flip in range(4):
        quarter = lax.bitwise_xor(place[0], flip)
        for part in range(2):
            at = pl.ds(pl.multiple_of((2 * quarter + part) * size, 16), size)
            for matrix, source in enumerate((sums_up, sums_down)):
                if last:
                    target = whole_grads.at[part, flip, matrix]
                elif part == 0:
                    target = (keep_x if flip % 2 == 0 else send_x).at[flip // 2, matrix]
                else:
                    target = (keep_y if flip < 2 else send_y).at[flip % 2, matrix]
                sem = piece_sems.at[len(copies)]
                copies.append(pltpu.make_async_copy(source.at[at], target, sem))
    for copy in copies:
        copy.start()
    targets = ((out_mine, out_other), (back_mine, back_other))

    def out_copy(index, part, first, sem):
        target = targets[index][part]
        source = summed.at[index, pl.ds(part * half, target.shape[0]), pl.ds(first, chunk)]
        return pltpu.make_async_copy(source, target.at[:, pl.ds(first, chunk)], sem)

    def finish_chunk(step, carry):
        first = pl.multiple_of(step * chunk, chunk)
        at = pl.ds(first, chunk)
        back = dot_rows(grad_low[...], weights[at, :])
        out = dot(active[...], weights[width : 2 * width, at])
        for index, value in enumerate((out, back)):
            summed[index, :, at] = value.astype(BF16)
            for part in range(2):
                out_copy(index, part, first, out_sems.at[step, index, part]).start()
        return carry

    lax.fori_loop(0, len(chunks), finish_chunk, 0)
    for step in range(len(chunks)):
        for index in range(2):
            for part in range(2):
                out_copy(index, part, step * chunk, out_sems.at[step, index, part]).wait()
    for copy in copies:
        copy.wait()


def hidden_block(place, pieces, normed, grads, last):
    rows, width = normed[0].shape
    size = width // 8
    if last:
        grad_shapes = (kept((2, 4, 2, size, width), BF16),)
    else:
        grad_shapes = (kept((2, 2, size, width), BF16),) * 4
    return pl.pallas_call(
        functools.partial(hidden_kernel, last),
        out_shape=(
            *grad_shapes,
            shape((8, width), F32),
            kept((rows, width), BF16),
            kept((rows, width), BF16),
            kept((rows, width), BF16),
            kept((rows, width), BF16),
        ),
        in_specs=[SMEM] + [ANY] * (len(pieces) + 4),
        out_specs=(ANY,) * len(grad_shapes) + (VMEM,) + (ANY,) * 4,
        scratch_shapes=[
            pltpu.VMEM((2 * width + 16, width), BF16),
            pltpu.VMEM((2 * rows, width), BF16),
            pltpu.VMEM((2 * rows, width), BF16),
            pltpu.VMEM((2 * rows, width), BF16),
            pltpu.VMEM((2 * rows, width), BF16),
            pltpu.VMEM((width, width), BF16),
            pltpu.VMEM((width, width), BF16),
            pltpu.VMEM((2, 2 * rows, width), BF16),
            pltpu.SemaphoreType.DMA((16,)),
            pltpu.SemaphoreType.DMA((4,)),
            pltpu.SemaphoreType.DMA((width // 256, 2, 2)),
        ],
        compiler_params=params(44),
        cost_estimate=cost(rows * width * width * 24, rows * width * 24 + 8e6),
    )(place, *pieces, *from_hbm(*normed, *grads))


def first_sums_kernel(keep_x, keep_y, got_x, got_y, send_y, send_x, base):
    add = lambda u, v: u.astype(F32) + v.astype(F32)
    base[0] = add(keep_x[0], got_x[0])
    base[1] = add(keep_y[0], got_y[0])
    send_y[...] = add(keep_x[1], got_x[1]).astype(BF16)
    send_x[...] = add(keep_y[1], got_y[1]).astype(BF16)


def plane_sums_kernel(base, next_y, next_x, plane):
    plane[0] = (base[0] + next_y[...].astype(F32)).astype(BF16)
    plane[1] = (base[1] + next_x[...].astype(F32)).astype(BF16)


def depth_sums_kernel(core, local_far, far, near, keep, send):
    halves = []
    for half in range(2):
        first = jnp.where(core == 0, local_far[half], far[half])
        halves.append(first.astype(F32) + near[half].astype(F32))
    keep[...] = jnp.where(core == 0, halves[0], halves[1])
    send[...] = jnp.where(core == 0, halves[1], halves[0]).astype(BF16)


def pair_send_kernel(core, own, got, send):
    send[...] = jnp.where(core == 0, own[1], got[0])


def pair_sums_kernel(core, own, got, received, keep, send_x, send_y, send_xy):
    for flip, ref in enumerate((keep, send_x, send_y, send_xy)):
        half = jnp.where(core == 0, own[0, flip], got[1, flip])
        ref[...] = (half.astype(F32) + received[flip].astype(F32)).astype(BF16)


def half_split_kernel(core, both, keep, send):
    keep[...] = jnp.where(core == 0, both[0], both[1])
    send[...] = jnp.where(core == 0, both[1], both[0])


def last_sums_kernel(keep, received, *rest):
    total = rest[-1]
    total[0:1] = (keep[...] + received[...].astype(F32)).astype(BF16)
    both = rest[0][...].astype(F32)
    for ref in rest[1:-1]:
        both = both + ref[...].astype(F32)
    total[1:3] = both.astype(BF16)


def total_kernel(*refs):
    total = refs[0][...].astype(F32)
    for ref in refs[1:-1]:
        total = total + ref[...].astype(F32)
    refs[-1][...] = total.astype(refs[-1].dtype)


def sums_kernel(parts, place, *refs):
    ins = sum(count for _, count, _ in parts)
    in_refs, out_refs = refs[:ins], refs[ins:]
    for body, count, outs in parts:
        mine, in_refs = in_refs[:count], in_refs[count:]
        results, out_refs = out_refs[:outs], out_refs[outs:]
        with_core = (depth_sums_kernel, pair_send_kernel, pair_sums_kernel, half_split_kernel)
        lead = (place[1],) if body in with_core else ()
        rows = mine[0].shape[-2]
        chunk = 32 if rows % 32 == 0 else 16

        @pl.loop(0, rows // chunk)
        def _(step):
            at = pl.ds(pl.multiple_of(step * chunk, chunk), chunk)
            views = [
                ref.at[(slice(None),) * (len(ref.shape) - 2) + (at, slice(None))]
                for ref in (*mine, *results)
            ]
            body(*lead, *views)


def sums(place, *work):
    parts, args, out_shapes = [], [], []
    for body, arrays in work:
        like = arrays[0].shape
        if body is first_sums_kernel:
            outs = [shape(like[1:], BF16), shape(like[1:], BF16), shape(like, F32)]
        elif body is plane_sums_kernel:
            outs = [shape(like, BF16)]
        elif body is pair_send_kernel:
            outs = [shape(like[1:], BF16)]
        elif body is pair_sums_kernel:
            outs = [shape(like[2:], BF16)] * 4
        elif body is half_split_kernel:
            outs = [shape(like[1:], BF16)] * 2
        elif body is depth_sums_kernel:
            outs = [shape(like[1:], F32), shape(like[1:], BF16)]
        else:
            dims = (3, *like[1:]) if body is last_sums_kernel else like
            outs = [shape(dims, arrays[0].dtype if body is total_kernel else BF16)]
        parts.append((body, len(arrays), len(outs)))
        args += arrays
        out_shapes += outs
    moved = sum(4 * np.prod(o.shape) for o in out_shapes)
    results = pl.pallas_call(
        functools.partial(sums_kernel, tuple(parts)),
        out_shape=tuple(out_shapes),
        in_specs=[SMEM] + [VMEM] * len(args),
        out_specs=(VMEM,) * len(out_shapes),
        compiler_params=params(16),
        cost_estimate=cost(0, moved),
    )(place, *args)
    grouped = []
    for _, _, count in parts:
        grouped.append(tuple(results[:count]))
        results = results[count:]
    return grouped


def finish_kernel(side, place, *refs):
    parts, outs, wide, sems = refs[:4], refs[-6:-2], refs[-2], refs[-1]
    matrices, half = parts[0].shape[:2]
    grad_input, grad_mixer = outs[:2]
    part = place[1] if side == 0 else 1 - place[1]
    copies = []
    for flip in range(4):
        quarter = lax.bitwise_xor(place[0], flip)
        at = pl.ds(pl.multiple_of((2 * quarter + part) * half, 8), half)
        for matrix in range(matrices):
            source, sem = wide.at[flip, matrix], sems.at[flip, matrix]

            @pl.loop(0, half // 16)
            def _(step):
                rows = pl.ds(pl.multiple_of(step * 16, 16), 16)
                wide[flip, matrix, rows, :] = parts[flip][matrix, rows, :].astype(F32)

            if matrix:
                copies.append(pltpu.make_async_copy(source, outs[1 + matrix].at[at], sem))
                copies[-1].start()
                continue
            rows = pl.ds(pl.multiple_of(part * half, 8), half)
            copies.append(pltpu.make_async_copy(source, grad_mixer.at[rows], sem))

            @pl.when(quarter < 3)
            def _():
                pltpu.make_async_copy(source, grad_input.at[at], sem).start()

            @pl.when(quarter == 3)
            def _():
                copies[-1].start()

    for copy in copies:
        copy.wait()


def finish(place, parts, side, before):
    matrices, half, width = parts[0].shape
    extra = before or ()
    return pl.pallas_call(
        functools.partial(finish_kernel, side),
        out_shape=tuple(kept((count * half, width), F32) for count in (6, 2, 8, 8)),
        in_specs=[SMEM] + [VMEM] * 4 + [ANY] * len(extra),
        out_specs=(ANY,) * 4,
        scratch_shapes=[
            pltpu.VMEM((4, matrices, half, width), F32),
            pltpu.SemaphoreType.DMA((4, matrices)),
        ],
        input_output_aliases={5 + index: index for index in range(len(extra))},
        compiler_params=params(12),
        cost_estimate=cost(0, half * width * 72),
    )(place, *parts, *extra)


def local(
    tokens,
    visible_counts,
    norm_one_gain,
    norm_one_shift,
    input_weight,
    input_bias,
    mixer_weight,
    mixer_bias,
    norm_two_gain,
    norm_two_shift,
    up_weight,
    up_bias,
    down_weight,
    down_bias,
    output_grad,
    groups,
    outer,
):
    width = tokens.shape[1]
    rows = tokens.shape[0]
    cols = mixer_weight.shape[0]
    t = lax.axis_index("t")
    core = lax.axis_index("c")
    place = jnp.stack([2 * lax.axis_index("a") + lax.axis_index("b"), core, t]).astype(jnp.int32)
    one_row = lambda v: v.reshape(1, -1)

    swap = [(0, 1), (1, 0)]
    cross = [(0, 3), (1, 2), (2, 1), (3, 0)]
    to_near = [(z, (z + 1) % groups) for z in range(groups)] + [
        (groups + z, groups + (z + 2) % groups) for z in range(groups)
    ]
    to_far = [(groups + z, groups + (z + 3) % groups) for z in range(groups)]
    home_near = [(j, i) for i, j in to_near]
    home_far = [(j, i) for i, j in to_far]

    def spread(piece):
        return (
            piece,
            lax.ppermute(piece, "b", swap),
            lax.ppermute(piece, "a", swap),
            lax.ppermute(piece, ("a", "b"), cross),
        )

    def together(*groups):
        return lax.optimization_barrier(groups)

    def after(value, *others):
        return lax.optimization_barrier((value, *others))[0]

    def first_exchange(send_x, send_y, keep_x, keep_y):
        got_x = lax.ppermute(send_x, "b", swap)
        got_y = lax.ppermute(send_y, "a", swap)
        return keep_x, keep_y, got_x, got_y

    def second_exchange(send_y, send_x, base):
        return base, lax.ppermute(send_y, "a", swap), lax.ppermute(send_x, "b", swap)

    def direct(keep, send_x, send_y, send_xy):
        return (
            keep,
            lax.ppermute(send_x, "b", swap),
            lax.ppermute(send_y, "a", swap),
            lax.ppermute(send_xy, ("a", "b"), cross),
        )

    def over_outer(value):
        return lax.psum(value.astype(F32), "o").astype(BF16) if outer > 1 else value

    projection = input_weight.transpose(1, 2, 0).reshape(3 * cols, width)
    normed_one = norm_one(
        place,
        visible_counts,
        tokens,
        norm_one_gain,
        norm_one_shift,
    )
    piece_one, tail_one = pack_attention(
        place, projection, mixer_weight, after(input_bias, normed_one), up_bias
    )
    depth_near_one = lax.ppermute(piece_one, ("c", "t"), to_near)
    normed_other = lax.ppermute(normed_one, "c", swap)
    piece_two = pack_hidden(place, up_weight, down_weight)
    both_two = jnp.concatenate([up_weight, down_weight])
    depth_near_one, normed_other, piece_two, both_two = together(
        depth_near_one, normed_other, piece_two, both_two
    )
    near_one = spread(depth_near_one)
    far_projection = lax.ppermute(after(projection, depth_near_one), ("c", "t"), to_far)
    far_mixer = lax.ppermute(after(tail_one, depth_near_one), ("c", "t"), to_far)
    near_two = lax.ppermute(after(piece_two, far_mixer, *near_one), ("c", "t"), to_near)

    own_one = (projection, tail_one)
    far_one = (far_projection, far_mixer)
    saved, soft, part = attention(place, own_one, near_one, far_one, normed_other, None, BF16)
    saved, soft, part, near_two = together(saved, soft, part, near_two)
    grad_other = lax.ppermute(after(output_grad, part), "c", swap)
    part_received = lax.ppermute(part, "c", swap)
    near_x = lax.ppermute(near_two, "b", swap)
    near_y = lax.ppermute(near_two, "a", swap)
    far_two = lax.ppermute(after(both_two, near_two), ("c", "t"), to_far)
    saved, soft, part = attention(
        place, own_one, near_one, far_one, normed_one, (saved, soft), BF16
    )
    part, part_received, near_x, near_y, grad_other = together(
        part, part_received, near_x, near_y, grad_other
    )
    quarter = near_two.shape[0] // 2
    near_up = lax.ppermute(near_y[:quarter], "b", swap)
    near_down = lax.ppermute(near_x[quarter:], "a", swap)
    first_sum, normed_two = norm_two(
        tokens,
        part,
        part_received,
        one_row(mixer_bias),
        one_row(norm_two_gain),
        one_row(norm_two_shift),
    )
    normed_two, first_sum, near_up, near_down = together(
        normed_two, first_sum, near_up, near_down
    )
    normed_two_other = lax.ppermute(normed_two, "c", swap)
    normed_two_both = (normed_two, normed_two_other)

    grad_both = (output_grad, grad_other)
    pieces = (near_two, near_x, near_y, near_up, near_down, depth_near_one)
    near_outs = hidden_block(place, pieces, normed_two_both, grad_both, False)
    near_outs, far_two = together(near_outs, far_two)
    *grads_near, bias_near, out_near, out_send, back_near, back_send = near_outs
    stage_near = first_exchange(*grads_near)
    back_near_received = lax.ppermute(back_send, "c", swap)
    out_near_received = lax.ppermute(out_send, "c", swap)
    shards = (both_two, tail_one, far_two, far_mixer)
    far_outs = hidden_block(place, shards, normed_two_both, grad_both, True)
    far_outs, stage_near, back_near_received, out_near_received = together(
        far_outs, stage_near, back_near_received, out_near_received
    )
    grads_far, bias_far, out_far, out_send, back_far_mine, back_send = far_outs

    got_far = lax.ppermute(grads_far, ("c", "t"), home_far)
    back_received = lax.ppermute(back_send, "c", swap)
    (stage_near,) = sums(place, (first_sums_kernel, stage_near))
    back_received = after(back_received, *stage_near)
    stage_near = second_exchange(*stage_near)
    grad_first_low, sums_two = norm_two_back(
        (back_near, back_near_received, back_far_mine, back_received),
        first_sum,
        one_row(norm_two_gain),
        output_grad,
    )
    first_other = lax.ppermute(grad_first_low, "c", swap)
    out_received = lax.ppermute(after(out_send, first_other), "c", swap)

    normed_both = (normed_one, normed_other)
    first_both = (grad_first_low, first_other)
    *grads_one_near, bias_one_near, back_near, back_send = attention_back(
        place, 1, None, near_one, normed_both, first_both, saved, soft
    )
    grads_one_near, back_near, back_send, stage_near, got_far, out_received = together(
        grads_one_near, back_near, back_send, stage_near, got_far, out_received
    )
    one_near = direct(*grads_one_near)
    (plane_near,), (send_far,) = sums(
        place, (plane_sums_kernel, stage_near), (pair_send_kernel, (grads_far, got_far))
    )
    depth_near = lax.ppermute(plane_near, ("c", "t"), home_near)
    received_far = lax.ppermute(send_far, "c", swap)
    back_near_send = after(back_send, received_far)
    grad_low_late = after(grad_first_low, plane_near)
    *grads_one_far, bias_one_far, back_far_mine, back_send = attention_back(
        place, 0, own_one, far_one, normed_both, (grad_low_late, first_other), saved, soft
    )
    grads_one_far, back_far_mine, back_send, one_near, received_far, depth_near = together(
        grads_one_far, back_far_mine, back_send, one_near, received_far, depth_near
    )
    back_near_received = lax.ppermute(back_near_send, "c", swap)

    one_far = direct(*grads_one_far)
    back_received = lax.ppermute(back_send, "c", swap)
    (one_near,), sums_far, (keep_two, send_two) = sums(
        place,
        (total_kernel, one_near),
        (pair_sums_kernel, (grads_far, got_far, received_far)),
        (half_split_kernel, (depth_near,)),
    )
    one_depth_near = lax.ppermute(one_near, ("c", "t"), home_near)
    received_two = lax.ppermute(send_two, "c", swap)
    grad_tokens, vectors = norm_one_back(
        groups,
        place,
        (back_near, back_near_received, back_far_mine, back_received),
        tokens,
        one_row(norm_one_gain),
        grad_first_low,
        sums_two,
        bias_near,
        bias_far,
        bias_one_near,
        bias_one_far,
    )
    vectors_core = lax.ppermute(vectors, "c", swap)
    vectors_core, one_far, received_two = together(vectors_core, one_far, received_two)
    (one_far,), (vectors,) = sums(
        place, (total_kernel, one_far), (total_kernel, (vectors, vectors_core))
    )
    one_depth_far = lax.ppermute(one_far, ("c", "t"), home_far)
    sums_far = direct(*sums_far)
    result = (
        first_sum
        + (out_near.astype(F32) + out_near_received.astype(F32))
        + (out_far.astype(F32) + out_received.astype(F32))
        + down_bias
    ).astype(BF16)
    one_depth_far, one_depth_near, result = together(one_depth_far, one_depth_near, result)
    ((keep_one, send_one),) = sums(
        place, (depth_sums_kernel, (one_far, one_depth_far, one_depth_near))
    )
    received_one = lax.ppermute(send_one, "c", swap)
    vectors_plane = spread(vectors)
    received_one, vectors_plane, sums_far = together(received_one, vectors_plane, sums_far)
    (parts,), (vectors,) = sums(
        place,
        (last_sums_kernel, (keep_one, received_one, *sums_far, keep_two, received_two)),
        (total_kernel, vectors_plane),
    )
    mine = spread(over_outer(parts))
    turns = [
        lax.ppermute(vectors, "t", [(z, (z + k) % groups) for z in range(groups)])
        for k in range(1, groups)
    ]
    vectors = sum(turns, vectors)
    if outer > 1:
        vectors = lax.psum(vectors, "o")
    grad_up_bias = lax.dynamic_slice_in_dim(vectors, 6 + t, 1)[0]
    grad_input_bias = lax.dynamic_slice_in_dim(vectors, 6 + groups + t, 1).reshape(-1, cols)[:2]
    rows_out = [vectors[index] for index in range(6)]
    mine, rows_out, grad_up_bias, grad_input_bias = together(
        mine, rows_out, grad_up_bias, grad_input_bias
    )
    other = tuple(lax.ppermute(part, "c", swap) for part in mine)
    half_done = finish(place, mine, 0, None)
    other, half_done = together(other, half_done)
    grad_input, grad_mixer, grad_up, grad_down = finish(place, other, 1, half_done)
    grad_input = grad_input.reshape(3, cols, width).transpose(2, 0, 1)
    return (
        result,
        grad_tokens,
        rows_out[0],
        rows_out[1],
        grad_input,
        grad_input_bias,
        grad_mixer,
        rows_out[4],
        rows_out[2],
        rows_out[3],
        grad_up,
        grad_up_bias,
        grad_down,
        rows_out[5],
    )


def solution(mesh):
    dp, groups = mesh.shape["dp"], mesh.shape["tensor"]
    outer = dp // 8
    split = jax.sharding.Mesh(
        mesh.devices.reshape(outer, 2, 2, 2, groups), ("o", "a", "b", "c", "t")
    )
    dp_axes = ("o", "a", "b", "c")
    all_axes = dp_axes + ("t",)
    in_specs = (
        P(all_axes, None),
        P(dp_axes),
        P(),
        P(),
        P(None, None, "t"),
        P(None, "t"),
        P("t", None),
        P(),
        P(),
        P(),
        P(None, "t"),
        P("t"),
        P("t", None),
        P(),
        P(all_axes, None),
    )
    out_specs = (
        P(all_axes, None),
        P(all_axes, None),
        P(),
        P(),
        P(None, None, "t"),
        P(None, "t"),
        P("t", None),
        P(),
        P(),
        P(),
        P(None, "t"),
        P("t"),
        P("t", None),
        P(),
    )
    return jax.shard_map(
        functools.partial(local, groups=groups, outer=outer),
        mesh=split,
        in_specs=in_specs,
        out_specs=out_specs,
        check_vma=False,
    )
```
